32 devices in a mesh: dp: 8 (over z, core), ctx: 4 (over y, x).
Axes of the slice: x: 2, y: 2, z: 4, core: 2. Of those that a mesh axis runs over, the one named last changes fastest.
Arguments:
- hidden_in: bfloat16 [8, 2048, 2048], P('dp', 'ctx'), may hold values from -6 to 6
- ln_gain: bfloat16 [2048], P(('dp', 'ctx')), may hold values from 0.099609375 to 1.8984375
- ln_bias: bfloat16 [2048], P(('dp', 'ctx')), may hold values from -4 to 4
- w_qkv: bfloat16 [2048, 6144], P(('dp', 'ctx')), may hold values from -0.125 to 0.125
- b_qkv: bfloat16 [6144], P(('dp', 'ctx')), may hold values from -4 to 4
- w_out: bfloat16 [2048, 2048], P(('dp', 'ctx')), may hold values from -2 to 2
- b_out: bfloat16 [2048], P(('dp', 'ctx')), may hold values from -4 to 4
- w_up: bfloat16 [2048, 8192], P(('dp', 'ctx')), may hold values from -0.125 to 0.125
- b_up: bfloat16 [8192], P(('dp', 'ctx')), may hold values from -4 to 4
- w_down: bfloat16 [8192, 2048], P(('dp', 'ctx')), may hold values from -0.0625 to 0.0625
- b_down: bfloat16 [2048], P(('dp', 'ctx')), may hold values from -4 to 4
- segment_ids: int32 [8, 2048], P('dp'), may hold values from 0 to 3, as said below
- positions: int32 [8, 2048], P('dp', 'ctx'), may hold values from 0 to 1023, as said below
- token_order: int32 [8, 2048], P('dp'), may hold values from 0 to 2047, as said below
- grad_out: bfloat16 [8, 2048, 2048], P('dp', 'ctx'), may hold values from -6 to 6
Outputs:
- output: bfloat16 [8, 2048, 2048], P('dp', 'ctx')
- grad_in: bfloat16 [8, 2048, 2048], P('dp', 'ctx')
- grad_ln_gain: float32 [2048], P(('dp', 'ctx'))
- grad_ln_bias: float32 [2048], P(('dp', 'ctx'))
- grad_w_qkv: float32 [2048, 6144], P(('dp', 'ctx'))
- grad_b_qkv: float32 [6144], P(('dp', 'ctx'))
- grad_w_out: float32 [2048, 2048], P(('dp', 'ctx'))
- grad_b_out: float32 [2048], P(('dp', 'ctx'))
- grad_w_up: float32 [2048, 8192], P(('dp', 'ctx'))
- grad_b_up: float32 [8192], P(('dp', 'ctx'))
- grad_w_down: float32 [8192, 2048], P(('dp', 'ctx'))
- grad_b_down: float32 [2048], P(('dp', 'ctx'))
The draws below stay inside these ranges and needn't reach their ends.
Inputs may be any that keep to these rules, and one draw needn't show every extreme that they name: Each row's places 0 to 2047 form 4 documents of consecutive places, numbered in order of place, one of which holds exactly 1024 places; segment_ids gives the document of the place token_order assigns to each slot. `positions`: A slot's place minus the first place of its document. `token_order`: each row is a permutation of its places that moves whole runs of 128 places: slots 128 b to 128 b + 127 hold the places of one run in rising order.
All inputs are finite; a program needn't handle non-finite values.
Results may differ from the reference program's by a relative error of at most 0.0095.
Values may be sent and summed in bfloat16 or wider, within the bound.
No kernel may reach another device: no remote copies, remote signals or barrier semaphores. Data moves between devices by JAX's collectives and lax.ppermute only.
A program may use at most 512 MiB of HBM per device.

```python
import jax
import jax.numpy as jnp
from jax import lax

D = 2048
HEADS = 32
FF = 8192
HEAD = 64
ROT = 32
ROW_LEN = 2048
BLK = 128
DOCS = 4
ROWS = 8


def packed_layout(key):
    base_key = jax.random.fold_in(key, 11)
    row_keys = jax.random.split(base_key, ROWS)

    def one_row(row_key):
        cut_key, block_key, place_key = jax.random.split(row_key, 3)
        half_len = ROW_LEN // 2
        cuts = jnp.sort(jax.random.permutation(cut_key, half_len - 1)[:DOCS - 2].astype(jnp.int32) + 1)
        edges = jnp.concatenate([jnp.zeros((1,), jnp.int32), cuts, jnp.full((1,), half_len, jnp.int32)])
        short_lengths = edges[1:] - edges[:-1]
        long_index = jax.random.randint(place_key, (), 0, DOCS).astype(jnp.int32)
        doc_index = jnp.arange(DOCS, dtype=jnp.int32)
        current = short_lengths[jnp.clip(doc_index, 0, DOCS - 2)]
        previous = short_lengths[jnp.clip(doc_index - 1, 0, DOCS - 2)]
        lengths = jnp.where(doc_index < long_index, current, jnp.where(doc_index == long_index, half_len, previous))
        boundaries = jnp.cumsum(lengths).astype(jnp.int32)[:DOCS - 1]
        places = jnp.arange(ROW_LEN, dtype=jnp.int32)
        segment_place = jnp.sum((places[:, None] >= boundaries[None, :]).astype(jnp.int32), axis=1)
        starts = jnp.concatenate([jnp.zeros((1,), jnp.int32), boundaries])
        position_place = places - starts[segment_place]
        blocks = jax.random.permutation(block_key, ROW_LEN // BLK).astype(jnp.int32)
        slot_order = blocks[places // BLK] * BLK + places % BLK
        return (segment_place[slot_order], position_place[slot_order], slot_order)
    return jax.vmap(one_row)(row_keys)


def draw_segment_ids(key, part):
    return packed_layout(key)[0]


def draw_positions(key, part):
    return packed_layout(key)[1]


def draw_token_order(key, part):
    return packed_layout(key)[2]


def steps_of(stream_key, extent, shards, least, largest):
    level, own = 1.0, jax.random.fold_in(stream_key, 6)
    for position, parts in shards:
        steps = jnp.exp(jax.random.uniform(jax.random.fold_in(own, position), (parts,), jnp.float32, least / len(shards), largest / len(shards)))
        level = level * jnp.repeat(steps, extent[position] // parts).reshape([-1 if axis == position else 1 for axis in range(len(extent))])
    return level


def noise(own_key, extent, deviation, bound, cuts=(), kind=jnp.bfloat16):
    array = jax.random.normal(own_key, extent, jnp.float32) * deviation
    if len(cuts) > 0:
        array = steps_of(own_key, extent, cuts, -0.22, 0.18) * array
    return jnp.clip(array, min=-bound, max=bound).astype(kind)


def setup_inputs(seed: int = 0) -> dict:
    key_list = jax.random.split(jax.random.key(seed), 16)
    hidden_in = noise(key_list[0], (ROWS, ROW_LEN, D), 1.0, 6.0, ((0, 8), (1, 4)))
    ln_gain = jnp.clip(1.0 + 0.18 * jax.random.normal(key_list[1], (D,), jnp.float32), 0.099609375, 1.8984375).astype(jnp.bfloat16)
    ln_bias = noise(key_list[2], (D,), 0.3, 4.0, ((0, 32),))
    w_qkv = noise(key_list[3], (D, 3 * D), D ** -0.5, 0.125, ((0, 32),))
    b_qkv = noise(key_list[4], (3 * D,), 0.3, 4.0, ((0, 32),))
    w_out = noise(key_list[5], (D, D), (max(D // 256, 1)) ** -0.5, 2.0, ((0, 32),))
    b_out = noise(key_list[6], (D,), 0.3, 4.0, ((0, 32),))
    w_up = noise(key_list[7], (D, FF), D ** -0.5, 0.125, ((0, 32),))
    b_up = noise(key_list[8], (FF,), 0.3, 4.0, ((0, 32),))
    w_down = noise(key_list[9], (FF, D), FF ** -0.5, 0.0625, ((0, 32),))
    b_down = noise(key_list[10], (D,), 0.3, 4.0, ((0, 32),))
    segment_ids = draw_segment_ids(jax.random.fold_in(key_list[15], 71), 0)
    positions = draw_positions(jax.random.fold_in(key_list[15], 71), 0)
    token_order = draw_token_order(jax.random.fold_in(key_list[15], 71), 0)
    grad_out = noise(key_list[14], (ROWS, ROW_LEN, D), 1.0, 6.0, ((0, 8), (1, 4)))
    return {"hidden_in": hidden_in, "ln_gain": ln_gain, "ln_bias": ln_bias, "w_qkv": w_qkv, "b_qkv": b_qkv, "w_out": w_out, "b_out": b_out, "w_up": w_up, "b_up": b_up, "w_down": w_down, "b_down": b_down, "segment_ids": segment_ids, "positions": positions, "token_order": token_order, "grad_out": grad_out}


@jax.custom_vjp
def low(v):
    return lax.optimization_barrier(v.astype(jnp.bfloat16)).astype(jnp.float32)

@jax.custom_vjp
def low_back(v):
    return v

def low_keep(v):
    return (low(v), None)

def low_pass(kept, grad):
    return (grad,)

def back_keep(v):
    return (v, None)

def back_low(kept, grad):
    return (low(grad),)
low.defvjp(low_keep, low_pass)
low_back.defvjp(back_keep, back_low)
EPS = 1e-05
NEG = -1e+30

def angle_table(position_row):
    half_width = ROT // 2
    frequency = 10000.0 ** (-jnp.arange(half_width, dtype=jnp.float32) * 2.0 / ROT)
    angles = position_row.astype(jnp.float32)[..., None] * frequency
    return (jnp.cos(angles)[..., None, :], jnp.sin(angles)[..., None, :])

def rotate(values, cosine, sine_table):
    half_width = cosine.shape[-1]
    front_part = values[..., :half_width]
    back_part = values[..., half_width:2 * half_width]
    return jnp.concatenate([front_part * cosine - back_part * sine_table, back_part * cosine + front_part * sine_table, values[..., 2 * half_width:]], axis=-1)

def layer_row(params, row_in, segment_row, position_row, order_row):
    gain, shift, w_qkv, b_qkv, w_out, b_out, w_up, b_up, w_down, b_down = params
    exact = lax.Precision.HIGHEST
    length = row_in.shape[0]
    average = lax.optimization_barrier(jnp.mean(row_in, axis=-1, keepdims=True))
    centred = row_in - average
    variance = lax.optimization_barrier(jnp.mean(centred * centred, axis=-1, keepdims=True))
    normed = low(centred * lax.rsqrt(variance + EPS) * gain + shift)
    qkv = low_back(jnp.dot(normed, w_qkv, precision=exact) + b_qkv)
    cosine, sine_table = angle_table(position_row)
    queries = low(rotate(qkv[:, :D].reshape(length, HEADS, HEAD), cosine, sine_table))
    keys_rot = low(rotate(qkv[:, D:2 * D].reshape(length, HEADS, HEAD), cosine, sine_table))
    values = low(qkv[:, 2 * D:].reshape(length, HEADS, HEAD))
    allowed = (segment_row[:, None] == segment_row[None, :]) & (order_row[None, :] <= order_row[:, None])

    def one_head(pieces):
        q_head, k_head, v_head = pieces
        raw_scores = low_back(jnp.dot(q_head, k_head.T, precision=exact) * HEAD ** (-0.5))
        scores = jnp.where(allowed, raw_scores, NEG)
        row_top = lax.optimization_barrier(jnp.max(scores, axis=-1, keepdims=True))
        weights = jnp.exp(scores - row_top)
        probabilities = low(weights / lax.optimization_barrier(jnp.sum(weights, axis=-1, keepdims=True)))
        return low(low_back(jnp.dot(probabilities, v_head, precision=exact)))
    mixed_out = lax.map(jax.checkpoint(one_head), (jnp.moveaxis(queries, 1, 0), jnp.moveaxis(keys_rot, 1, 0), jnp.moveaxis(values, 1, 0)))
    attended = jnp.moveaxis(mixed_out, 0, 1).reshape(length, D)
    attn_out = jnp.dot(attended, w_out, precision=exact) + b_out
    up_proj = low_back(jnp.dot(normed, w_up, precision=exact) + b_up)
    active = low(jax.nn.gelu(up_proj, approximate=True))
    mlp_out = jnp.dot(active, w_down, precision=exact) + b_down
    return row_in + attn_out + mlp_out

def reference(hidden_in, ln_gain, ln_bias, w_qkv, b_qkv, w_out, b_out, w_up, b_up, w_down, b_down, segment_ids, positions, token_order, grad_out):
    params = (ln_gain.astype(jnp.float32), ln_bias.astype(jnp.float32), w_qkv.astype(jnp.float32), b_qkv.astype(jnp.float32), w_out.astype(jnp.float32), b_out.astype(jnp.float32), w_up.astype(jnp.float32), b_up.astype(jnp.float32), w_down.astype(jnp.float32), b_down.astype(jnp.float32))
    hidden_f = hidden_in.astype(jnp.float32)

    def whole_layer(param_set, hidden_all):

        def row_step(carried, row_items):
            return (carried, layer_row(param_set, row_items[0], row_items[1], row_items[2], row_items[3]))
        carried, outputs = lax.scan(row_step, jnp.zeros((), jnp.float32), (hidden_all, segment_ids, positions, token_order))
        return outputs
    output, pullback = jax.vjp(whole_layer, params, hidden_f)
    param_grads, grad_in = pullback(grad_out.astype(jnp.float32))
    return (output.astype(jnp.bfloat16), grad_in.astype(jnp.bfloat16), param_grads[0], param_grads[1], param_grads[2], param_grads[3], param_grads[4], param_grads[5], param_grads[6], param_grads[7], param_grads[8], param_grads[9])
```

```python
import functools
import math

import jax
import jax.numpy as jnp
from jax import lax
from jax.experimental import pallas as pl
from jax.experimental.pallas import tpu as pltpu
from jax.sharding import PartitionSpec as P

HEAD = 64
ROT = 32
BLK = 128
DOCS = 4
EPS = 1e-05
NEG = -1e30
PAIR = 2 * HEAD
KEYS = 256
LONGEST = 1024
PAIRS = 2
LOOSE = 2
SCALE = HEAD**-0.5
ALL = ("dp", "ctx")
BF = jnp.bfloat16
F32 = jnp.float32


def partner(x):
    lane = lax.broadcasted_iota(jnp.int32, x.shape, 1) % HEAD
    return jnp.where(
        lane < ROT // 2, pltpu.roll(x, PAIR - ROT // 2, 1), pltpu.roll(x, ROT // 2, 1)
    )


def dot(a, b):
    return jnp.dot(a, b, preferred_element_type=F32)


def dot_t(a, b):
    return lax.dot_general(a, b, (((1,), (1,)), ((), ())), preferred_element_type=F32)


def aligned_rows(index, size):
    return pl.ds(pl.multiple_of(index * size, size), size)


def attention_kernel(
    place_ref,
    slot_ref,
    low_ref,
    qkv_ref,
    cot_ref,
    cos_ref,
    sin_ref,
    first_ref,
    att_ref,
    grad_ref,
    q_st,
    do_st,
    k_s,
    v_s,
    k_t,
    v_t,
    dk_s,
    dv_s,
    p_s,
    dp_s,
):
    slots = qkv_ref.shape[0]
    blocks = slots // BLK
    pairs = k_s.shape[0]
    lane_first = lax.broadcasted_iota(jnp.int32, (BLK, PAIR), 1) < HEAD
    row_first = lax.broadcasted_iota(jnp.int32, (PAIR, BLK), 0) < HEAD

    def stack(value):
        zero = jnp.zeros_like(value)
        both = [jnp.where(lane_first, value, zero), jnp.where(lane_first, zero, value)]
        return jnp.concatenate(both, axis=0).astype(BF)

    def columns(pair, which, count=3):
        start = (pair * count + which) * PAIR
        return slice(start, start + PAIR)

    def load_block(b, carry):
        rows = aligned_rows(b, BLK)
        place = place_ref[b]
        out_rows = aligned_rows(place, BLK)
        cosine = cos_ref[rows, :]
        sine = sin_ref[rows, :]
        for pair in range(pairs):
            q = qkv_ref[rows, columns(pair, 0)]
            k = qkv_ref[rows, columns(pair, 1)]
            v = qkv_ref[rows, columns(pair, 2)]
            q = (q * cosine + partner(q) * sine).astype(BF).astype(F32) * SCALE
            k = k * cosine + partner(k) * sine
            q_st[pair, aligned_rows(place, 2 * BLK), :] = stack(q)
            do = cot_ref[rows, columns(pair, 0, 1)].astype(F32)
            do_st[pair, aligned_rows(place, 2 * BLK), :] = stack(do)
            k_s[pair, out_rows, :] = k.astype(BF)
            v_s[pair, out_rows, :] = v.astype(BF)
            k_t[pair, out_rows, :] = k.T.astype(BF)
            v_t[pair, out_rows, :] = v.T.astype(BF)
        return carry

    lax.fori_loop(0, blocks, load_block, 0, unroll=LOOSE)
    dk_s[...] = jnp.zeros_like(dk_s)
    dv_s[...] = jnp.zeros_like(dv_s)

    def tiles_of(i, low, count):
        stacked = aligned_rows(i, 2 * BLK)
        first = first_ref[pl.ds(i, 1), :]
        row = lax.broadcasted_iota(jnp.int32, (KEYS, BLK), 0)
        own = i * BLK + lax.broadcasted_iota(jnp.int32, (1, BLK), 1)
        every = range(pairs)
        top = [None] * pairs
        for t in range(count):
            keys = aligned_rows(low + t, KEYS)
            part = slice(t * KEYS, (t + 1) * KEYS)
            place = (low + t) * KEYS
            allowed = row >= first - place
            if t == count - 1:
                allowed = allowed & (row <= own - place)
            allowed = jnp.concatenate([allowed, allowed], axis=1)
            for pair in every:
                s = dot_t(k_s[pair, keys, :], q_st[pair, stacked, :])
                s = jnp.where(allowed, s, NEG)
                p_s[pair, part, :] = s
                dp_s[pair, part, :] = dot_t(v_s[pair, keys, :], do_st[pair, stacked, :])
                here = jnp.max(s, axis=0, keepdims=True)
                top[pair] = here if t == 0 else jnp.maximum(top[pair], here)
        total = [0.0] * pairs
        inner = [0.0] * pairs
        for t in range(count):
            part = slice(t * KEYS, (t + 1) * KEYS)
            for pair in every:
                p = jnp.exp(p_s[pair, part, :] - top[pair])
                p_s[pair, part, :] = p
                total[pair] += jnp.sum(p, axis=0, keepdims=True)
                inner[pair] += jnp.sum(p * dp_s[pair, part, :], axis=0, keepdims=True)
        inverse = [1.0 / x for x in total]
        inner = [x * y for x, y in zip(inner, inverse)]
        out = [0.0] * pairs
        dq = [0.0] * pairs
        for t in range(count):
            part = slice(t * KEYS, (t + 1) * KEYS)
            keys = aligned_rows(low + t, KEYS)
            for pair in every:
                p = p_s[pair, part, :] * inverse[pair]
                ds = (p * (dp_s[pair, part, :] - inner[pair])).astype(BF)
                p = p.astype(BF)
                v_turned = v_t[pair, keys, :]
                k_turned = k_t[pair, keys, :]
                v_turned = jnp.concatenate([v_turned[:BLK], v_turned[BLK:]], axis=1)
                k_turned = jnp.concatenate([k_turned[:BLK], k_turned[BLK:]], axis=1)
                out[pair] += dot(v_turned, p)
                dq[pair] += dot(k_turned, ds)
                dv_s[pair, keys, :] += dot(p, do_st[pair, stacked, :])
                dk_s[pair, keys, :] += dot(ds, q_st[pair, stacked, :])
        slot_rows = aligned_rows(slot_ref[i], BLK)
        for pair in every:
            x = jnp.where(row_first, out[pair][:, :BLK], out[pair][:, BLK:]).T
            att_ref[slot_rows, columns(pair, 0, 1)] = x.astype(BF)
            x = (jnp.where(row_first, dq[pair][:, :BLK], dq[pair][:, BLK:]) * SCALE).T
            x = x * cos_ref[slot_rows, :] - partner(x) * sin_ref[slot_rows, :]
            grad_ref[slot_rows, columns(pair, 0)] = x.astype(BF)

    most = p_s.shape[1] // KEYS

    def query_block(i, carry):
        low = low_ref[i]
        count = (i * BLK) // KEYS + 1 - low
        for n in range(1, most + 1):
            pl.when(count == n)(functools.partial(tiles_of, i, low, n))
        return carry

    lax.fori_loop(0, blocks, query_block, 0)

    def store_block(b, carry):
        rows = aligned_rows(b, BLK)
        in_rows = aligned_rows(place_ref[b], BLK)
        for pair in range(pairs):
            dk = dk_s[pair, in_rows, :]
            dk = dk * cos_ref[rows, :] - partner(dk) * sin_ref[rows, :]
            grad_ref[rows, columns(pair, 1)] = dk.astype(BF)
            grad_ref[rows, columns(pair, 2)] = dv_s[pair, in_rows, :].astype(BF)
        return carry

    lax.fori_loop(0, blocks, store_block, 0, unroll=LOOSE)


def attention(qkv, cotangent, cosine, sine, first_place, block_place, slot_block):
    slots, width = qkv.shape
    groups = width // (3 * PAIR)
    pairs = math.gcd(groups, PAIRS)
    wide = pairs * PAIR
    blocks = slots // BLK
    low = first_place[:, 0] // KEYS
    once = pl.Buffered(1)
    most = min(LONGEST // KEYS + 1, slots // KEYS)
    grid_spec = pltpu.PrefetchScalarGridSpec(
        num_scalar_prefetch=3,
        grid=(groups // pairs,),
        in_specs=[
            pl.BlockSpec((slots, 3 * wide), lambda g, *_: (0, g)),
            pl.BlockSpec((slots, wide), lambda g, *_: (0, g)),
            pl.BlockSpec((slots, PAIR), lambda g, *_: (0, 0), pipeline_mode=once),
            pl.BlockSpec((slots, PAIR), lambda g, *_: (0, 0), pipeline_mode=once),
            pl.BlockSpec((blocks, BLK), lambda g, *_: (0, 0), pipeline_mode=once),
        ],
        out_specs=[
            pl.BlockSpec((slots, wide), lambda g, *_: (0, g)),
            pl.BlockSpec((slots, 3 * wide), lambda g, *_: (0, g)),
        ],
        scratch_shapes=[
            pltpu.VMEM((pairs, 2 * slots, PAIR), BF),
            pltpu.VMEM((pairs, 2 * slots, PAIR), BF),
            pltpu.VMEM((pairs, slots, PAIR), BF),
            pltpu.VMEM((pairs, slots, PAIR), BF),
            pltpu.VMEM((pairs, slots, PAIR), BF),
            pltpu.VMEM((pairs, slots, PAIR), BF),
            pltpu.VMEM((pairs, slots, PAIR), F32),
            pltpu.VMEM((pairs, slots, PAIR), F32),
            pltpu.VMEM((pairs, most * KEYS, 2 * BLK), F32),
            pltpu.VMEM((pairs, most * KEYS, 2 * BLK), F32),
        ],
    )
    tiles = groups * blocks * (blocks // 4)
    return pl.pallas_call(
        attention_kernel,
        out_shape=[
            jax.ShapeDtypeStruct((slots, groups * PAIR), BF),
            jax.ShapeDtypeStruct((slots, width), BF),
        ],
        grid_spec=grid_spec,
        compiler_params=pltpu.CompilerParams(vmem_limit_bytes=50 * 1024 * 1024),
        cost_estimate=pl.CostEstimate(
            flops=12 * tiles * 2 * BLK * BLK * PAIR * 4,
            bytes_accessed=qkv.size * 6 + cotangent.size * 4,
            transcendentals=tiles * 2 * BLK * BLK,
        ),
        name="attention",
    )(block_place, slot_block, low, qkv, cotangent, cosine, sine, first_place)


def exchange(value, axis, size, offset):
    return lax.ppermute(value, axis, [(i, i ^ offset) for i in range(size)])


def after(value, *others):
    return lax.optimization_barrier((value,) + others)[0]


def half_blocks(size):
    if size == 4:
        return [(0, 0), (0, 1), (1, 0), (2, 1), (2, 0), (3, 0), (1, 1), (3, 1)]
    return [(j, half) for j in range(size) for half in range(2)]


def gather_steps(value, size, first=None):
    half = value.shape[0] // 2
    found = {(0, 0): value[:half], (0, 1): value[half:]}
    if size != 4:
        for j in range(1, size):
            other = exchange(value, "ctx", size, j)
            found[j, 0], found[j, 1] = other[:half], other[half:]
        return found, found[1, 0]
    one = exchange(value, "ctx", size, 1)
    two = exchange(value, "ctx", size, 2)
    found[1, 0], found[1, 1] = one[:half], one[half:]
    found[2, 0], found[2, 1] = two[:half], two[half:]
    found[3, 0] = exchange(one[:half], "ctx", size, 2)
    found[3, 1] = exchange(two[half:], "ctx", size, 1)
    return found, lax.optimization_barrier((one, two))[0]


def sum_blocks(piece, size):
    if size != 4:
        total = piece(0, 2)
        for j in range(1, size):
            total = total + exchange(piece(2 * j, 2 * j + 2).astype(BF), "ctx", size, j).astype(F32)
        return total
    far = exchange(piece(4, 6).astype(BF), "ctx", size, 2).astype(F32)
    near = exchange(piece(6, 8).astype(BF), "ctx", size, 1).astype(F32)
    middle = piece(2, 4)
    own = piece(0, 2)
    half = own.shape[0] // 2
    top = exchange((middle[:half] + far[half:]).astype(BF), "ctx", size, 1)
    low = exchange((middle[half:] + near[half:]).astype(BF), "ctx", size, 2)
    top = own[:half] + far[:half] + top.astype(F32)
    low = own[half:] + near[:half] + low.astype(F32)
    return jnp.concatenate([top, low], axis=0)


def gather_small(value, devices):
    copies = jnp.broadcast_to(value, (devices,) + value.shape)
    return lax.all_to_all(copies, ALL, split_axis=0, concat_axis=0, tiled=True)


def gather_dp(value):
    return lax.all_gather(value, "dp", axis=0, tiled=True)


def scatter_dp(value):
    return lax.psum_scatter(value, "dp", scatter_dimension=0, tiled=True)


def swap_ctx(value):
    return lax.all_to_all(value, "ctx", split_axis=0, concat_axis=0, tiled=True)


def swap_ctx_steps(value, size):
    c = lax.axis_index("ctx")
    blocks = value.reshape((size, -1) + value.shape[1:])
    result = blocks
    for j in range(1, size):
        block = lax.dynamic_index_in_dim(blocks, c ^ j, 0)
        block = exchange(block, "ctx", size, j)
        result = lax.dynamic_update_slice_in_dim(result, block, c ^ j, 0)
    return result.reshape(value.shape)


def matmul(a, b):
    return jnp.dot(a, b, preferred_element_type=F32)


def matmul_t(a, b):
    return lax.dot_general(a, b, (((1,), (1,)), ((), ())), preferred_element_type=F32)


def outer(a, b):
    return lax.dot_general(a, b, (((0,), (0,)), ((), ())), preferred_element_type=F32)


def standardise(hidden):
    average = jnp.mean(hidden, axis=-1, keepdims=True)
    centred = hidden - average
    variance = jnp.mean(centred * centred, axis=-1, keepdims=True)
    scale = lax.rsqrt(variance + EPS)
    return centred * scale, scale


def gelu_pair(x):
    root = math.sqrt(2.0 / math.pi)
    t = jnp.tanh(root * (x + 0.044715 * (x * x * x)))
    value = 0.5 * x * (1.0 + t)
    slope = 0.5 * (1.0 + t) + 0.5 * x * (1.0 - t * t) * (root * (1.0 + 3 * 0.044715 * x * x))
    return value, slope


def on_device(
    hidden_in,
    ln_gain,
    ln_bias,
    w_qkv,
    b_qkv,
    w_out,
    b_out,
    w_up,
    b_up,
    w_down,
    b_down,
    segment_ids,
    positions,
    token_order,
    grad_out,
):
    N, C = lax.axis_size("dp"), lax.axis_size("ctx")
    c = lax.axis_index("ctx")
    rows, own_slots, width = hidden_in.shape
    assert rows == 1
    heads = width // HEAD
    own_heads = heads // C
    groups = own_heads // 2
    ff_block = w_down.shape[0]
    row_block = w_qkv.shape[0]
    own_ff = N * ff_block
    hidden_own = hidden_in.reshape(own_slots, width)
    grad_own = grad_out.reshape(own_slots, width)

    found, arrived = gather_steps(hidden_own, C)
    hidden_all = jnp.concatenate([found[key] for key in half_blocks(C)], axis=0)
    found, _ = gather_steps(after(grad_own, arrived), C)
    grad_all = jnp.concatenate([found[key] for key in half_blocks(C)], axis=0)

    sizes = [ln_gain.shape[0], ln_bias.shape[0], b_qkv.shape[0], b_out.shape[0]]
    sizes += [b_up.shape[0], b_down.shape[0]]
    cuts = [sum(sizes[:i]) for i in range(1, len(sizes))]
    small = jnp.concatenate([ln_gain, ln_bias, b_qkv, b_out, b_up, b_down])
    pieces = jnp.split(gather_small(small, N * C), cuts, axis=1)
    gain, shift, qkv_bias, out_bias, up_bias, down_bias = [p.reshape(-1).astype(F32) for p in pieces]
    qkv_send = w_qkv.reshape(row_block, 3, groups, 2, C, HEAD).transpose(4, 0, 2, 1, 3, 5)
    qkv_send = qkv_send.reshape(C * row_block, 3 * own_heads * HEAD)
    up_send = w_up.reshape(row_block, N, C, ff_block).transpose(2, 0, 1, 3)
    up_send = up_send.reshape(C * row_block, own_ff)
    aligned = row_block == HEAD
    if aligned:
        w_out_own = gather_dp(w_out)
    else:
        everything = lax.all_gather(w_out, ALL, axis=0, tiled=True)
        everything = everything.reshape(own_heads, C, HEAD, width)
        w_out_own = lax.dynamic_index_in_dim(everything, c, 1, keepdims=False)
        w_out_own = w_out_own.reshape(own_heads * HEAD, width)
    up_rows = swap_ctx_steps(up_send, C)
    qkv_rows = swap_ctx_steps(after(qkv_send, arrived), C)
    w_up_own = gather_dp(up_rows)
    w_qkv_own = gather_dp(qkv_rows)

    half_block = jnp.array([j for j, _ in half_blocks(C)], jnp.int32) ^ c
    half_block = 2 * half_block + jnp.array([half for _, half in half_blocks(C)], jnp.int32)
    row_order, row_ids = token_order.reshape(-1), segment_ids.reshape(-1)
    slots = row_order.shape[0]
    first = jnp.zeros_like(row_order)
    for document in range(DOCS):
        inside = row_ids == document
        first = jnp.where(inside, jnp.min(jnp.where(inside, row_order, slots)), first)
    order_all, first_all = [
        jnp.take(x.reshape(2 * C, -1), half_block, axis=0).reshape(-1) for x in (row_order, first)
    ]
    position_all = order_all - first_all
    block_place = order_all[::BLK] // BLK
    slot_block = jnp.argsort(block_place).astype(jnp.int32)
    first_place = jnp.take(first_all.reshape(-1, BLK), slot_block, axis=0)
    half = ROT // 2
    frequency = 10000.0 ** (-jnp.arange(half, dtype=F32) * 2.0 / ROT)
    angles = position_all.astype(F32)[:, None] * frequency
    cosine, sine = jnp.cos(angles), jnp.sin(angles)
    rest = jnp.zeros((slots, HEAD - ROT), F32)
    cosine = jnp.concatenate([cosine, cosine, rest + 1.0] * 2, axis=1)
    sine = jnp.concatenate([-sine, sine, rest] * 2, axis=1)

    own_bias = lax.dynamic_index_in_dim(qkv_bias.reshape(3, groups, 2, C, HEAD), c, 3, keepdims=False)
    own_bias = own_bias.transpose(1, 0, 2, 3).reshape(-1)
    hidden_all, cosine, sine, first_place, block_place, slot_block, own_bias = (
        lax.optimization_barrier(
            (hidden_all, cosine, sine, first_place, block_place, slot_block, own_bias)
        )
    )
    xhat_all, _ = standardise(hidden_all.astype(F32))
    normed = (xhat_all * gain + shift).astype(BF)
    w_down_own = gather_dp(after(w_down, arrived))
    own_up_bias = lax.dynamic_index_in_dim(up_bias.reshape(N, C, ff_block), c, 1, keepdims=False)
    up = matmul(normed, w_up_own) + own_up_bias.reshape(-1)
    value, slope = gelu_pair(up)
    active = value.astype(BF)
    down_part = outer(active, grad_all).astype(BF)
    down_grad = scatter_dp(down_part).astype(F32)

    qkv = matmul(after(normed, down_part), w_qkv_own) + own_bias
    d_attended = matmul_t(after(grad_all, down_part), w_out_own).astype(BF)
    attended, d_qkv = attention(
        qkv, d_attended, cosine, sine, first_place, block_place, slot_block
    )

    def column_grad(part, shape):
        return swap_ctx(scatter_dp(part)).reshape((C, row_block) + shape)

    qkv_part = outer(after(normed, down_grad), d_qkv).astype(BF)
    qkv_grad = column_grad(qkv_part, (groups, 3, 2, HEAD))
    qkv_grad = qkv_grad.transpose(1, 3, 2, 4, 0, 5).reshape(w_qkv.shape).astype(F32)
    out_part = outer(after(attended, qkv_part), grad_all)
    if aligned:
        out_part = out_part.astype(BF)
        out_grad = scatter_dp(out_part).astype(F32)
    else:
        spread = jnp.zeros((own_heads, C, HEAD, width), F32)
        spread = lax.dynamic_update_index_in_dim(
            spread, out_part.reshape(own_heads, HEAD, width), c, 1
        )
        out_grad = lax.psum_scatter(
            spread.reshape(heads * HEAD, width), ALL, scatter_dimension=0, tiled=True
        )

    step = own_slots // 2
    attended_then, active_then = lax.optimization_barrier((attended, active, out_part))[:2]

    def out_piece(start, stop):
        rows = slice(start * step, stop * step)
        return matmul(attended_then[rows], w_out_own) + matmul(active_then[rows], w_down_own)

    output = hidden_own.astype(F32) + sum_blocks(out_piece, C) + (out_bias + down_bias)
    output = output.astype(BF).reshape(hidden_in.shape)

    d_up = (matmul_t(after(grad_all, attended), w_down_own) * slope).astype(BF)
    up_part = outer(normed, d_up).astype(BF)
    up_grad = column_grad(up_part, (N, ff_block))
    up_grad = up_grad.transpose(1, 2, 0, 3).reshape(w_up.shape).astype(F32)

    d_qkv_then, d_up_then = lax.optimization_barrier((d_qkv, d_up, up_part))[:2]

    def normed_piece(start, stop):
        rows = slice(start * step, stop * step)
        return matmul_t(d_qkv_then[rows], w_qkv_own) + matmul_t(d_up_then[rows], w_up_own)

    d_normed = sum_blocks(normed_piece, C)
    xhat, scale = standardise(hidden_own.astype(F32))
    e = d_normed * gain
    d_hidden = e - jnp.mean(e, axis=-1, keepdims=True)
    d_hidden = (d_hidden - xhat * jnp.mean(e * xhat, axis=-1, keepdims=True)) * scale
    grad_in = (grad_own.astype(F32) + d_hidden).astype(BF).reshape(hidden_in.shape)

    devices = N * C
    gain_grad = jnp.sum(d_normed * xhat, axis=0)
    shift_grad = jnp.sum(d_normed, axis=0)
    bias_grad = jnp.sum(grad_own.astype(F32), axis=0)
    up_bias_grad = jnp.sum(d_up.astype(F32), axis=0).reshape(N, 1, ff_block)
    qkv_bias_grad = jnp.sum(d_qkv.astype(F32), axis=0).reshape(groups, 3, 2, HEAD)
    qkv_bias_grad = qkv_bias_grad.transpose(1, 0, 2, 3)[:, :, :, None, :]
    mine = jnp.arange(C) == c
    up_bias_grad = jnp.where(mine[None, :, None], up_bias_grad, 0.0)
    qkv_bias_grad = jnp.where(mine[None, None, None, :, None], qkv_bias_grad, 0.0)
    small = [gain_grad, shift_grad, qkv_bias_grad, bias_grad, up_bias_grad]
    small = jnp.concatenate([s.reshape(devices, -1) for s in small], axis=1)
    small = lax.all_to_all(small, ALL, split_axis=0, concat_axis=0, tiled=True)
    small = jnp.split(jnp.sum(small, axis=0), cuts[:4])

    return (
        output,
        grad_in,
        small[0],
        small[1],
        qkv_grad,
        small[2],
        out_grad,
        small[3],
        up_grad,
        small[4],
        down_grad,
        small[3],
    )


def solution(mesh):
    both = P(("dp", "ctx"))
    matrix = P(("dp", "ctx"), None)
    slots = P("dp", "ctx", None)
    in_specs = (
        slots,
        both,
        both,
        matrix,
        both,
        matrix,
        both,
        matrix,
        both,
        matrix,
        both,
        P("dp", None),
        P("dp", "ctx"),
        P("dp", None),
        slots,
    )
    out_specs = (
        slots,
        slots,
        both,
        both,
        matrix,
        both,
        matrix,
        both,
        matrix,
        both,
        matrix,
        both,
    )
    return jax.shard_map(
        on_device, mesh=mesh, in_specs=in_specs, out_specs=out_specs, check_vma=False
    )
```

```python
import functools
import math

import jax
import jax.numpy as jnp
from jax import lax
from jax.experimental import pallas as pl
from jax.experimental.pallas import tpu as pltpu
from jax.sharding import PartitionSpec as P

HEAD = 64
ROT = 32
BLK = 128
DOCS = 4
EPS = 1e-05
NEG = -1e30
PAIR = 2 * HEAD
KEYS = 256
LONGEST = 1024
PAIRS = 2
LOOSE = 2
SCALE = HEAD**-0.5
ALL = ("dp", "ctx")
BF = jnp.bfloat16
F32 = jnp.float32


def partner(x):
    lane = lax.broadcasted_iota(jnp.int32, x.shape, 1) % HEAD
    return jnp.where(
        lane < ROT // 2, pltpu.roll(x, PAIR - ROT // 2, 1), pltpu.roll(x, ROT // 2, 1)
    )


def dot(a, b):
    return jnp.dot(a, b, preferred_element_type=F32)


def dot_t(a, b):
    return lax.dot_general(a, b, (((1,), (1,)), ((), ())), preferred_element_type=F32)


def aligned_rows(index, size):
    return pl.ds(pl.multiple_of(index * size, size), size)


def attention_kernel(
    place_ref,
    slot_ref,
    low_ref,
    qkv_ref,
    cot_ref,
    cos_ref,
    sin_ref,
    first_ref,
    att_ref,
    grad_ref,
    q_st,
    do_st,
    k_s,
    v_s,
    k_t,
    v_t,
    dk_s,
    dv_s,
    p_s,
    dp_s,
):
    slots = qkv_ref.shape[0]
    blocks = slots // BLK
    pairs = k_s.shape[0]
    lane_first = lax.broadcasted_iota(jnp.int32, (BLK, PAIR), 1) < HEAD
    row_first = lax.broadcasted_iota(jnp.int32, (PAIR, BLK), 0) < HEAD

    def stack(value):
        zero = jnp.zeros_like(value)
        both = [jnp.where(lane_first, value, zero), jnp.where(lane_first, zero, value)]
        return jnp.concatenate(both, axis=0).astype(BF)

    def columns(pair, which, count=3):
        start = (pair * count + which) * PAIR
        return slice(start, start + PAIR)

    def load_block(b, carry):
        rows = aligned_rows(b, BLK)
        place = place_ref[b]
        out_rows = aligned_rows(place, BLK)
        cosine = cos_ref[rows, :]
        sine = sin_ref[rows, :]
        for pair in range(pairs):
            q = qkv_ref[rows, columns(pair, 0)]
            k = qkv_ref[rows, columns(pair, 1)]
            v = qkv_ref[rows, columns(pair, 2)]
            q = (q * cosine + partner(q) * sine).astype(BF).astype(F32) * SCALE
            k = k * cosine + partner(k) * sine
            q_st[pair, aligned_rows(place, 2 * BLK), :] = stack(q)
            do = cot_ref[rows, columns(pair, 0, 1)].astype(F32)
            do_st[pair, aligned_rows(place, 2 * BLK), :] = stack(do)
            k_s[pair, out_rows, :] = k.astype(BF)
            v_s[pair, out_rows, :] = v.astype(BF)
            k_t[pair, out_rows, :] = k.T.astype(BF)
            v_t[pair, out_rows, :] = v.T.astype(BF)
        return carry

    lax.fori_loop(0, blocks, load_block, 0, unroll=LOOSE)
    dk_s[...] = jnp.zeros_like(dk_s)
    dv_s[...] = jnp.zeros_like(dv_s)

    def tiles_of(i, low, count):
        stacked = aligned_rows(i, 2 * BLK)
        first = first_ref[pl.ds(i, 1), :]
        row = lax.broadcasted_iota(jnp.int32, (KEYS, BLK), 0)
        own = i * BLK + lax.broadcasted_iota(jnp.int32, (1, BLK), 1)
        every = range(pairs)
        top = [None] * pairs
        for t in range(count):
            keys = aligned_rows(low + t, KEYS)
            part = slice(t * KEYS, (t + 1) * KEYS)
            place = (low + t) * KEYS
            allowed = row >= first - place
            if t == count - 1:
                allowed = allowed & (row <= own - place)
            allowed = jnp.concatenate([allowed, allowed], axis=1)
            for pair in every:
                s = dot_t(k_s[pair, keys, :], q_st[pair, stacked, :])
                s = jnp.where(allowed, s, NEG)
                p_s[pair, part, :] = s
                dp_s[pair, part, :] = dot_t(v_s[pair, keys, :], do_st[pair, stacked, :])
                here = jnp.max(s, axis=0, keepdims=True)
                top[pair] = here if t == 0 else jnp.maximum(top[pair], here)
        total = [0.0] * pairs
        inner = [0.0] * pairs
        for t in range(count):
            part = slice(t * KEYS, (t + 1) * KEYS)
            for pair in every:
                p = jnp.exp(p_s[pair, part, :] - top[pair])
                p_s[pair, part, :] = p
                total[pair] += jnp.sum(p, axis=0, keepdims=True)
                inner[pair] += jnp.sum(p * dp_s[pair, part, :], axis=0, keepdims=True)
        inverse = [1.0 / x for x in total]
        inner = [x * y for x, y in zip(inner, inverse)]
        out = [0.0] * pairs
        dq = [0.0] * pairs
        for t in range(count):
            part = slice(t * KEYS, (t + 1) * KEYS)
            keys = aligned_rows(low + t, KEYS)
            for pair in every:
                p = p_s[pair, part, :] * inverse[pair]
                ds = (p * (dp_s[pair, part, :] - inner[pair])).astype(BF)
                p = p.astype(BF)
                v_turned = v_t[pair, keys, :]
                k_turned = k_t[pair, keys, :]
                v_turned = jnp.concatenate([v_turned[:BLK], v_turned[BLK:]], axis=1)
                k_turned = jnp.concatenate([k_turned[:BLK], k_turned[BLK:]], axis=1)
                out[pair] += dot(v_turned, p)
                dq[pair] += dot(k_turned, ds)
                dv_s[pair, keys, :] += dot(p, do_st[pair, stacked, :])
                dk_s[pair, keys, :] += dot(ds, q_st[pair, stacked, :])
        slot_rows = aligned_rows(slot_ref[i], BLK)
        for pair in every:
            x = jnp.where(row_first, out[pair][:, :BLK], out[pair][:, BLK:]).T
            att_ref[slot_rows, columns(pair, 0, 1)] = x.astype(BF)
            x = (jnp.where(row_first, dq[pair][:, :BLK], dq[pair][:, BLK:]) * SCALE).T
            x = x * cos_ref[slot_rows, :] - partner(x) * sin_ref[slot_rows, :]
            grad_ref[slot_rows, columns(pair, 0)] = x.astype(BF)

    most = p_s.shape[1] // KEYS

    def query_block(i, carry):
        low = low_ref[i]
        count = (i * BLK) // KEYS + 1 - low
        for n in range(1, most + 1):
            pl.when(count == n)(functools.partial(tiles_of, i, low, n))
        return carry

    lax.fori_loop(0, blocks, query_block, 0)

    def store_block(b, carry):
        rows = aligned_rows(b, BLK)
        in_rows = aligned_rows(place_ref[b], BLK)
        for pair in range(pairs):
            dk = dk_s[pair, in_rows, :]
            dk = dk * cos_ref[rows, :] - partner(dk) * sin_ref[rows, :]
            grad_ref[rows, columns(pair, 1)] = dk.astype(BF)
            grad_ref[rows, columns(pair, 2)] = dv_s[pair, in_rows, :].astype(BF)
        return carry

    lax.fori_loop(0, blocks, store_block, 0, unroll=LOOSE)


def attention(qkv, cotangent, cosine, sine, first_place, block_place, slot_block):
    slots, width = qkv.shape
    groups = width // (3 * PAIR)
    pairs = math.gcd(groups, PAIRS)
    wide = pairs * PAIR
    blocks = slots // BLK
    low = first_place[:, 0] // KEYS
    once = pl.Buffered(1)
    most = min(LONGEST // KEYS + 1, slots // KEYS)
    grid_spec = pltpu.PrefetchScalarGridSpec(
        num_scalar_prefetch=3,
        grid=(groups // pairs,),
        in_specs=[
            pl.BlockSpec((slots, 3 * wide), lambda g, *_: (0, g)),
            pl.BlockSpec((slots, wide), lambda g, *_: (0, g)),
            pl.BlockSpec((slots, PAIR), lambda g, *_: (0, 0), pipeline_mode=once),
            pl.BlockSpec((slots, PAIR), lambda g, *_: (0, 0), pipeline_mode=once),
            pl.BlockSpec((blocks, BLK), lambda g, *_: (0, 0), pipeline_mode=once),
        ],
        out_specs=[
            pl.BlockSpec((slots, wide), lambda g, *_: (0, g)),
            pl.BlockSpec((slots, 3 * wide), lambda g, *_: (0, g)),
        ],
        scratch_shapes=[
            pltpu.VMEM((pairs, 2 * slots, PAIR), BF),
            pltpu.VMEM((pairs, 2 * slots, PAIR), BF),
            pltpu.VMEM((pairs, slots, PAIR), BF),
            pltpu.VMEM((pairs, slots, PAIR), BF),
            pltpu.VMEM((pairs, slots, PAIR), BF),
            pltpu.VMEM((pairs, slots, PAIR), BF),
            pltpu.VMEM((pairs, slots, PAIR), F32),
            pltpu.VMEM((pairs, slots, PAIR), F32),
            pltpu.VMEM((pairs, most * KEYS, 2 * BLK), F32),
            pltpu.VMEM((pairs, most * KEYS, 2 * BLK), F32),
        ],
    )
    tiles = groups * blocks * (blocks // 4)
    return pl.pallas_call(
        attention_kernel,
        out_shape=[
            jax.ShapeDtypeStruct((slots, groups * PAIR), BF),
            jax.ShapeDtypeStruct((slots, width), BF),
        ],
        grid_spec=grid_spec,
        compiler_params=pltpu.CompilerParams(vmem_limit_bytes=50 * 1024 * 1024),
        cost_estimate=pl.CostEstimate(
            flops=tiles * 2 * BLK * BLK * PAIR,
            bytes_accessed=qkv.size,
            transcendentals=0,
        ),
        name="attention",
    )(block_place, slot_block, low, qkv, cotangent, cosine, sine, first_place)


def pick_rows(found, order, rows):
    arrays, places = [], []
    for key in order:
        array, start = found[key]
        held = [i for i, known in enumerate(arrays) if known is array]
        if not held:
            arrays.append(array)
            held = [len(arrays) - 1]
        places.append((held[0], start // rows))
    return arrays, places


def join_blocks(found, order, rows, gain=None, shift=None):
    arrays, places = pick_rows(found, order, rows)
    width = arrays[0].shape[1]
    norm = gain is not None

    def kernel(*refs):
        out = refs[-1]
        step = pl.program_id(0)
        for number, (which, block) in enumerate(places):

            @pl.when(step == number)
            def _(ref=refs[which], block=block):
                x = ref[block * rows : (block + 1) * rows, :]
                if norm:
                    x, _ = standardise(x.astype(F32))
                    x = (x * refs[-3][...] + refs[-2][...]).astype(BF)
                out[...] = x

    once = pl.Buffered(1)
    in_specs = [pl.BlockSpec(a.shape, lambda i: (0, 0), pipeline_mode=once) for a in arrays]
    extra = []
    if norm:
        extra = [gain[None, :], shift[None, :]]
        in_specs += [pl.BlockSpec((1, width), lambda i: (0, 0), pipeline_mode=once)] * 2
    size = len(order) * rows * width
    return pl.pallas_call(
        kernel,
        grid=(len(order),),
        in_specs=in_specs,
        out_specs=pl.BlockSpec((rows, width), lambda i: (i, 0)),
        out_shape=jax.ShapeDtypeStruct((len(order) * rows, width), BF),
        compiler_params=pltpu.CompilerParams(vmem_limit_bytes=40 * 1024 * 1024),
        cost_estimate=pl.CostEstimate(
            flops=size * (10 if norm else 1), bytes_accessed=4 * size, transcendentals=0
        ),
        name="norm_rows" if norm else "join_rows",
    )(*arrays, *extra)


def deal_columns(matrix, chunks):
    rows = matrix.shape[0]
    width = sum(stop - start for start, stop in chunks[0])

    def kernel(x_ref, o_ref):
        x = x_ref[...].astype(F32)
        for target, parts in enumerate(chunks):
            part = jnp.concatenate([x[:, start:stop] for start, stop in parts], axis=1)
            o_ref[target] = part.astype(BF)

    return pl.pallas_call(
        kernel,
        out_shape=jax.ShapeDtypeStruct((len(chunks), rows, width), BF),
        cost_estimate=pl.CostEstimate(
            flops=matrix.size, bytes_accessed=4 * matrix.size, transcendentals=0
        ),
        name="deal_columns",
    )(matrix)


def collect_columns(blocks, chunks):
    order = []
    for source, parts in enumerate(chunks):
        place = 0
        for start, stop in parts:
            order.append((start, source, place, place + stop - start))
            place += stop - start
    order.sort()
    width = blocks.shape[0] * blocks.shape[2]

    def kernel(x_ref, o_ref):
        x = [x_ref[source].astype(F32) for source in range(len(chunks))]
        o_ref[...] = jnp.concatenate([x[i][:, low:high] for _, i, low, high in order], axis=1)

    return pl.pallas_call(
        kernel,
        out_shape=jax.ShapeDtypeStruct((blocks.shape[1], width), F32),
        cost_estimate=pl.CostEstimate(
            flops=blocks.size, bytes_accessed=6 * blocks.size, transcendentals=0
        ),
        name="collect_columns",
    )(blocks)


def exchange(value, axis, size, offset):
    return lax.ppermute(value, axis, [(i, i ^ offset) for i in range(size)])


def after(value, *others):
    return lax.optimization_barrier((value,) + others)[0]


def half_blocks(size):
    if size == 4:
        return [(0, 0), (0, 1), (1, 0), (2, 1), (2, 0), (3, 0), (1, 1), (3, 1)]
    return [(j, half) for j in range(size) for half in range(2)]


def split_halves(value, j, found):
    half = value.shape[0] // 2
    found[j, 0], found[j, 1] = (value, 0), (value, half)


def gather_two(first, second, size, wait):
    send = functools.partial(exchange, axis="ctx", size=size)
    half = first.shape[0] // 2
    left, right = {}, {}
    split_halves(first, 0, left)
    split_halves(second, 0, right)
    if size != 4:
        for j in range(1, size):
            split_halves(send(first, offset=j), j, left)
        for j in range(1, size):
            split_halves(send(second, offset=j), j, right)
        return left, right, first
    one, two = send(first, offset=1), send(first, offset=2)
    split_halves(one, 1, left)
    split_halves(two, 2, left)
    one, two, second = lax.optimization_barrier((one, two, second) + wait)[:3]
    near = send(jnp.concatenate([two[half:], second], axis=0), offset=1)
    far = send(jnp.concatenate([one[:half], second], axis=0), offset=2)
    left[3, 0], left[3, 1] = (far, 0), (near, 0)
    right[1, 0], right[1, 1] = (near, half), (near, 2 * half)
    right[2, 0], right[2, 1] = (far, half), (far, 2 * half)
    right[3, 0] = (send(near[half : 2 * half], offset=2), 0)
    right[3, 1] = (send(far[2 * half :], offset=1), 0)
    return left, right, one


def sum_cut(size):
    return 4 if size == 4 else 2


def sum_blocks(away, size):
    away = away.astype(BF)
    if size != 4:
        blocks = away.reshape(size - 1, -1, away.shape[1])
        arrived = tuple(exchange(blocks[j - 1], "ctx", size, j) for j in range(1, size))
        return arrived, lambda own: sum([x.astype(F32) for x in arrived], own)
    half = away.shape[0] // 4
    arrived = (
        exchange(away[: 2 * half], "ctx", size, 2),
        exchange(away[2 * half :], "ctx", size, 1),
    )

    def finish(own):
        far, near = arrived[0].astype(F32), arrived[1].astype(F32)
        top = exchange((own[2 * half : 3 * half] + far[half:]).astype(BF), "ctx", size, 1)
        low = exchange((own[3 * half :] + near[half:]).astype(BF), "ctx", size, 2)
        top = own[:half] + far[:half] + top.astype(F32)
        low = own[half : 2 * half] + near[:half] + low.astype(F32)
        return jnp.concatenate([top, low], axis=0)

    return arrived, finish


def gather_small(value, devices):
    copies = jnp.broadcast_to(value, (devices,) + value.shape)
    return lax.all_to_all(copies, ALL, split_axis=0, concat_axis=0, tiled=True)


def gather_dp(value):
    return lax.all_gather(value, "dp", axis=0, tiled=True)


def scatter_dp(value):
    return lax.psum_scatter(value, "dp", scatter_dimension=0, tiled=True)


def swap_ctx(value):
    return lax.all_to_all(value, "ctx", split_axis=0, concat_axis=0, tiled=True)


def matmul(a, b):
    return jnp.dot(a, b, preferred_element_type=F32)


def matmul_t(a, b):
    return lax.dot_general(a, b, (((1,), (1,)), ((), ())), preferred_element_type=F32)


def outer(a, b):
    return lax.dot_general(a, b, (((0,), (0,)), ((), ())), preferred_element_type=F32)


def standardise(hidden):
    average = jnp.mean(hidden, axis=-1, keepdims=True)
    centred = hidden - average
    variance = jnp.mean(centred * centred, axis=-1, keepdims=True)
    scale = lax.rsqrt(variance + EPS)
    return centred * scale, scale


def gelu_pair(x):
    root = math.sqrt(2.0 / math.pi)
    t = jnp.tanh(root * (x + 0.044715 * (x * x * x)))
    value = 0.5 * x * (1.0 + t)
    slope = 0.5 * (1.0 + t) + 0.5 * x * (1.0 - t * t) * (root * (1.0 + 3 * 0.044715 * x * x))
    return value, slope


def on_device(
    hidden_in,
    ln_gain,
    ln_bias,
    w_qkv,
    b_qkv,
    w_out,
    b_out,
    w_up,
    b_up,
    w_down,
    b_down,
    segment_ids,
    positions,
    token_order,
    grad_out,
):
    N, C = lax.axis_size("dp"), lax.axis_size("ctx")
    c = lax.axis_index("ctx")
    rows, own_slots, width = hidden_in.shape
    assert rows == 1
    heads = width // HEAD
    own_heads = heads // C
    groups = own_heads // 2
    ff_block = w_down.shape[0]
    row_block = w_qkv.shape[0]
    own_ff = N * ff_block
    hidden_own = hidden_in.reshape(own_slots, width)
    grad_own = grad_out.reshape(own_slots, width)


    sizes = [ln_gain.shape[0], ln_bias.shape[0], b_qkv.shape[0], b_out.shape[0]]
    sizes += [b_up.shape[0], b_down.shape[0]]
    cuts = [sum(sizes[:i]) for i in range(1, len(sizes))]
    small = jnp.concatenate([ln_gain, ln_bias, b_qkv, b_out, b_up, b_down])
    small = gather_small(small, N * C)
    hidden_parts, grad_parts, arrived = gather_two(hidden_own, grad_own, C, (small,))
    pieces = jnp.split(small, cuts, axis=1)
    gain, shift, qkv_bias, out_bias, up_bias, down_bias = [p.reshape(-1).astype(F32) for p in pieces]
    qkv_chunks = [
        [
            (part * width + (i * C + t) * HEAD, part * width + (i * C + t + 1) * HEAD)
            for pair in range(groups)
            for part in range(3)
            for i in (2 * pair, 2 * pair + 1)
        ]
        for t in range(C)
    ]
    up_chunks = [
        [((i * C + t) * ff_block, (i * C + t + 1) * ff_block) for i in range(N)] for t in range(C)
    ]
    aligned = row_block == HEAD
    if aligned:
        w_out_own = gather_dp(w_out)
    else:
        everything = lax.all_gather(w_out, ALL, axis=0, tiled=True)
        everything = everything.reshape(own_heads, C, HEAD, width)
        w_out_own = lax.dynamic_index_in_dim(everything, c, 1, keepdims=False)
        w_out_own = w_out_own.reshape(own_heads * HEAD, width)
    up_rows = swap_ctx(deal_columns(w_up, up_chunks)).reshape(C * row_block, -1)
    qkv_send = deal_columns(w_qkv, qkv_chunks)
    qkv_rows = swap_ctx(after(qkv_send, arrived)).reshape(C * row_block, -1)
    w_up_own = gather_dp(up_rows)
    w_qkv_own = gather_dp(qkv_rows)

    half_block = jnp.array([j for j, _ in half_blocks(C)], jnp.int32) ^ c
    half_block = 2 * half_block + jnp.array([half for _, half in half_blocks(C)], jnp.int32)
    row_order, row_ids = token_order.reshape(-1), segment_ids.reshape(-1)
    slots = row_order.shape[0]
    first = jnp.zeros_like(row_order)
    for document in range(DOCS):
        inside = row_ids == document
        first = jnp.where(inside, jnp.min(jnp.where(inside, row_order, slots)), first)
    order_all, first_all = [
        jnp.take(x.reshape(2 * C, -1), half_block, axis=0).reshape(-1) for x in (row_order, first)
    ]
    position_all = order_all - first_all
    block_place = order_all[::BLK] // BLK
    slot_block = jnp.argsort(block_place).astype(jnp.int32)
    first_place = jnp.take(first_all.reshape(-1, BLK), slot_block, axis=0)
    half = ROT // 2
    frequency = 10000.0 ** (-jnp.arange(half, dtype=F32) * 2.0 / ROT)
    angles = position_all.astype(F32)[:, None] * frequency
    cosine, sine = jnp.cos(angles), jnp.sin(angles)
    rest = jnp.zeros((slots, HEAD - ROT), F32)
    cosine = jnp.concatenate([cosine, cosine, rest + 1.0] * 2, axis=1)
    sine = jnp.concatenate([-sine, sine, rest] * 2, axis=1)

    own_bias = lax.dynamic_index_in_dim(qkv_bias.reshape(3, groups, 2, C, HEAD), c, 3, keepdims=False)
    own_bias = own_bias.transpose(1, 0, 2, 3).reshape(-1)
    gain, cosine, sine, first_place, block_place, slot_block, own_bias = lax.optimization_barrier(
        (gain, cosine, sine, first_place, block_place, slot_block, own_bias)
    )
    step = own_slots // 2
    normed = join_blocks(hidden_parts, half_blocks(C), step, gain, shift)
    w_down_own = gather_dp(after(w_down, arrived))
    own_up_bias = lax.dynamic_index_in_dim(up_bias.reshape(N, C, ff_block), c, 1, keepdims=False)
    up = matmul(normed, w_up_own) + own_up_bias.reshape(-1)
    value, slope = gelu_pair(up)
    active, slope = lax.optimization_barrier((value.astype(BF), slope))
    if C == 4:
        for key in ((3, 0), (3, 1)):
            grad_parts[key] = (after(grad_parts[key][0], active), grad_parts[key][1])
    grad_all = join_blocks(grad_parts, half_blocks(C), step)
    down_part = outer(active, grad_all).astype(BF)
    down_grad = scatter_dp(down_part).astype(F32)

    qkv = matmul(after(normed, down_part), w_qkv_own) + own_bias
    d_attended = matmul_t(after(grad_all, down_part), w_out_own).astype(BF)
    attended, d_qkv = attention(
        qkv, d_attended, cosine, sine, first_place, block_place, slot_block
    )

    def column_grad(part, chunks):
        own = scatter_dp(part)
        return collect_columns(swap_ctx(own.reshape(C, row_block, -1)), chunks)

    cut = sum_cut(C) * step

    def out_rows(rows, attended):
        return matmul(attended[rows], w_out_own) + matmul(active[rows], w_down_own)

    out_part = outer(attended, after(grad_all, w_down_own))
    if aligned:
        out_part = out_part.astype(BF)
        out_grad = scatter_dp(out_part).astype(F32)
    else:
        spread = jnp.zeros((own_heads, C, HEAD, width), F32)
        spread = lax.dynamic_update_index_in_dim(
            spread, out_part.reshape(own_heads, HEAD, width), c, 1
        )
        out_grad = lax.psum_scatter(
            spread.reshape(heads * HEAD, width), ALL, scatter_dimension=0, tiled=True
        )

    qkv_part = outer(after(normed, down_grad, out_part), d_qkv).astype(BF)
    qkv_grad = column_grad(qkv_part, qkv_chunks)

    out_away = out_rows(slice(cut, None), after(attended, qkv_part)).astype(BF)
    out_arrived, finish = sum_blocks(out_away, C)
    grad_then = after(grad_all, out_away)
    d_up = (matmul_t(grad_then, w_down_own) * slope).astype(BF)
    up_part = outer(after(normed, *out_arrived), d_up).astype(BF)
    up_grad = column_grad(up_part, up_chunks)
    out_near = out_rows(slice(0, cut), after(attended, up_part))
    out_sum = finish(out_near)
    output = hidden_own.astype(F32) + out_sum + (out_bias + down_bias)
    output = output.astype(BF).reshape(hidden_in.shape)

    d_qkv_then, d_up_then = lax.optimization_barrier((d_qkv, d_up, up_part))[:2]

    def normed_rows(rows):
        return matmul_t(d_qkv_then[rows], w_qkv_own) + matmul_t(d_up_then[rows], w_up_own)

    d_away = normed_rows(slice(cut, None)).astype(BF)
    d_near = normed_rows(slice(0, cut))
    d_normed = sum_blocks(d_away, C)[1](after(d_near, qkv_grad))
    d_normed = after(d_normed, up_grad)
    xhat, scale = standardise(hidden_own.astype(F32))
    e = d_normed * gain
    d_hidden = e - jnp.mean(e, axis=-1, keepdims=True)
    d_hidden = (d_hidden - xhat * jnp.mean(e * xhat, axis=-1, keepdims=True)) * scale
    grad_in = (grad_own.astype(F32) + d_hidden).astype(BF).reshape(hidden_in.shape)

    devices = N * C
    gain_grad = jnp.sum(d_normed * xhat, axis=0)
    shift_grad = jnp.sum(d_normed, axis=0)
    bias_grad = jnp.sum(grad_own.astype(F32), axis=0)
    up_bias_grad = jnp.sum(d_up.astype(F32), axis=0).reshape(N, 1, ff_block)
    qkv_bias_grad = jnp.sum(d_qkv.astype(F32), axis=0).reshape(groups, 3, 2, HEAD)
    qkv_bias_grad = qkv_bias_grad.transpose(1, 0, 2, 3)[:, :, :, None, :]
    mine = jnp.arange(C) == c
    up_bias_grad = jnp.where(mine[None, :, None], up_bias_grad, 0.0)
    qkv_bias_grad = jnp.where(mine[None, None, None, :, None], qkv_bias_grad, 0.0)
    small = [gain_grad, shift_grad, qkv_bias_grad, bias_grad, up_bias_grad]
    small = jnp.concatenate([s.reshape(devices, -1) for s in small], axis=1)
    small = after(small, grad_in)
    small = lax.all_to_all(small, ALL, split_axis=0, concat_axis=0, tiled=True)
    small = jnp.split(jnp.sum(small, axis=0), cuts[:4])

    return (
        output,
        grad_in,
        small[0],
        small[1],
        qkv_grad,
        small[2],
        out_grad,
        small[3],
        up_grad,
        small[4],
        down_grad,
        small[3],
    )


def solution(mesh):
    both = P(("dp", "ctx"))
    matrix = P(("dp", "ctx"), None)
    slots = P("dp", "ctx", None)
    in_specs = (
        slots,
        both,
        both,
        matrix,
        both,
        matrix,
        both,
        matrix,
        both,
        matrix,
        both,
        P("dp", None),
        P("dp", "ctx"),
        P("dp", None),
        slots,
    )
    out_specs = (
        slots,
        slots,
        both,
        both,
        matrix,
        both,
        matrix,
        both,
        matrix,
        both,
        matrix,
        both,
    )
    return jax.shard_map(
        on_device, mesh=mesh, in_specs=in_specs, out_specs=out_specs, check_vma=False
    )
```

```python
import functools
import math

import jax
import jax.numpy as jnp
from jax import lax
from jax.experimental import pallas as pl
from jax.experimental.pallas import tpu as pltpu
from jax.sharding import PartitionSpec as P

HEAD = 64
ROT = 32
BLK = 128
DOCS = 4
EPS = 1e-05
NEG = -1e30
PAIR = 2 * HEAD
KEYS = 256
LONGEST = 1024
PAIRS = 2
LOOSE = 2
FRACTION = 5.0
SCALE = HEAD**-0.5
ALL = ("dp", "ctx")
BF = jnp.bfloat16
F32 = jnp.float32


def partner(x):
    lane = lax.broadcasted_iota(jnp.int32, x.shape, 1) % HEAD
    return jnp.where(
        lane < ROT // 2, pltpu.roll(x, PAIR - ROT // 2, 1), pltpu.roll(x, ROT // 2, 1)
    )


def dot(a, b):
    return jnp.dot(a, b, preferred_element_type=F32)


def dot_t(a, b):
    return lax.dot_general(a, b, (((1,), (1,)), ((), ())), preferred_element_type=F32)


def aligned_rows(index, size):
    return pl.ds(pl.multiple_of(index * size, size), size)


def attention_kernel(
    place_ref,
    slot_ref,
    low_ref,
    qkv_ref,
    cot_ref,
    cos_ref,
    sin_ref,
    first_ref,
    att_ref,
    grad_ref,
    q_st,
    do_st,
    k_s,
    v_s,
    k_t,
    v_t,
    dk_s,
    dv_s,
    p_s,
    dp_s,
):
    slots = qkv_ref.shape[0]
    blocks = slots // BLK
    pairs = k_s.shape[0]
    lane_first = lax.broadcasted_iota(jnp.int32, (BLK, PAIR), 1) < HEAD
    row_first = lax.broadcasted_iota(jnp.int32, (PAIR, BLK), 0) < HEAD

    def stack(value):
        zero = jnp.zeros_like(value)
        both = [jnp.where(lane_first, value, zero), jnp.where(lane_first, zero, value)]
        return jnp.concatenate(both, axis=0).astype(BF)

    def columns(pair, which, count=3):
        start = (pair * count + which) * PAIR
        return slice(start, start + PAIR)

    def load_block(b, carry):
        rows = aligned_rows(b, BLK)
        place = place_ref[b]
        out_rows = aligned_rows(place, BLK)
        cosine = cos_ref[rows, :]
        sine = sin_ref[rows, :]
        for pair in range(pairs):
            q = qkv_ref[rows, columns(pair, 0)]
            k = qkv_ref[rows, columns(pair, 1)]
            v = qkv_ref[rows, columns(pair, 2)]
            q = (q * cosine + partner(q) * sine).astype(BF).astype(F32) * SCALE
            k = k * cosine + partner(k) * sine
            q_st[pair, aligned_rows(place, 2 * BLK), :] = stack(q)
            do = cot_ref[rows, columns(pair, 0, 1)].astype(F32)
            do_st[pair, aligned_rows(place, 2 * BLK), :] = stack(do)
            k_s[pair, out_rows, :] = k.astype(BF)
            v_s[pair, out_rows, :] = v.astype(BF)
            k_t[pair, out_rows, :] = k.T.astype(BF)
            v_t[pair, out_rows, :] = v.T.astype(BF)
        return carry

    lax.fori_loop(0, blocks, load_block, 0, unroll=LOOSE)
    dk_s[...] = jnp.zeros_like(dk_s)
    dv_s[...] = jnp.zeros_like(dv_s)

    def tiles_of(i, low, count):
        stacked = aligned_rows(i, 2 * BLK)
        first = first_ref[pl.ds(i, 1), :]
        row = lax.broadcasted_iota(jnp.int32, (KEYS, BLK), 0)
        own = i * BLK + lax.broadcasted_iota(jnp.int32, (1, BLK), 1)
        every = range(pairs)
        top = [None] * pairs
        for t in range(count):
            keys = aligned_rows(low + t, KEYS)
            part = slice(t * KEYS, (t + 1) * KEYS)
            place = (low + t) * KEYS
            allowed = row >= first - place
            if t == count - 1:
                allowed = allowed & (row <= own - place)
            allowed = jnp.concatenate([allowed, allowed], axis=1)
            for pair in every:
                s = dot_t(k_s[pair, keys, :], q_st[pair, stacked, :])
                s = jnp.where(allowed, s, NEG)
                p_s[pair, part, :] = s
                dp_s[pair, part, :] = dot_t(v_s[pair, keys, :], do_st[pair, stacked, :])
                here = jnp.max(s, axis=0, keepdims=True)
                top[pair] = here if t == 0 else jnp.maximum(top[pair], here)
        total = [0.0] * pairs
        inner = [0.0] * pairs
        for t in range(count):
            part = slice(t * KEYS, (t + 1) * KEYS)
            for pair in every:
                p = jnp.exp(p_s[pair, part, :] - top[pair])
                p_s[pair, part, :] = p
                total[pair] += jnp.sum(p, axis=0, keepdims=True)
                inner[pair] += jnp.sum(p * dp_s[pair, part, :], axis=0, keepdims=True)
        inverse = [1.0 / x for x in total]
        inner = [x * y for x, y in zip(inner, inverse)]
        out = [0.0] * pairs
        dq = [0.0] * pairs
        for t in range(count):
            part = slice(t * KEYS, (t + 1) * KEYS)
            keys = aligned_rows(low + t, KEYS)
            for pair in every:
                p = p_s[pair, part, :] * inverse[pair]
                ds = (p * (dp_s[pair, part, :] - inner[pair])).astype(BF)
                p = p.astype(BF)
                v_turned = v_t[pair, keys, :]
                k_turned = k_t[pair, keys, :]
                v_turned = jnp.concatenate([v_turned[:BLK], v_turned[BLK:]], axis=1)
                k_turned = jnp.concatenate([k_turned[:BLK], k_turned[BLK:]], axis=1)
                out[pair] += dot(v_turned, p)
                dq[pair] += dot(k_turned, ds)
                dv_s[pair, keys, :] += dot(p, do_st[pair, stacked, :])
                dk_s[pair, keys, :] += dot(ds, q_st[pair, stacked, :])
        slot_rows = aligned_rows(slot_ref[i], BLK)
        for pair in every:
            x = jnp.where(row_first, out[pair][:, :BLK], out[pair][:, BLK:]).T
            att_ref[slot_rows, columns(pair, 0, 1)] = x.astype(BF)
            x = (jnp.where(row_first, dq[pair][:, :BLK], dq[pair][:, BLK:]) * SCALE).T
            x = x * cos_ref[slot_rows, :] - partner(x) * sin_ref[slot_rows, :]
            grad_ref[slot_rows, columns(pair, 0)] = x.astype(BF)

    most = p_s.shape[1] // KEYS

    def query_block(i, carry):
        low = low_ref[i]
        count = (i * BLK) // KEYS + 1 - low
        for n in range(1, most + 1):
            pl.when(count == n)(functools.partial(tiles_of, i, low, n))
        return carry

    lax.fori_loop(0, blocks, query_block, 0)

    def store_block(b, carry):
        rows = aligned_rows(b, BLK)
        in_rows = aligned_rows(place_ref[b], BLK)
        for pair in range(pairs):
            dk = dk_s[pair, in_rows, :]
            dk = dk * cos_ref[rows, :] - partner(dk) * sin_ref[rows, :]
            grad_ref[rows, columns(pair, 1)] = dk.astype(BF)
            grad_ref[rows, columns(pair, 2)] = dv_s[pair, in_rows, :].astype(BF)
        return carry

    lax.fori_loop(0, blocks, store_block, 0, unroll=LOOSE)


def attention(qkv, cotangent, cosine, sine, first_place, block_place, slot_block):
    slots, width = qkv.shape
    groups = width // (3 * PAIR)
    pairs = math.gcd(groups, PAIRS)
    wide = pairs * PAIR
    blocks = slots // BLK
    low = first_place[:, 0] // KEYS
    once = pl.Buffered(1)
    most = min(LONGEST // KEYS + 1, slots // KEYS)
    grid_spec = pltpu.PrefetchScalarGridSpec(
        num_scalar_prefetch=3,
        grid=(groups // pairs,),
        in_specs=[
            pl.BlockSpec((slots, 3 * wide), lambda g, *_: (0, g)),
            pl.BlockSpec((slots, wide), lambda g, *_: (0, g)),
            pl.BlockSpec((slots, PAIR), lambda g, *_: (0, 0), pipeline_mode=once),
            pl.BlockSpec((slots, PAIR), lambda g, *_: (0, 0), pipeline_mode=once),
            pl.BlockSpec((blocks, BLK), lambda g, *_: (0, 0), pipeline_mode=once),
        ],
        out_specs=[
            pl.BlockSpec((slots, wide), lambda g, *_: (0, g)),
            pl.BlockSpec((slots, 3 * wide), lambda g, *_: (0, g)),
        ],
        scratch_shapes=[
            pltpu.VMEM((pairs, 2 * slots, PAIR), BF),
            pltpu.VMEM((pairs, 2 * slots, PAIR), BF),
            pltpu.VMEM((pairs, slots, PAIR), BF),
            pltpu.VMEM((pairs, slots, PAIR), BF),
            pltpu.VMEM((pairs, slots, PAIR), BF),
            pltpu.VMEM((pairs, slots, PAIR), BF),
            pltpu.VMEM((pairs, slots, PAIR), F32),
            pltpu.VMEM((pairs, slots, PAIR), F32),
            pltpu.VMEM((pairs, most * KEYS, 2 * BLK), F32),
            pltpu.VMEM((pairs, most * KEYS, 2 * BLK), F32),
        ],
    )
    tiles = groups * blocks * (blocks // 4)
    return pl.pallas_call(
        attention_kernel,
        out_shape=[
            jax.ShapeDtypeStruct((slots, groups * PAIR), BF),
            jax.ShapeDtypeStruct((slots, width), BF),
        ],
        grid_spec=grid_spec,
        compiler_params=pltpu.CompilerParams(vmem_limit_bytes=50 * 1024 * 1024),
        cost_estimate=pl.CostEstimate(
            flops=tiles * 2 * BLK * BLK * PAIR,
            bytes_accessed=qkv.size,
            transcendentals=0,
        ),
        name="attention",
    )(block_place, slot_block, low, qkv, cotangent, cosine, sine, first_place)


def pick_rows(found, order, rows):
    arrays, places = [], []
    for key in order:
        array, start = found[key]
        held = [i for i, known in enumerate(arrays) if known is array]
        if not held:
            arrays.append(array)
            held = [len(arrays) - 1]
        places.append((held[0], start // rows))
    return arrays, places


def norm_blocks(found, order, rows, gain, shift):
    arrays, places = pick_rows(found, order, rows)
    width = arrays[0].shape[1]

    def kernel(*refs):
        out = refs[-1]
        step = pl.program_id(0)
        for number, (which, block) in enumerate(places):

            @pl.when(step == number)
            def _(ref=refs[which], block=block):
                x = ref[block * rows : (block + 1) * rows, :]
                x, _ = standardise(x.astype(F32))
                out[...] = (x * refs[-3][...] + refs[-2][...]).astype(BF)

    once = pl.Buffered(1)
    in_specs = [pl.BlockSpec(a.shape, lambda i: (0, 0), pipeline_mode=once) for a in arrays]
    in_specs += [pl.BlockSpec((1, width), lambda i: (0, 0), pipeline_mode=once)] * 2
    size = len(order) * rows * width
    return pl.pallas_call(
        kernel,
        grid=(len(order),),
        in_specs=in_specs,
        out_specs=pl.BlockSpec((rows, width), lambda i: (i, 0)),
        out_shape=jax.ShapeDtypeStruct((len(order) * rows, width), BF),
        compiler_params=pltpu.CompilerParams(vmem_limit_bytes=40 * 1024 * 1024),
        cost_estimate=pl.CostEstimate(flops=size * 10, bytes_accessed=4 * size, transcendentals=0),
        name="norm_rows",
    )(*arrays, gain[None, :], shift[None, :])


def join_blocks(found, order, rows):
    arrays, places = pick_rows(found, order, rows)
    width = arrays[0].shape[1]

    def kernel(*refs):
        out, arrived = refs[-2], refs[-1]
        copies = []
        for number, (which, block) in enumerate(places):
            source = refs[which].at[pl.ds(block * rows, rows), :]
            target = out.at[pl.ds(number * rows, rows), :]
            copies.append(pltpu.make_async_copy(source, target, arrived.at[number]))
        for copy in copies:
            copy.start()
        for copy in copies:
            copy.wait()

    size = len(order) * rows * width
    return pl.pallas_call(
        kernel,
        in_specs=[pl.BlockSpec(memory_space=pl.ANY)] * len(arrays),
        out_specs=pl.BlockSpec(memory_space=pl.ANY),
        out_shape=jax.ShapeDtypeStruct((len(order) * rows, width), BF),
        scratch_shapes=[pltpu.SemaphoreType.DMA((len(order),))],
        cost_estimate=pl.CostEstimate(flops=size, bytes_accessed=4 * size, transcendentals=0),
        name="join_rows",
    )(*arrays)


def deal_columns(matrices, chunks):
    rows = matrices[0].shape[0]
    width = sum(stop - start for parts in chunks for start, stop in parts[0])
    size = rows * width * len(chunks[0])

    def kernel(*refs):
        values = [ref[...].astype(F32) for ref in refs[:-1]]
        for target in range(len(chunks[0])):
            part = [
                x[:, start:stop] for x, parts in zip(values, chunks) for start, stop in parts[target]
            ]
            refs[-1][target] = jnp.concatenate(part, axis=1).astype(BF)

    return pl.pallas_call(
        kernel,
        out_shape=jax.ShapeDtypeStruct((len(chunks[0]), rows, width), BF),
        cost_estimate=pl.CostEstimate(flops=size, bytes_accessed=4 * size, transcendentals=0),
        name="deal_columns",
    )(*matrices)


def collect_columns(blocks, chunks):
    order = []
    for source, parts in enumerate(chunks):
        place = 0
        for start, stop in parts:
            order.append((start, source, place, place + stop - start))
            place += stop - start
    order.sort()
    width = blocks.shape[0] * blocks.shape[2]

    def kernel(x_ref, o_ref):
        x = [x_ref[source].astype(F32) for source in range(len(chunks))]
        o_ref[...] = jnp.concatenate([x[i][:, low:high] for _, i, low, high in order], axis=1)

    return pl.pallas_call(
        kernel,
        out_shape=jax.ShapeDtypeStruct((blocks.shape[1], width), F32),
        cost_estimate=pl.CostEstimate(
            flops=blocks.size, bytes_accessed=6 * blocks.size, transcendentals=0
        ),
        name="collect_columns",
    )(blocks)


def exchange(value, axis, size, offset):
    return lax.ppermute(value, axis, [(i, i ^ offset) for i in range(size)])


def after(value, *others):
    return lax.optimization_barrier((value,) + others)[0]


def half_blocks(size):
    if size == 4:
        return [(0, 0), (0, 1), (1, 0), (2, 1), (2, 0), (3, 0), (1, 1), (3, 1)]
    return [(j, half) for j in range(size) for half in range(2)]


def split_halves(value, j, found):
    half = value.shape[0] // 2
    found[j, 0], found[j, 1] = (value, 0), (value, half)


def gather_two(first, second, size, wait):
    send = functools.partial(exchange, axis="ctx", size=size)
    half = first.shape[0] // 2
    left, right = {}, {}
    split_halves(first, 0, left)
    split_halves(second, 0, right)
    if size != 4:
        for j in range(1, size):
            split_halves(send(first, offset=j), j, left)
        for j in range(1, size):
            split_halves(send(second, offset=j), j, right)
        return left, right, first
    one, two = send(first, offset=1), send(first, offset=2)
    split_halves(one, 1, left)
    split_halves(two, 2, left)
    one, two, second = lax.optimization_barrier((one, two, second) + wait)[:3]
    near = send(jnp.concatenate([two[half:], second], axis=0), offset=1)
    far = send(jnp.concatenate([one[:half], second], axis=0), offset=2)
    left[3, 0], left[3, 1] = (far, 0), (near, 0)
    right[1, 0], right[1, 1] = (near, half), (near, 2 * half)
    right[2, 0], right[2, 1] = (far, half), (far, 2 * half)
    right[3, 0] = (send(near[half : 2 * half], offset=2), 0)
    right[3, 1] = (send(far[2 * half :], offset=1), 0)
    return left, right, one


def sum_cut(size):
    return 4 if size == 4 else 2


def sum_blocks(away, size):
    away = away.astype(BF)
    if size != 4:
        blocks = away.reshape(size - 1, -1, away.shape[1])
        arrived = tuple(exchange(blocks[j - 1], "ctx", size, j) for j in range(1, size))
        return arrived, lambda own: (sum([x.astype(F32) for x in arrived], own), arrived)
    half = away.shape[0] // 4
    arrived = (
        exchange(away[: 2 * half], "ctx", size, 2),
        exchange(away[2 * half :], "ctx", size, 1),
    )

    def finish(own):
        far, near = arrived[0].astype(F32), arrived[1].astype(F32)
        top = exchange((own[2 * half : 3 * half] + far[half:]).astype(BF), "ctx", size, 1)
        low = exchange((own[3 * half :] + near[half:]).astype(BF), "ctx", size, 2)
        last = (top, low)
        top = own[:half] + far[:half] + top.astype(F32)
        low = own[half : 2 * half] + near[:half] + low.astype(F32)
        return jnp.concatenate([top, low], axis=0), last

    return arrived, finish


def gather_small(value, devices):
    copies = jnp.broadcast_to(value, (devices,) + value.shape)
    return lax.all_to_all(copies, ALL, split_axis=0, concat_axis=0, tiled=True)


def gather_dp(value):
    return lax.all_gather(value, "dp", axis=0, tiled=True)


def scatter_dp(value):
    return lax.psum_scatter(value, "dp", scatter_dimension=0, tiled=True)


def swap_ctx(value):
    return lax.all_to_all(value, "ctx", split_axis=0, concat_axis=0, tiled=True)


def matmul(a, b):
    return jnp.dot(a, b, preferred_element_type=F32)


def matmul_t(a, b):
    return lax.dot_general(a, b, (((1,), (1,)), ((), ())), preferred_element_type=F32)


def outer(a, b):
    return lax.dot_general(a, b, (((0,), (0,)), ((), ())), preferred_element_type=F32)


CONTRACT = {"nn": ((1,), (0,)), "nt": ((1,), (1,)), "tn": ((0,), (0,))}


def tile_of(size):
    return next(t for t in (1024, 768, 512, 384, 256, 128, size) if size % t == 0)


def product(kind, pairs, outs=(BF,), finish=None, extras=(), row_range=None):
    a, b = pairs[0]
    rows = a.shape[1] if kind == "tn" else a.shape[0]
    columns = b.shape[0] if kind == "nt" else b.shape[1]
    low, high = row_range or (0, rows)
    tall, wide = tile_of(high - low), tile_of(columns)
    skip = low // tall
    in_specs, operands = [], []
    for a, b in pairs:
        if kind == "tn":
            in_specs.append(pl.BlockSpec((a.shape[0], tall), lambda j, i: (0, i + skip)))
        else:
            in_specs.append(pl.BlockSpec((tall, a.shape[1]), lambda j, i: (i + skip, 0)))
        if kind == "nt":
            in_specs.append(pl.BlockSpec((wide, b.shape[1]), lambda j, i: (j, 0)))
        else:
            in_specs.append(pl.BlockSpec((b.shape[0], wide), lambda j, i: (0, j)))
        operands += [a, b]
    for extra in extras:
        if extra.shape[0] == 1:
            in_specs.append(pl.BlockSpec((1, wide), lambda j, i: (0, j)))
        else:
            in_specs.append(pl.BlockSpec((tall, wide), lambda j, i: (i + skip, j)))
        operands.append(extra)
    count, chunk = len(pairs), min(256, wide)
    depth = sum(a.shape[0] if kind == "tn" else a.shape[1] for a, _ in pairs)

    def kernel(*refs):
        for start in range(0, wide, chunk):
            part = slice(start, start + chunk)
            total = None
            for p in range(count):
                right = refs[2 * p + 1]
                right = right[part, :] if kind == "nt" else right[:, part]
                term = lax.dot_general(
                    refs[2 * p][...], right, (CONTRACT[kind], ((), ())), preferred_element_type=F32
                )
                total = term if total is None else total + term
            more = [refs[2 * count + n][:, part] for n in range(len(extras))]
            results = finish(total, *more) if finish else (total,)
            for ref, value in zip(refs[-len(outs) :], results):
                ref[:, part] = value.astype(ref.dtype)

    shape = (high - low, columns)
    result = pl.pallas_call(
        kernel,
        grid=(columns // wide, (high - low) // tall),
        in_specs=in_specs,
        out_specs=[pl.BlockSpec((tall, wide), lambda j, i: (i, j))] * len(outs),
        out_shape=[jax.ShapeDtypeStruct(shape, dtype) for dtype in outs],
        compiler_params=pltpu.CompilerParams(vmem_limit_bytes=56 * 1024 * 1024),
        cost_estimate=pl.CostEstimate(
            flops=int(2 * FRACTION * shape[0] * shape[1] * depth),
            bytes_accessed=shape[0] * shape[1],
            transcendentals=0,
        ),
        name="product_" + kind,
    )(*operands)
    return result if len(outs) > 1 else result[0]


def standardise(hidden):
    average = jnp.mean(hidden, axis=-1, keepdims=True)
    centred = hidden - average
    variance = jnp.mean(centred * centred, axis=-1, keepdims=True)
    scale = lax.rsqrt(variance + EPS)
    return centred * scale, scale


def gelu_pair(x):
    root, cubic = math.sqrt(2.0 / math.pi), 0.044715
    square = x * x
    gate = 0.5 + 0.5 * jnp.tanh(x * (root + (root * cubic) * square))
    value = x * gate
    slope = gate + value * (1.0 - gate) * (2.0 * root + (6.0 * root * cubic) * square)
    return value, slope


def on_device(
    hidden_in,
    ln_gain,
    ln_bias,
    w_qkv,
    b_qkv,
    w_out,
    b_out,
    w_up,
    b_up,
    w_down,
    b_down,
    segment_ids,
    positions,
    token_order,
    grad_out,
):
    N, C = lax.axis_size("dp"), lax.axis_size("ctx")
    c = lax.axis_index("ctx")
    rows, own_slots, width = hidden_in.shape
    assert rows == 1
    heads = width // HEAD
    own_heads = heads // C
    groups = own_heads // 2
    ff_block = w_down.shape[0]
    row_block = w_qkv.shape[0]
    own_ff = N * ff_block
    hidden_own = hidden_in.reshape(own_slots, width)
    grad_own = grad_out.reshape(own_slots, width)


    sizes = [ln_gain.shape[0], ln_bias.shape[0], b_qkv.shape[0], b_out.shape[0]]
    sizes += [b_up.shape[0], b_down.shape[0]]
    cuts = [sum(sizes[:i]) for i in range(1, len(sizes))]
    small = jnp.concatenate([ln_gain, ln_bias, b_qkv, b_out, b_up, b_down])
    small = gather_small(small, N * C)
    hidden_parts, grad_parts, arrived = gather_two(hidden_own, grad_own, C, (small,))
    pieces = jnp.split(small, cuts, axis=1)
    gain, shift, qkv_bias, out_bias, up_bias, down_bias = [p.reshape(-1).astype(F32) for p in pieces]
    qkv_chunks = [
        [
            (part * width + (i * C + t) * HEAD, part * width + (i * C + t + 1) * HEAD)
            for pair in range(groups)
            for part in range(3)
            for i in (2 * pair, 2 * pair + 1)
        ]
        for t in range(C)
    ]
    up_chunks = [
        [((i * C + t) * ff_block, (i * C + t + 1) * ff_block) for i in range(N)] for t in range(C)
    ]
    aligned = row_block == HEAD
    if aligned:
        w_out_own = gather_dp(w_out)
    else:
        everything = lax.all_gather(w_out, ALL, axis=0, tiled=True)
        everything = everything.reshape(own_heads, C, HEAD, width)
        w_out_own = lax.dynamic_index_in_dim(everything, c, 1, keepdims=False)
        w_out_own = w_out_own.reshape(own_heads * HEAD, width)
    both_rows = swap_ctx(deal_columns((w_up, w_qkv), (up_chunks, qkv_chunks)))
    both_rows = both_rows.reshape(C * row_block, -1)
    up_rows, qkv_rows = both_rows[:, :own_ff], both_rows[:, own_ff:]
    w_up_own = gather_dp(up_rows)
    w_qkv_own = gather_dp(qkv_rows)

    half_block = jnp.array([j for j, _ in half_blocks(C)], jnp.int32) ^ c
    half_block = 2 * half_block + jnp.array([half for _, half in half_blocks(C)], jnp.int32)
    row_order, row_ids = token_order.reshape(-1), segment_ids.reshape(-1)
    slots = row_order.shape[0]
    first = jnp.zeros_like(row_order)
    for document in range(DOCS):
        inside = row_ids == document
        first = jnp.where(inside, jnp.min(jnp.where(inside, row_order, slots)), first)
    order_all, first_all = [
        jnp.take(x.reshape(2 * C, -1), half_block, axis=0).reshape(-1) for x in (row_order, first)
    ]
    position_all = order_all - first_all
    block_place = order_all[::BLK] // BLK
    slot_block = jnp.argsort(block_place).astype(jnp.int32)
    first_place = jnp.take(first_all.reshape(-1, BLK), slot_block, axis=0)
    half = ROT // 2
    frequency = 10000.0 ** (-jnp.arange(half, dtype=F32) * 2.0 / ROT)
    angles = position_all.astype(F32)[:, None] * frequency
    cosine, sine = jnp.cos(angles), jnp.sin(angles)
    rest = jnp.zeros((slots, HEAD - ROT), F32)
    cosine = jnp.concatenate([cosine, cosine, rest + 1.0] * 2, axis=1)
    sine = jnp.concatenate([-sine, sine, rest] * 2, axis=1)

    own_bias = lax.dynamic_index_in_dim(qkv_bias.reshape(3, groups, 2, C, HEAD), c, 3, keepdims=False)
    own_bias = own_bias.transpose(1, 0, 2, 3).reshape(-1)
    gain, cosine, sine, first_place, block_place, slot_block, own_bias = lax.optimization_barrier(
        (gain, cosine, sine, first_place, block_place, slot_block, own_bias)
    )
    step = own_slots // 2
    normed = norm_blocks(hidden_parts, half_blocks(C), step, gain, shift)
    w_down_own = gather_dp(after(w_down, arrived))
    own_up_bias = lax.dynamic_index_in_dim(up_bias.reshape(N, C, ff_block), c, 1, keepdims=False)
    up = matmul(after(normed, w_out_own), w_up_own) + own_up_bias.reshape(-1)
    value, slope = gelu_pair(up)
    active, slope = lax.optimization_barrier((value.astype(BF), slope))
    if C == 4:
        for key in ((3, 0), (3, 1)):
            grad_parts[key] = (after(grad_parts[key][0], active), grad_parts[key][1])
    grad_all = join_blocks(grad_parts, half_blocks(C), step)
    down_part = outer(active, grad_all).astype(BF)
    down_grad = scatter_dp(down_part).astype(F32)

    qkv = matmul(after(normed, down_part), w_qkv_own) + own_bias
    d_attended = matmul_t(after(grad_all, down_part), w_out_own).astype(BF)
    attended, d_qkv = attention(
        qkv, d_attended, cosine, sine, first_place, block_place, slot_block
    )

    def column_grad(part, chunks):
        own = scatter_dp(part)
        return collect_columns(swap_ctx(own.reshape(C, row_block, -1)), chunks)

    cut = sum_cut(C) * step

    def out_rows(rows, attended):
        return matmul(attended[rows], w_out_own) + matmul(active[rows], w_down_own)

    out_part = outer(attended, after(grad_all, w_down_own))
    if aligned:
        out_part = out_part.astype(BF)
        out_grad = scatter_dp(out_part).astype(F32)
    else:
        spread = jnp.zeros((own_heads, C, HEAD, width), F32)
        spread = lax.dynamic_update_index_in_dim(
            spread, out_part.reshape(own_heads, HEAD, width), c, 1
        )
        out_grad = lax.psum_scatter(
            spread.reshape(heads * HEAD, width), ALL, scatter_dimension=0, tiled=True
        )

    qkv_part = outer(after(normed, down_grad, out_part), d_qkv).astype(BF)
    qkv_grad = column_grad(qkv_part, qkv_chunks)

    out_away = out_rows(slice(cut, None), after(attended, qkv_part)).astype(BF)
    out_arrived, finish = sum_blocks(out_away, C)
    out_near = out_rows(slice(0, cut), after(attended, out_away))
    grad_then = after(grad_all, out_near)
    d_up = (matmul_t(grad_then, w_down_own) * slope).astype(BF)
    up_part = outer(normed, d_up).astype(BF)
    up_grad = column_grad(up_part, up_chunks)
    out_sum, out_last = finish(after(out_near, d_up))
    output = hidden_own.astype(F32) + out_sum + (out_bias + down_bias)
    output = output.astype(BF).reshape(hidden_in.shape)

    d_qkv_then, d_up_then = lax.optimization_barrier((d_qkv, d_up, up_part, qkv_grad) + out_last)[:2]

    def normed_rows(row_range, dtype):
        pairs = [(d_qkv_then, w_qkv_own), (d_up_then, w_up_own)]
        return product("nt", pairs, (dtype,), row_range=row_range)

    d_away = normed_rows((cut, slots), BF)
    d_near = normed_rows((0, cut), F32)
    d_normed, _ = sum_blocks(d_away, C)[1](d_near)
    xhat, scale = standardise(hidden_own.astype(F32))
    e = d_normed * gain
    d_hidden = e - jnp.mean(e, axis=-1, keepdims=True)
    d_hidden = (d_hidden - xhat * jnp.mean(e * xhat, axis=-1, keepdims=True)) * scale
    grad_in = (grad_own.astype(F32) + d_hidden).astype(BF).reshape(hidden_in.shape)

    devices = N * C
    gain_grad = jnp.sum(d_normed * xhat, axis=0)
    shift_grad = jnp.sum(d_normed, axis=0)
    bias_grad = jnp.sum(grad_own.astype(F32), axis=0)
    up_bias_grad = jnp.sum(d_up.astype(F32), axis=0).reshape(N, 1, ff_block)
    qkv_bias_grad = jnp.sum(d_qkv.astype(F32), axis=0).reshape(groups, 3, 2, HEAD)
    qkv_bias_grad = qkv_bias_grad.transpose(1, 0, 2, 3)[:, :, :, None, :]
    mine = jnp.arange(C) == c
    up_bias_grad = jnp.where(mine[None, :, None], up_bias_grad, 0.0)
    qkv_bias_grad = jnp.where(mine[None, None, None, :, None], qkv_bias_grad, 0.0)
    small = [gain_grad, shift_grad, qkv_bias_grad, bias_grad, up_bias_grad]
    small = jnp.concatenate([s.reshape(devices, -1) for s in small], axis=1)
    small = after(small, grad_in)
    small = lax.all_to_all(small, ALL, split_axis=0, concat_axis=0, tiled=True)
    small = jnp.split(jnp.sum(small, axis=0), cuts[:4])

    return (
        output,
        grad_in,
        small[0],
        small[1],
        qkv_grad,
        small[2],
        out_grad,
        small[3],
        up_grad,
        small[4],
        down_grad,
        small[3],
    )


def solution(mesh):
    both = P(("dp", "ctx"))
    matrix = P(("dp", "ctx"), None)
    slots = P("dp", "ctx", None)
    in_specs = (
        slots,
        both,
        both,
        matrix,
        both,
        matrix,
        both,
        matrix,
        both,
        matrix,
        both,
        P("dp", None),
        P("dp", "ctx"),
        P("dp", None),
        slots,
    )
    out_specs = (
        slots,
        slots,
        both,
        both,
        matrix,
        both,
        matrix,
        both,
        matrix,
        both,
        matrix,
        both,
    )
    return jax.shard_map(
        on_device, mesh=mesh, in_specs=in_specs, out_specs=out_specs, check_vma=False
    )
```

```python
import functools
import math

import jax
import jax.numpy as jnp
from jax import lax
from jax.experimental import pallas as pl
from jax.experimental.pallas import tpu as pltpu
from jax.sharding import PartitionSpec as P

HEAD = 64
ROT = 32
BLK = 128
DOCS = 4
EPS = 1e-05
NEG = -1e30
PAIR = 2 * HEAD
KEYS = 256
LONGEST = 1024
PAIRS = 2
LOOSE = 2
FRACTION = 5.0
SCALE = HEAD**-0.5
ALL = ("dp", "ctx")
BF = jnp.bfloat16
F32 = jnp.float32


def partner(x):
    lane = lax.broadcasted_iota(jnp.int32, x.shape, 1) % HEAD
    return jnp.where(
        lane < ROT // 2, pltpu.roll(x, PAIR - ROT // 2, 1), pltpu.roll(x, ROT // 2, 1)
    )


def dot(a, b):
    return jnp.dot(a, b, preferred_element_type=F32)


def dot_t(a, b):
    return lax.dot_general(a, b, (((1,), (1,)), ((), ())), preferred_element_type=F32)


def aligned_rows(index, size):
    return pl.ds(pl.multiple_of(index * size, size), size)


def attention_kernel(
    place_ref,
    slot_ref,
    low_ref,
    qkv_ref,
    cot_ref,
    cos_ref,
    sin_ref,
    first_ref,
    att_ref,
    grad_ref,
    q_st,
    do_st,
    k_s,
    v_s,
    k_t,
    v_t,
    dk_s,
    dv_s,
    p_s,
    dp_s,
):
    slots = qkv_ref.shape[0]
    blocks = slots // BLK
    pairs = k_s.shape[0]
    lane_first = lax.broadcasted_iota(jnp.int32, (BLK, PAIR), 1) < HEAD
    row_first = lax.broadcasted_iota(jnp.int32, (PAIR, BLK), 0) < HEAD

    def stack(value):
        zero = jnp.zeros_like(value)
        both = [jnp.where(lane_first, value, zero), jnp.where(lane_first, zero, value)]
        return jnp.concatenate(both, axis=0).astype(BF)

    def columns(pair, which, count=3):
        start = (pair * count + which) * PAIR
        return slice(start, start + PAIR)

    def load_block(b, carry):
        rows = aligned_rows(b, BLK)
        place = place_ref[b]
        out_rows = aligned_rows(place, BLK)
        cosine = cos_ref[rows, :]
        sine = sin_ref[rows, :]
        for pair in range(pairs):
            q = qkv_ref[rows, columns(pair, 0)]
            k = qkv_ref[rows, columns(pair, 1)]
            v = qkv_ref[rows, columns(pair, 2)]
            q = (q * cosine + partner(q) * sine).astype(BF).astype(F32) * SCALE
            k = k * cosine + partner(k) * sine
            q_st[pair, aligned_rows(place, 2 * BLK), :] = stack(q)
            do = cot_ref[rows, columns(pair, 0, 1)].astype(F32)
            do_st[pair, aligned_rows(place, 2 * BLK), :] = stack(do)
            k_s[pair, out_rows, :] = k.astype(BF)
            v_s[pair, out_rows, :] = v.astype(BF)
            k_t[pair, out_rows, :] = k.T.astype(BF)
            v_t[pair, out_rows, :] = v.T.astype(BF)
        return carry

    lax.fori_loop(0, blocks, load_block, 0, unroll=LOOSE)
    dk_s[...] = jnp.zeros_like(dk_s)
    dv_s[...] = jnp.zeros_like(dv_s)

    def tiles_of(i, low, count):
        stacked = aligned_rows(i, 2 * BLK)
        first = first_ref[pl.ds(i, 1), :]
        row = lax.broadcasted_iota(jnp.int32, (KEYS, BLK), 0)
        own = i * BLK + lax.broadcasted_iota(jnp.int32, (1, BLK), 1)
        every = range(pairs)
        top = [None] * pairs
        for t in range(count):
            keys = aligned_rows(low + t, KEYS)
            part = slice(t * KEYS, (t + 1) * KEYS)
            place = (low + t) * KEYS
            allowed = row >= first - place
            if t == count - 1:
                allowed = allowed & (row <= own - place)
            allowed = jnp.concatenate([allowed, allowed], axis=1)
            for pair in every:
                s = dot_t(k_s[pair, keys, :], q_st[pair, stacked, :])
                s = jnp.where(allowed, s, NEG)
                p_s[pair, part, :] = s
                dp_s[pair, part, :] = dot_t(v_s[pair, keys, :], do_st[pair, stacked, :])
                here = jnp.max(s, axis=0, keepdims=True)
                top[pair] = here if t == 0 else jnp.maximum(top[pair], here)
        total = [0.0] * pairs
        inner = [0.0] * pairs
        for t in range(count):
            part = slice(t * KEYS, (t + 1) * KEYS)
            for pair in every:
                p = jnp.exp(p_s[pair, part, :] - top[pair])
                p_s[pair, part, :] = p
                total[pair] += jnp.sum(p, axis=0, keepdims=True)
                inner[pair] += jnp.sum(p * dp_s[pair, part, :], axis=0, keepdims=True)
        inverse = [1.0 / x for x in total]
        inner = [x * y for x, y in zip(inner, inverse)]
        out = [0.0] * pairs
        dq = [0.0] * pairs
        for t in range(count):
            part = slice(t * KEYS, (t + 1) * KEYS)
            keys = aligned_rows(low + t, KEYS)
            for pair in every:
                p = p_s[pair, part, :] * inverse[pair]
                ds = (p * (dp_s[pair, part, :] - inner[pair])).astype(BF)
                p = p.astype(BF)
                v_turned = v_t[pair, keys, :]
                k_turned = k_t[pair, keys, :]
                v_turned = jnp.concatenate([v_turned[:BLK], v_turned[BLK:]], axis=1)
                k_turned = jnp.concatenate([k_turned[:BLK], k_turned[BLK:]], axis=1)
                out[pair] += dot(v_turned, p)
                dq[pair] += dot(k_turned, ds)
                dv_s[pair, keys, :] += dot(p, do_st[pair, stacked, :])
                dk_s[pair, keys, :] += dot(ds, q_st[pair, stacked, :])
        slot_rows = aligned_rows(slot_ref[i], BLK)
        for pair in every:
            x = jnp.where(row_first, out[pair][:, :BLK], out[pair][:, BLK:]).T
            att_ref[slot_rows, columns(pair, 0, 1)] = x.astype(BF)
            x = (jnp.where(row_first, dq[pair][:, :BLK], dq[pair][:, BLK:]) * SCALE).T
            x = x * cos_ref[slot_rows, :] - partner(x) * sin_ref[slot_rows, :]
            grad_ref[slot_rows, columns(pair, 0)] = x.astype(BF)

    most = p_s.shape[1] // KEYS

    def query_block(i, carry):
        low = low_ref[i]
        count = (i * BLK) // KEYS + 1 - low
        for n in range(1, most + 1):
            pl.when(count == n)(functools.partial(tiles_of, i, low, n))
        return carry

    lax.fori_loop(0, blocks, query_block, 0)

    def store_block(b, carry):
        rows = aligned_rows(b, BLK)
        in_rows = aligned_rows(place_ref[b], BLK)
        for pair in range(pairs):
            dk = dk_s[pair, in_rows, :]
            dk = dk * cos_ref[rows, :] - partner(dk) * sin_ref[rows, :]
            grad_ref[rows, columns(pair, 1)] = dk.astype(BF)
            grad_ref[rows, columns(pair, 2)] = dv_s[pair, in_rows, :].astype(BF)
        return carry

    lax.fori_loop(0, blocks, store_block, 0, unroll=LOOSE)


def attention(qkv, cotangent, cosine, sine, first_place, block_place, slot_block):
    slots, width = qkv.shape
    groups = width // (3 * PAIR)
    pairs = math.gcd(groups, PAIRS)
    wide = pairs * PAIR
    blocks = slots // BLK
    low = first_place[:, 0] // KEYS
    once = pl.Buffered(1)
    most = min(LONGEST // KEYS + 1, slots // KEYS)
    grid_spec = pltpu.PrefetchScalarGridSpec(
        num_scalar_prefetch=3,
        grid=(groups // pairs,),
        in_specs=[
            pl.BlockSpec((slots, 3 * wide), lambda g, *_: (0, g)),
            pl.BlockSpec((slots, wide), lambda g, *_: (0, g)),
            pl.BlockSpec((slots, PAIR), lambda g, *_: (0, 0), pipeline_mode=once),
            pl.BlockSpec((slots, PAIR), lambda g, *_: (0, 0), pipeline_mode=once),
            pl.BlockSpec((blocks, BLK), lambda g, *_: (0, 0), pipeline_mode=once),
        ],
        out_specs=[
            pl.BlockSpec((slots, wide), lambda g, *_: (0, g)),
            pl.BlockSpec((slots, 3 * wide), lambda g, *_: (0, g)),
        ],
        scratch_shapes=[
            pltpu.VMEM((pairs, 2 * slots, PAIR), BF),
            pltpu.VMEM((pairs, 2 * slots, PAIR), BF),
            pltpu.VMEM((pairs, slots, PAIR), BF),
            pltpu.VMEM((pairs, slots, PAIR), BF),
            pltpu.VMEM((pairs, slots, PAIR), BF),
            pltpu.VMEM((pairs, slots, PAIR), BF),
            pltpu.VMEM((pairs, slots, PAIR), F32),
            pltpu.VMEM((pairs, slots, PAIR), F32),
            pltpu.VMEM((pairs, most * KEYS, 2 * BLK), F32),
            pltpu.VMEM((pairs, most * KEYS, 2 * BLK), F32),
        ],
    )
    tiles = groups * blocks * (blocks // 4)
    return pl.pallas_call(
        attention_kernel,
        out_shape=[
            jax.ShapeDtypeStruct((slots, groups * PAIR), BF),
            jax.ShapeDtypeStruct((slots, width), BF),
        ],
        grid_spec=grid_spec,
        compiler_params=pltpu.CompilerParams(vmem_limit_bytes=50 * 1024 * 1024),
        cost_estimate=pl.CostEstimate(
            flops=tiles * 2 * BLK * BLK * PAIR,
            bytes_accessed=qkv.size,
            transcendentals=0,
        ),
        name="attention",
    )(block_place, slot_block, low, qkv, cotangent, cosine, sine, first_place)


def pick_rows(found, order, rows):
    arrays, places = [], []
    for key in order:
        array, start = found[key]
        held = [i for i, known in enumerate(arrays) if known is array]
        if not held:
            arrays.append(array)
            held = [len(arrays) - 1]
        places.append((held[0], start // rows))
    return arrays, places


def visit_blocks(body, found, order, rows, extra, outs, name):
    arrays, places = pick_rows(found, order, rows)
    width = arrays[0].shape[1]

    def kernel(*refs):
        step = pl.program_id(0)
        given = refs[len(arrays) : len(arrays) + len(extra)]
        for number, (which, block) in enumerate(places):

            @pl.when(step == number)
            def _(ref=refs[which], block=block):
                results = body(ref[block * rows : (block + 1) * rows, :], *[g[...] for g in given])
                for out, value in zip(refs[-outs:], results):
                    out[...] = value

    once = pl.Buffered(1)
    held = arrays + list(extra)
    size = len(order) * rows * width
    return pl.pallas_call(
        kernel,
        grid=(len(order),),
        in_specs=[pl.BlockSpec(a.shape, lambda i: (0, 0), pipeline_mode=once) for a in held],
        out_specs=[pl.BlockSpec((rows, width), lambda i: (i, 0))] * outs,
        out_shape=[jax.ShapeDtypeStruct((len(order) * rows, width), BF)] * outs,
        compiler_params=pltpu.CompilerParams(vmem_limit_bytes=40 * 1024 * 1024),
        cost_estimate=pl.CostEstimate(flops=size * 10, bytes_accessed=4 * size, transcendentals=0),
        name=name,
    )(*held)


def norm_blocks(found, order, rows, gain, shift):
    def body(x, gain, shift):
        x, _ = standardise(x.astype(F32))
        return (x * gain + shift).astype(BF), x.astype(BF)

    return visit_blocks(body, found, order, rows, [gain[None, :], shift[None, :]], 2, "norm_rows")


def join_blocks(found, order, rows):
    return visit_blocks(lambda x: (x,), found, order, rows, [], 1, "join_rows")[0]


def deal_columns(matrices, chunks):
    rows = matrices[0].shape[0]
    width = sum(stop - start for parts in chunks for start, stop in parts[0])
    size = rows * width * len(chunks[0])

    def kernel(*refs):
        values = [ref[...].astype(F32) for ref in refs[:-1]]
        for target in range(len(chunks[0])):
            part = [
                x[:, start:stop] for x, parts in zip(values, chunks) for start, stop in parts[target]
            ]
            refs[-1][target] = jnp.concatenate(part, axis=1).astype(BF)

    return pl.pallas_call(
        kernel,
        out_shape=jax.ShapeDtypeStruct((len(chunks[0]), rows, width), BF),
        cost_estimate=pl.CostEstimate(flops=size, bytes_accessed=4 * size, transcendentals=0),
        name="deal_columns",
    )(*matrices)


def collect_columns(blocks, chunks):
    order = []
    for source, parts in enumerate(chunks):
        place = 0
        for start, stop in parts:
            order.append((start, source, place, place + stop - start))
            place += stop - start
    order.sort()
    width = blocks.shape[0] * blocks.shape[2]

    def kernel(x_ref, o_ref):
        x = [x_ref[source].astype(F32) for source in range(len(chunks))]
        o_ref[...] = jnp.concatenate([x[i][:, low:high] for _, i, low, high in order], axis=1)

    return pl.pallas_call(
        kernel,
        out_shape=jax.ShapeDtypeStruct((blocks.shape[1], width), F32),
        cost_estimate=pl.CostEstimate(
            flops=blocks.size, bytes_accessed=6 * blocks.size, transcendentals=0
        ),
        name="collect_columns",
    )(blocks)


def exchange(value, axis, size, offset):
    return lax.ppermute(value, axis, [(i, i ^ offset) for i in range(size)])


def after(value, *others):
    return lax.optimization_barrier((value,) + others)[0]


def half_blocks(size):
    if size == 4:
        return [(0, 0), (0, 1), (1, 0), (2, 1), (2, 0), (3, 0), (1, 1), (3, 1)]
    return [(j, half) for j in range(size) for half in range(2)]


def split_halves(value, j, found):
    half = value.shape[0] // 2
    found[j, 0], found[j, 1] = (value, 0), (value, half)


def gather_two(first, second, size, wait):
    send = functools.partial(exchange, axis="ctx", size=size)
    half = first.shape[0] // 2
    left, right = {}, {}
    split_halves(first, 0, left)
    split_halves(second, 0, right)
    if size != 4:
        for j in range(1, size):
            split_halves(send(first, offset=j), j, left)
        for j in range(1, size):
            split_halves(send(second, offset=j), j, right)
        return left, right, (right[1, 0][0],)
    one, two = send(first, offset=1), send(first, offset=2)
    split_halves(one, 1, left)
    split_halves(two, 2, left)
    one, two, second = lax.optimization_barrier((one, two, second) + wait)[:3]
    near = send(jnp.concatenate([two[half:], second], axis=0), offset=1)
    far = send(jnp.concatenate([one[:half], second], axis=0), offset=2)
    left[3, 0], left[3, 1] = (far, 0), (near, 0)
    right[1, 0], right[1, 1] = (near, half), (near, 2 * half)
    right[2, 0], right[2, 1] = (far, half), (far, 2 * half)
    right[3, 0] = (send(near[half : 2 * half], offset=2), 0)
    right[3, 1] = (send(far[2 * half :], offset=1), 0)
    return left, right, (near, far)


def sum_ranges(size):
    if size == 4:
        return (0, 4), [(4, 6), (6, 8)]
    return (0, 2), [(2 * j, 2 * j + 2) for j in range(1, size)]


def sum_send(pieces, size):
    distances = (2, 1) if size == 4 else range(1, size)
    return tuple(exchange(x.astype(BF), "ctx", size, j) for x, j in zip(pieces, distances))


def sum_end(own, arrived, size):
    if size != 4:
        return sum([x.astype(F32) for x in arrived], own), arrived
    half = own.shape[0] // 4
    far, near = arrived[0].astype(F32), arrived[1].astype(F32)
    top = exchange((own[2 * half : 3 * half] + far[half:]).astype(BF), "ctx", size, 1)
    low = exchange((own[3 * half :] + near[half:]).astype(BF), "ctx", size, 2)
    last = (top, low)
    top = own[:half] + far[:half] + top.astype(F32)
    low = own[half : 2 * half] + near[:half] + low.astype(F32)
    return jnp.concatenate([top, low], axis=0), last


def gather_small(value, devices):
    copies = jnp.broadcast_to(value, (devices,) + value.shape)
    return lax.all_to_all(copies, ALL, split_axis=0, concat_axis=0, tiled=True)


def gather_dp(value):
    return lax.all_gather(value, "dp", axis=0, tiled=True)


def scatter_dp(value):
    return lax.psum_scatter(value, "dp", scatter_dimension=0, tiled=True)


def swap_ctx(value):
    return lax.all_to_all(value, "ctx", split_axis=0, concat_axis=0, tiled=True)


def matmul(a, b):
    return jnp.dot(a, b, preferred_element_type=F32)


def matmul_t(a, b):
    return lax.dot_general(a, b, (((1,), (1,)), ((), ())), preferred_element_type=F32)


def outer(a, b):
    return lax.dot_general(a, b, (((0,), (0,)), ((), ())), preferred_element_type=F32)


CONTRACT = {"nn": ((1,), (0,)), "nt": ((1,), (1,)), "tn": ((0,), (0,))}


def tile_of(size):
    return next(t for t in (1024, 768, 512, 384, 256, 128, size) if size % t == 0)


def product(kind, pairs, outs=(BF,), finish=None, extras=(), row_range=None):
    a, b = pairs[0]
    rows = a.shape[1] if kind == "tn" else a.shape[0]
    columns = b.shape[0] if kind == "nt" else b.shape[1]
    low, high = row_range or (0, rows)
    tall, wide = tile_of(high - low), tile_of(columns)
    skip = low // tall
    in_specs, operands = [], []
    for a, b in pairs:
        if kind == "tn":
            in_specs.append(pl.BlockSpec((a.shape[0], tall), lambda j, i: (0, i + skip)))
        else:
            in_specs.append(pl.BlockSpec((tall, a.shape[1]), lambda j, i: (i + skip, 0)))
        if kind == "nt":
            in_specs.append(pl.BlockSpec((wide, b.shape[1]), lambda j, i: (j, 0)))
        else:
            in_specs.append(pl.BlockSpec((b.shape[0], wide), lambda j, i: (0, j)))
        operands += [a, b]
    for extra in extras:
        if extra.shape[0] == 1:
            in_specs.append(pl.BlockSpec((1, wide), lambda j, i: (0, j)))
        else:
            in_specs.append(pl.BlockSpec((tall, wide), lambda j, i: (i + skip, j)))
        operands.append(extra)
    count, chunk = len(pairs), min(256, wide)
    depth = sum(a.shape[0] if kind == "tn" else a.shape[1] for a, _ in pairs)

    def kernel(*refs):
        for start in range(0, wide, chunk):
            part = slice(start, start + chunk)
            total = None
            for p in range(count):
                right = refs[2 * p + 1]
                right = right[part, :] if kind == "nt" else right[:, part]
                term = lax.dot_general(
                    refs[2 * p][...], right, (CONTRACT[kind], ((), ())), preferred_element_type=F32
                )
                total = term if total is None else total + term
            more = [refs[2 * count + n][:, part] for n in range(len(extras))]
            results = finish(total, *more) if finish else (total,)
            for ref, value in zip(refs[-len(outs) :], results):
                ref[:, part] = value.astype(ref.dtype)

    shape = (high - low, columns)
    result = pl.pallas_call(
        kernel,
        grid=(columns // wide, (high - low) // tall),
        in_specs=in_specs,
        out_specs=[pl.BlockSpec((tall, wide), lambda j, i: (i, j))] * len(outs),
        out_shape=[jax.ShapeDtypeStruct(shape, dtype) for dtype in outs],
        compiler_params=pltpu.CompilerParams(vmem_limit_bytes=56 * 1024 * 1024),
        cost_estimate=pl.CostEstimate(
            flops=int(2 * FRACTION * shape[0] * shape[1] * depth),
            bytes_accessed=shape[0] * shape[1],
            transcendentals=0,
        ),
        name="product_" + kind,
    )(*operands)
    return result if len(outs) > 1 else result[0]


def standardise(hidden):
    average = jnp.mean(hidden, axis=-1, keepdims=True)
    centred = hidden - average
    variance = jnp.mean(centred * centred, axis=-1, keepdims=True)
    scale = lax.rsqrt(variance + EPS)
    return centred * scale, scale


def gelu_pair(x):
    root, cubic = math.sqrt(2.0 / math.pi), 0.044715
    square = x * x
    gate = 0.5 + 0.5 * jnp.tanh(x * (root + (root * cubic) * square))
    value = x * gate
    slope = gate + value * (1.0 - gate) * (2.0 * root + (6.0 * root * cubic) * square)
    return value, slope


def on_device(
    hidden_in,
    ln_gain,
    ln_bias,
    w_qkv,
    b_qkv,
    w_out,
    b_out,
    w_up,
    b_up,
    w_down,
    b_down,
    segment_ids,
    positions,
    token_order,
    grad_out,
):
    N, C = lax.axis_size("dp"), lax.axis_size("ctx")
    c = lax.axis_index("ctx")
    rows, own_slots, width = hidden_in.shape
    assert rows == 1
    heads = width // HEAD
    own_heads = heads // C
    groups = own_heads // 2
    ff_block = w_down.shape[0]
    row_block = w_qkv.shape[0]
    own_ff = N * ff_block
    hidden_own = hidden_in.reshape(own_slots, width)
    grad_own = grad_out.reshape(own_slots, width)


    sizes = [ln_gain.shape[0], ln_bias.shape[0], b_qkv.shape[0], b_out.shape[0]]
    sizes += [b_up.shape[0], b_down.shape[0]]
    cuts = [sum(sizes[:i]) for i in range(1, len(sizes))]
    small = jnp.concatenate([ln_gain, ln_bias, b_qkv, b_out, b_up, b_down])
    small = gather_small(small, N * C)
    hidden_parts, grad_parts, arrived = gather_two(hidden_own, grad_own, C, (small,))
    pieces = jnp.split(small, cuts, axis=1)
    gain, shift, qkv_bias, out_bias, up_bias, down_bias = [p.reshape(-1).astype(F32) for p in pieces]
    qkv_chunks = [
        [
            (part * width + (i * C + t) * HEAD, part * width + (i * C + t + 1) * HEAD)
            for pair in range(groups)
            for part in range(3)
            for i in (2 * pair, 2 * pair + 1)
        ]
        for t in range(C)
    ]
    up_chunks = [
        [((i * C + t) * ff_block, (i * C + t + 1) * ff_block) for i in range(N)] for t in range(C)
    ]
    aligned = row_block == HEAD
    if aligned:
        w_out_own = gather_dp(w_out)
    else:
        everything = lax.all_gather(w_out, ALL, axis=0, tiled=True)
        everything = everything.reshape(own_heads, C, HEAD, width)
        w_out_own = lax.dynamic_index_in_dim(everything, c, 1, keepdims=False)
        w_out_own = w_out_own.reshape(own_heads * HEAD, width)
    up_rows = swap_ctx(deal_columns((w_up,), (up_chunks,))).reshape(C * row_block, -1)
    qkv_send = deal_columns((w_qkv,), (qkv_chunks,))
    qkv_rows = swap_ctx(after(qkv_send, *arrived)).reshape(C * row_block, -1)
    w_up_own = gather_dp(up_rows)
    w_qkv_own = gather_dp(qkv_rows)

    half_block = jnp.array([j for j, _ in half_blocks(C)], jnp.int32) ^ c
    half_block = 2 * half_block + jnp.array([half for _, half in half_blocks(C)], jnp.int32)
    row_order, row_ids = token_order.reshape(-1), segment_ids.reshape(-1)
    slots = row_order.shape[0]
    first = jnp.zeros_like(row_order)
    for document in range(DOCS):
        inside = row_ids == document
        first = jnp.where(inside, jnp.min(jnp.where(inside, row_order, slots)), first)
    order_all, first_all = [
        jnp.take(x.reshape(2 * C, -1), half_block, axis=0).reshape(-1) for x in (row_order, first)
    ]
    position_all = order_all - first_all
    block_place = order_all[::BLK] // BLK
    slot_block = jnp.argsort(block_place).astype(jnp.int32)
    first_place = jnp.take(first_all.reshape(-1, BLK), slot_block, axis=0)
    half = ROT // 2
    frequency = 10000.0 ** (-jnp.arange(half, dtype=F32) * 2.0 / ROT)
    angles = position_all.astype(F32)[:, None] * frequency
    cosine, sine = jnp.cos(angles), jnp.sin(angles)
    rest = jnp.zeros((slots, HEAD - ROT), F32)
    cosine = jnp.concatenate([cosine, cosine, rest + 1.0] * 2, axis=1)
    sine = jnp.concatenate([-sine, sine, rest] * 2, axis=1)

    own_bias = lax.dynamic_index_in_dim(qkv_bias.reshape(3, groups, 2, C, HEAD), c, 3, keepdims=False)
    own_bias = own_bias.transpose(1, 0, 2, 3).reshape(-1)
    gain, cosine, sine, first_place, block_place, slot_block, own_bias = lax.optimization_barrier(
        (gain, cosine, sine, first_place, block_place, slot_block, own_bias)
    )
    step = own_slots // 2
    normed, xhat_all = norm_blocks(hidden_parts, half_blocks(C), step, gain, shift)
    w_down_own = gather_dp(after(w_down, up_rows))
    own_up_bias = lax.dynamic_index_in_dim(up_bias.reshape(N, C, ff_block), c, 1, keepdims=False)
    up = matmul(after(normed, w_out_own), w_up_own) + own_up_bias.reshape(-1)
    value, slope = gelu_pair(up)
    active, slope = lax.optimization_barrier((value.astype(BF), slope))
    if C == 4:
        for key in ((3, 0), (3, 1)):
            grad_parts[key] = (after(grad_parts[key][0], active), grad_parts[key][1])
    grad_all = join_blocks(grad_parts, half_blocks(C), step)
    down_part = outer(active, grad_all).astype(BF)
    down_grad = scatter_dp(down_part).astype(F32)

    d_attended = matmul_t(after(grad_all, down_part), w_out_own).astype(BF)

    def column_grad(part, chunks):
        own = scatter_dp(part)
        return own, collect_columns(swap_ctx(own.reshape(C, row_block, -1)), chunks)

    d_up = (matmul_t(after(grad_all, d_attended), w_down_own) * slope).astype(BF)
    up_part = outer(normed, d_up).astype(BF)
    up_rows_grad, up_grad = column_grad(up_part, up_chunks)

    qkv = matmul(after(normed, up_part), w_qkv_own) + own_bias
    attended, d_qkv = attention(
        qkv, d_attended, cosine, sine, first_place, block_place, slot_block
    )

    near_range, away_ranges = sum_ranges(C)

    def out_rows(half_range, dtype, attended):
        pairs = [(active, w_down_own), (attended, w_out_own)]
        return product("nn", pairs, (dtype,), row_range=[i * step for i in half_range])

    out_away = [out_rows(r, BF, attended) for r in away_ranges]
    out_arrived = sum_send(out_away, C)
    out_near = out_rows(near_range, F32, after(attended, *out_away))
    qkv_part = outer(after(normed, out_near, down_grad), d_qkv).astype(BF)
    _, qkv_grad = column_grad(qkv_part, qkv_chunks)
    out_sum, out_last = sum_end(after(out_near, qkv_part), out_arrived, C)
    output = hidden_own.astype(F32) + out_sum + (out_bias + down_bias)
    output = output.astype(BF).reshape(hidden_in.shape)

    def normed_rows(half_range, dtype, d_qkv):
        pairs = [(d_qkv, w_qkv_own), (d_up, w_up_own)]
        return product("nt", pairs, (dtype,), row_range=[i * step for i in half_range])

    d_away = [normed_rows(r, BF, after(d_qkv, qkv_part)) for r in away_ranges]
    d_arrived = sum_send(d_away, C)
    d_near = normed_rows(near_range, F32, after(d_qkv, up_rows_grad, *d_away, *out_last))
    out_part = outer(after(attended, d_near), grad_all)
    if aligned:
        out_part = out_part.astype(BF)
        out_grad = scatter_dp(out_part).astype(F32)
    else:
        spread = jnp.zeros((own_heads, C, HEAD, width), F32)
        spread = lax.dynamic_update_index_in_dim(
            spread, out_part.reshape(own_heads, HEAD, width), c, 1
        )
        out_grad = lax.psum_scatter(
            spread.reshape(heads * HEAD, width), ALL, scatter_dimension=0, tiled=True
        )

    devices = N * C
    gain_grad = shift_grad = 0.0
    for r, piece in zip([near_range] + away_ranges, [d_near] + d_away):
        piece = piece.astype(F32)
        gain_grad += jnp.sum(piece * xhat_all[r[0] * step : r[1] * step].astype(F32), axis=0)
        shift_grad += jnp.sum(piece, axis=0)
    bias_grad = jnp.sum(grad_own.astype(F32), axis=0)
    up_bias_grad = jnp.sum(d_up.astype(F32), axis=0).reshape(N, 1, ff_block)
    qkv_bias_grad = jnp.sum(d_qkv.astype(F32), axis=0).reshape(groups, 3, 2, HEAD)
    qkv_bias_grad = qkv_bias_grad.transpose(1, 0, 2, 3)[:, :, :, None, :]
    mine = jnp.arange(C) == c
    up_bias_grad = jnp.where(mine[None, :, None], up_bias_grad, 0.0)
    qkv_bias_grad = jnp.where(mine[None, None, None, :, None], qkv_bias_grad, 0.0)
    small = [gain_grad, shift_grad, qkv_bias_grad, bias_grad, up_bias_grad]
    small = jnp.concatenate([s.reshape(devices, -1) for s in small], axis=1)
    small = lax.all_to_all(small, ALL, split_axis=0, concat_axis=0, tiled=True)
    small = jnp.split(jnp.sum(small, axis=0), cuts[:4])

    d_normed, _ = sum_end(d_near, d_arrived, C)
    d_normed = after(d_normed, up_grad, *small)
    xhat, scale = standardise(hidden_own.astype(F32))
    e = d_normed * gain
    d_hidden = e - jnp.mean(e, axis=-1, keepdims=True)
    d_hidden = (d_hidden - xhat * jnp.mean(e * xhat, axis=-1, keepdims=True)) * scale
    grad_in = (grad_own.astype(F32) + d_hidden).astype(BF).reshape(hidden_in.shape)

    return (
        output,
        grad_in,
        small[0],
        small[1],
        qkv_grad,
        small[2],
        out_grad,
        small[3],
        up_grad,
        small[4],
        down_grad,
        small[3],
    )


def solution(mesh):
    both = P(("dp", "ctx"))
    matrix = P(("dp", "ctx"), None)
    slots = P("dp", "ctx", None)
    in_specs = (
        slots,
        both,
        both,
        matrix,
        both,
        matrix,
        both,
        matrix,
        both,
        matrix,
        both,
        P("dp", None),
        P("dp", "ctx"),
        P("dp", None),
        slots,
    )
    out_specs = (
        slots,
        slots,
        both,
        both,
        matrix,
        both,
        matrix,
        both,
        matrix,
        both,
        matrix,
        both,
    )
    return jax.shard_map(
        on_device, mesh=mesh, in_specs=in_specs, out_specs=out_specs, check_vma=False
    )
```

```python
import functools
import math

import jax
import jax.numpy as jnp
from jax import lax
from jax.experimental import pallas as pl
from jax.experimental.pallas import tpu as pltpu
from jax.sharding import PartitionSpec as P

HEAD = 64
ROT = 32
BLK = 128
DOCS = 4
EPS = 1e-05
NEG = -1e30
PAIR = 2 * HEAD
KEYS = 256
LONGEST = 1024
PAIRS = 2
LOOSE = 2
FRACTION = 5.0
SCALE = HEAD**-0.5
ALL = ("dp", "ctx")
BF = jnp.bfloat16
F32 = jnp.float32


def partner(x):
    lane = lax.broadcasted_iota(jnp.int32, x.shape, 1) % HEAD
    return jnp.where(
        lane < ROT // 2, pltpu.roll(x, PAIR - ROT // 2, 1), pltpu.roll(x, ROT // 2, 1)
    )


def dot(a, b):
    return jnp.dot(a, b, preferred_element_type=F32)


def dot_t(a, b):
    return lax.dot_general(a, b, (((1,), (1,)), ((), ())), preferred_element_type=F32)


def aligned_rows(index, size):
    return pl.ds(pl.multiple_of(index * size, size), size)


def attention_kernel(
    place_ref,
    slot_ref,
    low_ref,
    qkv_ref,
    cot_ref,
    cos_ref,
    sin_ref,
    first_ref,
    att_ref,
    grad_ref,
    q_st,
    do_st,
    k_s,
    v_s,
    k_t,
    v_t,
    dk_s,
    dv_s,
    p_s,
    dp_s,
):
    slots = qkv_ref.shape[0]
    blocks = slots // BLK
    pairs = k_s.shape[0]
    lane_first = lax.broadcasted_iota(jnp.int32, (BLK, PAIR), 1) < HEAD
    row_first = lax.broadcasted_iota(jnp.int32, (PAIR, BLK), 0) < HEAD

    def stack(value):
        zero = jnp.zeros_like(value)
        both = [jnp.where(lane_first, value, zero), jnp.where(lane_first, zero, value)]
        return jnp.concatenate(both, axis=0).astype(BF)

    def columns(pair, which, count=3):
        start = (pair * count + which) * PAIR
        return slice(start, start + PAIR)

    def load_block(b, carry):
        rows = aligned_rows(b, BLK)
        place = place_ref[b]
        out_rows = aligned_rows(place, BLK)
        cosine = cos_ref[rows, :]
        sine = sin_ref[rows, :]
        for pair in range(pairs):
            q = qkv_ref[rows, columns(pair, 0)]
            k = qkv_ref[rows, columns(pair, 1)]
            v = qkv_ref[rows, columns(pair, 2)]
            q = (q * cosine + partner(q) * sine).astype(BF).astype(F32) * SCALE
            k = k * cosine + partner(k) * sine
            q_st[pair, aligned_rows(place, 2 * BLK), :] = stack(q)
            do = cot_ref[rows, columns(pair, 0, 1)].astype(F32)
            do_st[pair, aligned_rows(place, 2 * BLK), :] = stack(do)
            k_s[pair, out_rows, :] = k.astype(BF)
            v_s[pair, out_rows, :] = v.astype(BF)
            k_t[pair, out_rows, :] = k.T.astype(BF)
            v_t[pair, out_rows, :] = v.T.astype(BF)
        return carry

    lax.fori_loop(0, blocks, load_block, 0, unroll=LOOSE)
    dk_s[...] = jnp.zeros_like(dk_s)
    dv_s[...] = jnp.zeros_like(dv_s)

    def tiles_of(i, low, count):
        stacked = aligned_rows(i, 2 * BLK)
        first = first_ref[pl.ds(i, 1), :]
        row = lax.broadcasted_iota(jnp.int32, (KEYS, BLK), 0)
        own = i * BLK + lax.broadcasted_iota(jnp.int32, (1, BLK), 1)
        every = range(pairs)
        top = [None] * pairs
        for t in range(count):
            keys = aligned_rows(low + t, KEYS)
            part = slice(t * KEYS, (t + 1) * KEYS)
            place = (low + t) * KEYS
            allowed = row >= first - place
            if t == count - 1:
                allowed = allowed & (row <= own - place)
            allowed = jnp.concatenate([allowed, allowed], axis=1)
            for pair in every:
                s = dot_t(k_s[pair, keys, :], q_st[pair, stacked, :])
                s = jnp.where(allowed, s, NEG)
                p_s[pair, part, :] = s
                dp_s[pair, part, :] = dot_t(v_s[pair, keys, :], do_st[pair, stacked, :])
                here = jnp.max(s, axis=0, keepdims=True)
                top[pair] = here if t == 0 else jnp.maximum(top[pair], here)
        total = [0.0] * pairs
        inner = [0.0] * pairs
        for t in range(count):
            part = slice(t * KEYS, (t + 1) * KEYS)
            for pair in every:
                p = jnp.exp(p_s[pair, part, :] - top[pair])
                p_s[pair, part, :] = p
                total[pair] += jnp.sum(p, axis=0, keepdims=True)
                inner[pair] += jnp.sum(p * dp_s[pair, part, :], axis=0, keepdims=True)
        inverse = [1.0 / x for x in total]
        inner = [x * y for x, y in zip(inner, inverse)]
        out = [0.0] * pairs
        dq = [0.0] * pairs
        for t in range(count):
            part = slice(t * KEYS, (t + 1) * KEYS)
            keys = aligned_rows(low + t, KEYS)
            for pair in every:
                p = p_s[pair, part, :] * inverse[pair]
                ds = (p * (dp_s[pair, part, :] - inner[pair])).astype(BF)
                p = p.astype(BF)
                v_turned = v_t[pair, keys, :]
                k_turned = k_t[pair, keys, :]
                v_turned = jnp.concatenate([v_turned[:BLK], v_turned[BLK:]], axis=1)
                k_turned = jnp.concatenate([k_turned[:BLK], k_turned[BLK:]], axis=1)
                out[pair] += dot(v_turned, p)
                dq[pair] += dot(k_turned, ds)
                dv_s[pair, keys, :] += dot(p, do_st[pair, stacked, :])
                dk_s[pair, keys, :] += dot(ds, q_st[pair, stacked, :])
        slot_rows = aligned_rows(slot_ref[i], BLK)
        for pair in every:
            x = jnp.where(row_first, out[pair][:, :BLK], out[pair][:, BLK:]).T
            att_ref[slot_rows, columns(pair, 0, 1)] = x.astype(BF)
            x = (jnp.where(row_first, dq[pair][:, :BLK], dq[pair][:, BLK:]) * SCALE).T
            x = x * cos_ref[slot_rows, :] - partner(x) * sin_ref[slot_rows, :]
            grad_ref[slot_rows, columns(pair, 0)] = x.astype(BF)

    most = p_s.shape[1] // KEYS

    def query_block(i, carry):
        low = low_ref[i]
        count = (i * BLK) // KEYS + 1 - low
        for n in range(1, most + 1):
            pl.when(count == n)(functools.partial(tiles_of, i, low, n))
        return carry

    lax.fori_loop(0, blocks, query_block, 0)

    def store_block(b, carry):
        rows = aligned_rows(b, BLK)
        in_rows = aligned_rows(place_ref[b], BLK)
        for pair in range(pairs):
            dk = dk_s[pair, in_rows, :]
            dk = dk * cos_ref[rows, :] - partner(dk) * sin_ref[rows, :]
            grad_ref[rows, columns(pair, 1)] = dk.astype(BF)
            grad_ref[rows, columns(pair, 2)] = dv_s[pair, in_rows, :].astype(BF)
        return carry

    lax.fori_loop(0, blocks, store_block, 0, unroll=LOOSE)


def attention(qkv, cotangent, cosine, sine, first_place, block_place, slot_block):
    slots, width = qkv.shape
    groups = width // (3 * PAIR)
    pairs = math.gcd(groups, PAIRS)
    wide = pairs * PAIR
    blocks = slots // BLK
    low = first_place[:, 0] // KEYS
    once = pl.Buffered(1)
    most = min(LONGEST // KEYS + 1, slots // KEYS)
    grid_spec = pltpu.PrefetchScalarGridSpec(
        num_scalar_prefetch=3,
        grid=(groups // pairs,),
        in_specs=[
            pl.BlockSpec((slots, 3 * wide), lambda g, *_: (0, g)),
            pl.BlockSpec((slots, wide), lambda g, *_: (0, g)),
            pl.BlockSpec((slots, PAIR), lambda g, *_: (0, 0), pipeline_mode=once),
            pl.BlockSpec((slots, PAIR), lambda g, *_: (0, 0), pipeline_mode=once),
            pl.BlockSpec((blocks, BLK), lambda g, *_: (0, 0), pipeline_mode=once),
        ],
        out_specs=[
            pl.BlockSpec((slots, wide), lambda g, *_: (0, g)),
            pl.BlockSpec((slots, 3 * wide), lambda g, *_: (0, g)),
        ],
        scratch_shapes=[
            pltpu.VMEM((pairs, 2 * slots, PAIR), BF),
            pltpu.VMEM((pairs, 2 * slots, PAIR), BF),
            pltpu.VMEM((pairs, slots, PAIR), BF),
            pltpu.VMEM((pairs, slots, PAIR), BF),
            pltpu.VMEM((pairs, slots, PAIR), BF),
            pltpu.VMEM((pairs, slots, PAIR), BF),
            pltpu.VMEM((pairs, slots, PAIR), F32),
            pltpu.VMEM((pairs, slots, PAIR), F32),
            pltpu.VMEM((pairs, most * KEYS, 2 * BLK), F32),
            pltpu.VMEM((pairs, most * KEYS, 2 * BLK), F32),
        ],
    )
    tiles = groups * blocks * (blocks // 4)
    return pl.pallas_call(
        attention_kernel,
        out_shape=[
            jax.ShapeDtypeStruct((slots, groups * PAIR), BF),
            jax.ShapeDtypeStruct((slots, width), BF),
        ],
        grid_spec=grid_spec,
        compiler_params=pltpu.CompilerParams(vmem_limit_bytes=50 * 1024 * 1024),
        cost_estimate=pl.CostEstimate(
            flops=tiles * 2 * BLK * BLK * PAIR,
            bytes_accessed=qkv.size,
            transcendentals=0,
        ),
        name="attention",
    )(block_place, slot_block, low, qkv, cotangent, cosine, sine, first_place)


def pick_rows(found, order, rows):
    arrays, places = [], []
    for key in order:
        array, start = found[key]
        held = [i for i, known in enumerate(arrays) if known is array]
        if not held:
            arrays.append(array)
            held = [len(arrays) - 1]
        places.append((held[0], start // rows))
    return arrays, places


def visit_blocks(body, found, order, rows, extra, outs, name):
    arrays, places = pick_rows(found, order, rows)
    width = arrays[0].shape[1]

    def kernel(*refs):
        step = pl.program_id(0)
        given = refs[len(arrays) : len(arrays) + len(extra)]
        for number, (which, block) in enumerate(places):

            @pl.when(step == number)
            def _(ref=refs[which], block=block):
                results = body(ref[block * rows : (block + 1) * rows, :], *[g[...] for g in given])
                for out, value in zip(refs[-outs:], results):
                    out[...] = value

    once = pl.Buffered(1)
    held = arrays + list(extra)
    size = len(order) * rows * width
    return pl.pallas_call(
        kernel,
        grid=(len(order),),
        in_specs=[pl.BlockSpec(a.shape, lambda i: (0, 0), pipeline_mode=once) for a in held],
        out_specs=[pl.BlockSpec((rows, width), lambda i: (i, 0))] * outs,
        out_shape=[jax.ShapeDtypeStruct((len(order) * rows, width), BF)] * outs,
        compiler_params=pltpu.CompilerParams(vmem_limit_bytes=40 * 1024 * 1024),
        cost_estimate=pl.CostEstimate(flops=size * 10, bytes_accessed=4 * size, transcendentals=0),
        name=name,
    )(*held)


def norm_blocks(found, order, rows, gain, shift):
    def body(x, gain, shift):
        x, _ = standardise(x.astype(F32))
        return (x * gain + shift).astype(BF), x.astype(BF)

    return visit_blocks(body, found, order, rows, [gain[None, :], shift[None, :]], 2, "norm_rows")


def join_blocks(found, order, rows):
    return visit_blocks(lambda x: (x,), found, order, rows, [], 1, "join_rows")[0]


def deal_columns(matrices, chunks):
    rows = matrices[0].shape[0]
    width = sum(stop - start for parts in chunks for start, stop in parts[0])
    size = rows * width * len(chunks[0])

    def kernel(*refs):
        values = [ref[...].astype(F32) for ref in refs[:-1]]
        for target in range(len(chunks[0])):
            part = [
                x[:, start:stop] for x, parts in zip(values, chunks) for start, stop in parts[target]
            ]
            refs[-1][target] = jnp.concatenate(part, axis=1).astype(BF)

    return pl.pallas_call(
        kernel,
        out_shape=jax.ShapeDtypeStruct((len(chunks[0]), rows, width), BF),
        cost_estimate=pl.CostEstimate(flops=size, bytes_accessed=4 * size, transcendentals=0),
        name="deal_columns",
    )(*matrices)


def collect_columns(blocks, chunks):
    order = []
    for source, parts in enumerate(chunks):
        place = 0
        for start, stop in parts:
            order.append((start, source, place, place + stop - start))
            place += stop - start
    order.sort()
    width = blocks.shape[0] * blocks.shape[2]

    def kernel(x_ref, o_ref):
        x = [x_ref[source].astype(F32) for source in range(len(chunks))]
        o_ref[...] = jnp.concatenate([x[i][:, low:high] for _, i, low, high in order], axis=1)

    return pl.pallas_call(
        kernel,
        out_shape=jax.ShapeDtypeStruct((blocks.shape[1], width), F32),
        cost_estimate=pl.CostEstimate(
            flops=blocks.size, bytes_accessed=6 * blocks.size, transcendentals=0
        ),
        name="collect_columns",
    )(blocks)


def exchange(value, axis, size, offset):
    return lax.ppermute(value, axis, [(i, i ^ offset) for i in range(size)])


def after(value, *others):
    return lax.optimization_barrier((value,) + others)[0]


def half_blocks(size):
    if size == 4:
        return [(0, 0), (0, 1), (1, 0), (2, 1), (2, 0), (3, 0), (1, 1), (3, 1)]
    return [(j, half) for j in range(size) for half in range(2)]


def split_halves(value, j, found):
    half = value.shape[0] // 2
    found[j, 0], found[j, 1] = (value, 0), (value, half)


def gather_two(first, second, size, wait):
    send = functools.partial(exchange, axis="ctx", size=size)
    half = first.shape[0] // 2
    left, right = {}, {}
    split_halves(first, 0, left)
    split_halves(second, 0, right)
    if size != 4:
        for j in range(1, size):
            split_halves(send(first, offset=j), j, left)
        for j in range(1, size):
            split_halves(send(second, offset=j), j, right)
        return left, right
    one, two = send(first, offset=1), send(first, offset=2)
    split_halves(one, 1, left)
    split_halves(two, 2, left)
    one, two, second = lax.optimization_barrier((one, two, second) + wait)[:3]
    near = send(jnp.concatenate([two[half:], second], axis=0), offset=1)
    far = send(jnp.concatenate([one[:half], second], axis=0), offset=2)
    left[3, 0], left[3, 1] = (far, 0), (near, 0)
    right[1, 0], right[1, 1] = (near, half), (near, 2 * half)
    right[2, 0], right[2, 1] = (far, half), (far, 2 * half)
    right[3, 0] = (send(near[half : 2 * half], offset=2), 0)
    right[3, 1] = (send(far[2 * half :], offset=1), 0)
    return left, right


def sum_ranges(size):
    if size == 4:
        return (0, 4), [(4, 6), (6, 8)]
    return (0, 2), [(2 * j, 2 * j + 2) for j in range(1, size)]


def sum_send(pieces, size):
    distances = (2, 1) if size == 4 else range(1, size)
    return tuple(exchange(x.astype(BF), "ctx", size, j) for x, j in zip(pieces, distances))


def sum_end(own, arrived, size):
    if size != 4:
        return sum([x.astype(F32) for x in arrived], own), arrived
    half = own.shape[0] // 4
    far, near = arrived
    top = (own[2 * half : 3 * half] + far[half:].astype(F32)).astype(BF)
    low = (own[3 * half :] + near[half:].astype(F32)).astype(BF)
    last = (exchange(top, "ctx", size, 1), exchange(low, "ctx", size, 2))
    top = own[:half] + far[:half].astype(F32) + last[0].astype(F32)
    low = own[half : 2 * half] + near[:half].astype(F32) + last[1].astype(F32)
    return jnp.concatenate([top, low], axis=0), last


def gather_small(value, devices):
    copies = jnp.broadcast_to(value, (devices,) + value.shape)
    return lax.all_to_all(copies, ALL, split_axis=0, concat_axis=0, tiled=True)


def gather_dp(value):
    return lax.all_gather(value, "dp", axis=0, tiled=True)


def scatter_dp(value):
    return lax.psum_scatter(value, "dp", scatter_dimension=0, tiled=True)


def swap_ctx(value):
    return lax.all_to_all(value, "ctx", split_axis=0, concat_axis=0, tiled=True)


def matmul(a, b):
    return jnp.dot(a, b, preferred_element_type=F32)


def matmul_t(a, b):
    return lax.dot_general(a, b, (((1,), (1,)), ((), ())), preferred_element_type=F32)


def outer(a, b):
    return lax.dot_general(a, b, (((0,), (0,)), ((), ())), preferred_element_type=F32)


CONTRACT = {"nn": ((1,), (0,)), "nt": ((1,), (1,)), "tn": ((0,), (0,))}


def tile_of(size):
    return next(t for t in (1024, 768, 512, 384, 256, 128, size) if size % t == 0)


def product(kind, pairs, outs=(BF,), finish=None, extras=(), row_range=None):
    a, b = pairs[0]
    rows = a.shape[1] if kind == "tn" else a.shape[0]
    columns = b.shape[0] if kind == "nt" else b.shape[1]
    low, high = row_range or (0, rows)
    tall, wide = tile_of(high - low), tile_of(columns)
    skip = low // tall
    in_specs, operands = [], []
    for a, b in pairs:
        if kind == "tn":
            in_specs.append(pl.BlockSpec((a.shape[0], tall), lambda j, i: (0, i + skip)))
        else:
            in_specs.append(pl.BlockSpec((tall, a.shape[1]), lambda j, i: (i + skip, 0)))
        if kind == "nt":
            in_specs.append(pl.BlockSpec((wide, b.shape[1]), lambda j, i: (j, 0)))
        else:
            in_specs.append(pl.BlockSpec((b.shape[0], wide), lambda j, i: (0, j)))
        operands += [a, b]
    for extra in extras:
        if extra.shape[0] == 1:
            in_specs.append(pl.BlockSpec((1, wide), lambda j, i: (0, j)))
        else:
            in_specs.append(pl.BlockSpec((tall, wide), lambda j, i: (i + skip, j)))
        operands.append(extra)
    count, chunk = len(pairs), min(256, wide)
    depth = sum(a.shape[0] if kind == "tn" else a.shape[1] for a, _ in pairs)

    def kernel(*refs):
        for start in range(0, wide, chunk):
            part = slice(start, start + chunk)
            total = None
            for p in range(count):
                right = refs[2 * p + 1]
                right = right[part, :] if kind == "nt" else right[:, part]
                term = lax.dot_general(
                    refs[2 * p][...], right, (CONTRACT[kind], ((), ())), preferred_element_type=F32
                )
                total = term if total is None else total + term
            more = [refs[2 * count + n][:, part] for n in range(len(extras))]
            results = finish(total, *more) if finish else (total,)
            for ref, value in zip(refs[-len(outs) :], results):
                ref[:, part] = value.astype(ref.dtype)

    shape = (high - low, columns)
    result = pl.pallas_call(
        kernel,
        grid=(columns // wide, (high - low) // tall),
        in_specs=in_specs,
        out_specs=[pl.BlockSpec((tall, wide), lambda j, i: (i, j))] * len(outs),
        out_shape=[jax.ShapeDtypeStruct(shape, dtype) for dtype in outs],
        compiler_params=pltpu.CompilerParams(vmem_limit_bytes=56 * 1024 * 1024),
        cost_estimate=pl.CostEstimate(
            flops=int(2 * FRACTION * shape[0] * shape[1] * depth),
            bytes_accessed=shape[0] * shape[1],
            transcendentals=0,
        ),
        name="product_" + kind,
    )(*operands)
    return result if len(outs) > 1 else result[0]


def standardise(hidden):
    average = jnp.mean(hidden, axis=-1, keepdims=True)
    centred = hidden - average
    variance = jnp.mean(centred * centred, axis=-1, keepdims=True)
    scale = lax.rsqrt(variance + EPS)
    return centred * scale, scale


def gelu_pair(x):
    root, cubic = math.sqrt(2.0 / math.pi), 0.044715
    square = x * x
    gate = 0.5 + 0.5 * jnp.tanh(x * (root + (root * cubic) * square))
    value = x * gate
    slope = gate + value * (1.0 - gate) * (2.0 * root + (6.0 * root * cubic) * square)
    return value, slope


def on_device(
    hidden_in,
    ln_gain,
    ln_bias,
    w_qkv,
    b_qkv,
    w_out,
    b_out,
    w_up,
    b_up,
    w_down,
    b_down,
    segment_ids,
    positions,
    token_order,
    grad_out,
):
    N, C = lax.axis_size("dp"), lax.axis_size("ctx")
    c = lax.axis_index("ctx")
    rows, own_slots, width = hidden_in.shape
    assert rows == 1
    heads = width // HEAD
    own_heads = heads // C
    groups = own_heads // 2
    ff_block = w_down.shape[0]
    row_block = w_qkv.shape[0]
    own_ff = N * ff_block
    hidden_own = hidden_in.reshape(own_slots, width)
    grad_own = grad_out.reshape(own_slots, width)


    sizes = [ln_gain.shape[0], ln_bias.shape[0], b_qkv.shape[0], b_out.shape[0]]
    sizes += [b_up.shape[0], b_down.shape[0]]
    cuts = [sum(sizes[:i]) for i in range(1, len(sizes))]
    small = jnp.concatenate([ln_gain, ln_bias, b_qkv, b_out, b_up, b_down])
    small = gather_small(small, N * C)
    hidden_parts, grad_parts = gather_two(hidden_own, grad_own, C, (small,))
    pieces = jnp.split(small, cuts, axis=1)
    gain, shift, qkv_bias, out_bias, up_bias, down_bias = [p.reshape(-1).astype(F32) for p in pieces]
    qkv_chunks = [
        [
            (part * width + (i * C + t) * HEAD, part * width + (i * C + t + 1) * HEAD)
            for pair in range(groups)
            for part in range(3)
            for i in (2 * pair, 2 * pair + 1)
        ]
        for t in range(C)
    ]
    up_chunks = [
        [((i * C + t) * ff_block, (i * C + t + 1) * ff_block) for i in range(N)] for t in range(C)
    ]
    aligned = row_block == HEAD
    if aligned:
        w_out_own = gather_dp(w_out)
    else:
        everything = lax.all_gather(w_out, ALL, axis=0, tiled=True)
        everything = everything.reshape(own_heads, C, HEAD, width)
        w_out_own = lax.dynamic_index_in_dim(everything, c, 1, keepdims=False)
        w_out_own = w_out_own.reshape(own_heads * HEAD, width)
    up_rows = swap_ctx(deal_columns((w_up,), (up_chunks,))).reshape(C * row_block, -1)
    qkv_send = deal_columns((w_qkv,), (qkv_chunks,))
    w_up_own = gather_dp(up_rows)

    half_block = jnp.array([j for j, _ in half_blocks(C)], jnp.int32) ^ c
    half_block = 2 * half_block + jnp.array([half for _, half in half_blocks(C)], jnp.int32)
    row_order, row_ids = token_order.reshape(-1), segment_ids.reshape(-1)
    slots = row_order.shape[0]
    first = jnp.zeros_like(row_order)
    for document in range(DOCS):
        inside = row_ids == document
        first = jnp.where(inside, jnp.min(jnp.where(inside, row_order, slots)), first)
    order_all, first_all = [
        jnp.take(x.reshape(2 * C, -1), half_block, axis=0).reshape(-1) for x in (row_order, first)
    ]
    position_all = order_all - first_all
    block_place = order_all[::BLK] // BLK
    slot_block = jnp.argsort(block_place).astype(jnp.int32)
    first_place = jnp.take(first_all.reshape(-1, BLK), slot_block, axis=0)
    half = ROT // 2
    lane = jnp.arange(PAIR, dtype=jnp.int32) % HEAD
    frequency = 10000.0 ** (-(lane % half).astype(F32) * 2.0 / ROT)
    frequency = jnp.where(lane < ROT, frequency, 0.0)
    angles = position_all.astype(F32)[:, None] * frequency
    cosine, sine = jnp.cos(angles), jnp.sin(angles) * jnp.where(lane < half, -1.0, 1.0)

    own_bias = lax.dynamic_index_in_dim(qkv_bias.reshape(3, groups, 2, C, HEAD), c, 3, keepdims=False)
    own_bias = own_bias.transpose(1, 0, 2, 3).reshape(-1)
    gain, cosine, sine, first_place, block_place, slot_block, own_bias = lax.optimization_barrier(
        (gain, cosine, sine, first_place, block_place, slot_block, own_bias)
    )
    step = own_slots // 2
    normed, xhat_all = norm_blocks(hidden_parts, half_blocks(C), step, gain, shift)
    qkv_rows = swap_ctx(after(qkv_send, normed)).reshape(C * row_block, -1)
    w_qkv_own = gather_dp(qkv_rows)
    w_down_own = gather_dp(after(w_down, up_rows))
    own_up_bias = lax.dynamic_index_in_dim(up_bias.reshape(N, C, ff_block), c, 1, keepdims=False)
    up = matmul(after(normed, w_out_own), w_up_own) + own_up_bias.reshape(-1)
    value, slope = gelu_pair(up)
    active, slope = lax.optimization_barrier((value.astype(BF), slope))
    if C == 4:
        for key in ((3, 0), (3, 1)):
            grad_parts[key] = (after(grad_parts[key][0], active), grad_parts[key][1])
    grad_all = join_blocks(grad_parts, half_blocks(C), step)
    down_part = outer(active, grad_all).astype(BF)
    down_grad = scatter_dp(down_part).astype(F32)

    d_attended = matmul_t(after(grad_all, down_part), w_out_own).astype(BF)

    def column_grad(part, chunks):
        own = scatter_dp(part)
        return own, collect_columns(swap_ctx(own.reshape(C, row_block, -1)), chunks)

    d_up = (matmul_t(after(grad_all, d_attended), w_down_own) * slope).astype(BF)
    up_part = outer(normed, d_up).astype(BF)
    up_rows_grad, up_grad = column_grad(up_part, up_chunks)

    qkv = matmul(after(normed, up_part), w_qkv_own) + own_bias
    attended, d_qkv = attention(
        qkv, d_attended, cosine, sine, first_place, block_place, slot_block
    )

    near_range, away_ranges = sum_ranges(C)

    def out_rows(half_range, dtype, attended):
        pairs = [(active, w_down_own), (attended, w_out_own)]
        return product("nn", pairs, (dtype,), row_range=[i * step for i in half_range])

    out_away = [out_rows(r, BF, attended) for r in away_ranges]
    out_arrived = sum_send(out_away, C)
    out_part = outer(after(attended, *out_away), grad_all)
    if aligned:
        out_part = out_part.astype(BF)
        out_grad = scatter_dp(out_part).astype(F32)
    else:
        spread = jnp.zeros((own_heads, C, HEAD, width), F32)
        spread = lax.dynamic_update_index_in_dim(
            spread, out_part.reshape(own_heads, HEAD, width), c, 1
        )
        out_grad = lax.psum_scatter(
            spread.reshape(heads * HEAD, width), ALL, scatter_dimension=0, tiled=True
        )

    qkv_part = outer(after(normed, down_grad, out_part), d_qkv).astype(BF)
    _, qkv_grad = column_grad(qkv_part, qkv_chunks)
    out_near = out_rows(near_range, F32, after(attended, qkv_part))

    def normed_rows(half_range, dtype, d_qkv):
        pairs = [(d_qkv, w_qkv_own), (d_up, w_up_own)]
        return product("nt", pairs, (dtype,), row_range=[i * step for i in half_range])

    d_away = [normed_rows(r, BF, after(d_qkv, out_near)) for r in away_ranges]
    d_arrived = sum_send(d_away, C)
    out_sum, out_last = sum_end(after(out_near, *d_away), out_arrived, C)
    output = hidden_own.astype(F32) + out_sum + (out_bias + down_bias)
    output = output.astype(BF).reshape(hidden_in.shape)
    d_near = normed_rows(near_range, F32, after(d_qkv, up_rows_grad, *d_away, *out_arrived))

    devices = N * C
    gain_grad = shift_grad = 0.0
    for r, piece in zip([near_range] + away_ranges, [d_near] + d_away):
        piece = piece.astype(F32)
        gain_grad += jnp.sum(piece * xhat_all[r[0] * step : r[1] * step].astype(F32), axis=0)
        shift_grad += jnp.sum(piece, axis=0)
    bias_grad = jnp.sum(grad_own.astype(F32), axis=0)
    up_bias_grad = jnp.sum(d_up.astype(F32), axis=0).reshape(N, 1, ff_block)
    qkv_bias_grad = jnp.sum(d_qkv.astype(F32), axis=0).reshape(groups, 3, 2, HEAD)
    qkv_bias_grad = qkv_bias_grad.transpose(1, 0, 2, 3)[:, :, :, None, :]
    mine = jnp.arange(C) == c
    up_bias_grad = jnp.where(mine[None, :, None], up_bias_grad, 0.0)
    qkv_bias_grad = jnp.where(mine[None, None, None, :, None], qkv_bias_grad, 0.0)
    small = [gain_grad, shift_grad, qkv_bias_grad, bias_grad, up_bias_grad]
    small = jnp.concatenate([s.reshape(devices, -1) for s in small], axis=1)
    small = lax.all_to_all(small, ALL, split_axis=0, concat_axis=0, tiled=True)
    small = jnp.split(jnp.sum(small, axis=0), cuts[:4])

    d_normed, _ = sum_end(d_near, d_arrived, C)
    d_normed = after(d_normed, up_grad, *small)
    xhat, scale = standardise(hidden_own.astype(F32))
    e = d_normed * gain
    d_hidden = e - jnp.mean(e, axis=-1, keepdims=True)
    d_hidden = (d_hidden - xhat * jnp.mean(e * xhat, axis=-1, keepdims=True)) * scale
    grad_in = (grad_own.astype(F32) + d_hidden).astype(BF).reshape(hidden_in.shape)

    return (
        output,
        grad_in,
        small[0],
        small[1],
        qkv_grad,
        small[2],
        out_grad,
        small[3],
        up_grad,
        small[4],
        down_grad,
        small[3],
    )


def solution(mesh):
    both = P(("dp", "ctx"))
    matrix = P(("dp", "ctx"), None)
    slots = P("dp", "ctx", None)
    in_specs = (
        slots,
        both,
        both,
        matrix,
        both,
        matrix,
        both,
        matrix,
        both,
        matrix,
        both,
        P("dp", None),
        P("dp", "ctx"),
        P("dp", None),
        slots,
    )
    out_specs = (
        slots,
        slots,
        both,
        both,
        matrix,
        both,
        matrix,
        both,
        matrix,
        both,
        matrix,
        both,
    )
    return jax.shard_map(
        on_device, mesh=mesh, in_specs=in_specs, out_specs=out_specs, check_vma=False
    )
```

```python
import functools
import math

import jax
import jax.numpy as jnp
from jax import lax
from jax.experimental import pallas as pl
from jax.experimental.pallas import tpu as pltpu
from jax.sharding import PartitionSpec as P

HEAD = 64
ROT = 32
BLK = 128
DOCS = 4
EPS = 1e-05
NEG = -1e30
PAIR = 2 * HEAD
KEYS = 256
LONGEST = 1024
PAIRS = 2
LOOSE = 2
FRACTION = 5.0
SCALE = HEAD**-0.5
ALL = ("dp", "ctx")
BF = jnp.bfloat16
F32 = jnp.float32


def partner(x):
    lane = lax.broadcasted_iota(jnp.int32, x.shape, 1) % HEAD
    return jnp.where(
        lane < ROT // 2, pltpu.roll(x, PAIR - ROT // 2, 1), pltpu.roll(x, ROT // 2, 1)
    )


def dot(a, b):
    return jnp.dot(a, b, preferred_element_type=F32)


def dot_t(a, b):
    return lax.dot_general(a, b, (((1,), (1,)), ((), ())), preferred_element_type=F32)


def aligned_rows(index, size):
    return pl.ds(pl.multiple_of(index * size, size), size)


def attention_kernel(
    place_ref,
    slot_ref,
    low_ref,
    qkv_ref,
    cot_ref,
    cos_ref,
    sin_ref,
    first_ref,
    att_ref,
    grad_ref,
    q_st,
    do_st,
    k_s,
    v_s,
    k_t,
    v_t,
    dk_s,
    dv_s,
    p_s,
    dp_s,
):
    slots = qkv_ref.shape[0]
    blocks = slots // BLK
    pairs = k_s.shape[0]
    lane_first = lax.broadcasted_iota(jnp.int32, (BLK, PAIR), 1) < HEAD
    row_first = lax.broadcasted_iota(jnp.int32, (PAIR, BLK), 0) < HEAD

    def stack(value):
        zero = jnp.zeros_like(value)
        both = [jnp.where(lane_first, value, zero), jnp.where(lane_first, zero, value)]
        return jnp.concatenate(both, axis=0).astype(BF)

    def columns(pair, which, count=3):
        start = (pair * count + which) * PAIR
        return slice(start, start + PAIR)

    def load_block(b, carry):
        rows = aligned_rows(b, BLK)
        place = place_ref[b]
        out_rows = aligned_rows(place, BLK)
        cosine = cos_ref[rows, :]
        sine = sin_ref[rows, :]
        for pair in range(pairs):
            q = qkv_ref[rows, columns(pair, 0)]
            k = qkv_ref[rows, columns(pair, 1)]
            v = qkv_ref[rows, columns(pair, 2)]
            q = (q * cosine + partner(q) * sine).astype(BF).astype(F32) * SCALE
            k = k * cosine + partner(k) * sine
            q_st[pair, aligned_rows(place, 2 * BLK), :] = stack(q)
            do = cot_ref[rows, columns(pair, 0, 1)].astype(F32)
            do_st[pair, aligned_rows(place, 2 * BLK), :] = stack(do)
            k_s[pair, out_rows, :] = k.astype(BF)
            v_s[pair, out_rows, :] = v.astype(BF)
            k_t[pair, out_rows, :] = k.T.astype(BF)
            v_t[pair, out_rows, :] = v.T.astype(BF)
        return carry

    lax.fori_loop(0, blocks, load_block, 0, unroll=LOOSE)
    dk_s[...] = jnp.zeros_like(dk_s)
    dv_s[...] = jnp.zeros_like(dv_s)

    def tiles_of(i, low, count):
        stacked = aligned_rows(i, 2 * BLK)
        first = first_ref[pl.ds(i, 1), :]
        row = lax.broadcasted_iota(jnp.int32, (KEYS, BLK), 0)
        own = i * BLK + lax.broadcasted_iota(jnp.int32, (1, BLK), 1)
        every = range(pairs)
        top = [None] * pairs
        for t in range(count):
            keys = aligned_rows(low + t, KEYS)
            part = slice(t * KEYS, (t + 1) * KEYS)
            place = (low + t) * KEYS
            allowed = row >= first - place
            if t == count - 1:
                allowed = allowed & (row <= own - place)
            allowed = jnp.concatenate([allowed, allowed], axis=1)
            for pair in every:
                s = dot_t(k_s[pair, keys, :], q_st[pair, stacked, :])
                s = jnp.where(allowed, s, NEG)
                p_s[pair, part, :] = s
                dp_s[pair, part, :] = dot_t(v_s[pair, keys, :], do_st[pair, stacked, :])
                here = jnp.max(s, axis=0, keepdims=True)
                top[pair] = here if t == 0 else jnp.maximum(top[pair], here)
        total = [0.0] * pairs
        inner = [0.0] * pairs
        for t in range(count):
            part = slice(t * KEYS, (t + 1) * KEYS)
            for pair in every:
                p = jnp.exp(p_s[pair, part, :] - top[pair])
                p_s[pair, part, :] = p
                total[pair] += jnp.sum(p, axis=0, keepdims=True)
                inner[pair] += jnp.sum(p * dp_s[pair, part, :], axis=0, keepdims=True)
        inverse = [1.0 / x for x in total]
        inner = [x * y for x, y in zip(inner, inverse)]
        out = [0.0] * pairs
        dq = [0.0] * pairs
        for t in range(count):
            part = slice(t * KEYS, (t + 1) * KEYS)
            keys = aligned_rows(low + t, KEYS)
            for pair in every:
                p = p_s[pair, part, :] * inverse[pair]
                ds = (p * (dp_s[pair, part, :] - inner[pair])).astype(BF)
                p = p.astype(BF)
                v_turned = v_t[pair, keys, :]
                k_turned = k_t[pair, keys, :]
                v_turned = jnp.concatenate([v_turned[:BLK], v_turned[BLK:]], axis=1)
                k_turned = jnp.concatenate([k_turned[:BLK], k_turned[BLK:]], axis=1)
                out[pair] += dot(v_turned, p)
                dq[pair] += dot(k_turned, ds)
                dv_s[pair, keys, :] += dot(p, do_st[pair, stacked, :])
                dk_s[pair, keys, :] += dot(ds, q_st[pair, stacked, :])
        slot_rows = aligned_rows(slot_ref[i], BLK)
        for pair in every:
            x = jnp.where(row_first, out[pair][:, :BLK], out[pair][:, BLK:]).T
            att_ref[slot_rows, columns(pair, 0, 1)] = x.astype(BF)
            x = (jnp.where(row_first, dq[pair][:, :BLK], dq[pair][:, BLK:]) * SCALE).T
            x = x * cos_ref[slot_rows, :] - partner(x) * sin_ref[slot_rows, :]
            grad_ref[slot_rows, columns(pair, 0)] = x.astype(BF)

    most = p_s.shape[1] // KEYS

    def query_block(i, carry):
        low = low_ref[i]
        count = (i * BLK) // KEYS + 1 - low
        for n in range(1, most + 1):
            pl.when(count == n)(functools.partial(tiles_of, i, low, n))
        return carry

    lax.fori_loop(0, blocks, query_block, 0)

    def store_block(b, carry):
        rows = aligned_rows(b, BLK)
        in_rows = aligned_rows(place_ref[b], BLK)
        for pair in range(pairs):
            dk = dk_s[pair, in_rows, :]
            dk = dk * cos_ref[rows, :] - partner(dk) * sin_ref[rows, :]
            grad_ref[rows, columns(pair, 1)] = dk.astype(BF)
            grad_ref[rows, columns(pair, 2)] = dv_s[pair, in_rows, :].astype(BF)
        return carry

    lax.fori_loop(0, blocks, store_block, 0, unroll=LOOSE)


def attention(qkv, cotangent, cosine, sine, first_place, block_place, slot_block):
    slots, width = qkv.shape
    groups = width // (3 * PAIR)
    pairs = math.gcd(groups, PAIRS)
    wide = pairs * PAIR
    blocks = slots // BLK
    low = first_place[:, 0] // KEYS
    once = pl.Buffered(1)
    most = min(LONGEST // KEYS + 1, slots // KEYS)
    grid_spec = pltpu.PrefetchScalarGridSpec(
        num_scalar_prefetch=3,
        grid=(groups // pairs,),
        in_specs=[
            pl.BlockSpec((slots, 3 * wide), lambda g, *_: (0, g)),
            pl.BlockSpec((slots, wide), lambda g, *_: (0, g)),
            pl.BlockSpec((slots, PAIR), lambda g, *_: (0, 0), pipeline_mode=once),
            pl.BlockSpec((slots, PAIR), lambda g, *_: (0, 0), pipeline_mode=once),
            pl.BlockSpec((blocks, BLK), lambda g, *_: (0, 0), pipeline_mode=once),
        ],
        out_specs=[
            pl.BlockSpec((slots, wide), lambda g, *_: (0, g)),
            pl.BlockSpec((slots, 3 * wide), lambda g, *_: (0, g)),
        ],
        scratch_shapes=[
            pltpu.VMEM((pairs, 2 * slots, PAIR), BF),
            pltpu.VMEM((pairs, 2 * slots, PAIR), BF),
            pltpu.VMEM((pairs, slots, PAIR), BF),
            pltpu.VMEM((pairs, slots, PAIR), BF),
            pltpu.VMEM((pairs, slots, PAIR), BF),
            pltpu.VMEM((pairs, slots, PAIR), BF),
            pltpu.VMEM((pairs, slots, PAIR), F32),
            pltpu.VMEM((pairs, slots, PAIR), F32),
            pltpu.VMEM((pairs, most * KEYS, 2 * BLK), F32),
            pltpu.VMEM((pairs, most * KEYS, 2 * BLK), F32),
        ],
    )
    tiles = groups * blocks * (blocks // 4)
    return pl.pallas_call(
        attention_kernel,
        out_shape=[
            jax.ShapeDtypeStruct((slots, groups * PAIR), BF),
            jax.ShapeDtypeStruct((slots, width), BF),
        ],
        grid_spec=grid_spec,
        compiler_params=pltpu.CompilerParams(vmem_limit_bytes=50 * 1024 * 1024),
        cost_estimate=pl.CostEstimate(
            flops=tiles * 2 * BLK * BLK * PAIR,
            bytes_accessed=qkv.size,
            transcendentals=0,
        ),
        name="attention",
    )(block_place, slot_block, low, qkv, cotangent, cosine, sine, first_place)


def pick_rows(found, order, rows):
    arrays, places = [], []
    for key in order:
        array, start = found[key]
        held = [i for i, known in enumerate(arrays) if known is array]
        if not held:
            arrays.append(array)
            held = [len(arrays) - 1]
        places.append((held[0], start // rows))
    return arrays, places


def visit_blocks(body, found, order, rows, extra, outs, name):
    arrays, places = pick_rows(found, order, rows)
    width = arrays[0].shape[1]

    def kernel(*refs):
        step = pl.program_id(0)
        given = refs[len(arrays) : len(arrays) + len(extra)]
        for number, (which, block) in enumerate(places):

            @pl.when(step == number)
            def _(ref=refs[which], block=block):
                results = body(ref[block * rows : (block + 1) * rows, :], *[g[...] for g in given])
                for out, value in zip(refs[-outs:], results):
                    out[...] = value

    once = pl.Buffered(1)
    held = arrays + list(extra)
    size = len(order) * rows * width
    return pl.pallas_call(
        kernel,
        grid=(len(order),),
        in_specs=[pl.BlockSpec(a.shape, lambda i: (0, 0), pipeline_mode=once) for a in held],
        out_specs=[pl.BlockSpec((rows, width), lambda i: (i, 0))] * outs,
        out_shape=[jax.ShapeDtypeStruct((len(order) * rows, width), BF)] * outs,
        compiler_params=pltpu.CompilerParams(vmem_limit_bytes=40 * 1024 * 1024),
        cost_estimate=pl.CostEstimate(flops=size * 10, bytes_accessed=4 * size, transcendentals=0),
        name=name,
    )(*held)


def norm_blocks(found, order, rows, gain, shift):
    def body(x, gain, shift):
        x, _ = standardise(x.astype(F32))
        return (x * gain + shift).astype(BF), x.astype(BF)

    return visit_blocks(body, found, order, rows, [gain[None, :], shift[None, :]], 2, "norm_rows")


def join_blocks(found, order, rows):
    return visit_blocks(lambda x: (x,), found, order, rows, [], 1, "join_rows")[0]


def deal_columns(matrices, chunks):
    rows = matrices[0].shape[0]
    width = sum(stop - start for parts in chunks for start, stop in parts[0])
    size = rows * width * len(chunks[0])

    def kernel(*refs):
        values = [ref[...].astype(F32) for ref in refs[:-1]]
        for target in range(len(chunks[0])):
            part = [
                x[:, start:stop] for x, parts in zip(values, chunks) for start, stop in parts[target]
            ]
            refs[-1][target] = jnp.concatenate(part, axis=1).astype(BF)

    return pl.pallas_call(
        kernel,
        out_shape=jax.ShapeDtypeStruct((len(chunks[0]), rows, width), BF),
        cost_estimate=pl.CostEstimate(flops=size, bytes_accessed=4 * size, transcendentals=0),
        name="deal_columns",
    )(*matrices)


def collect_columns(blocks, chunks):
    order = []
    for source, parts in enumerate(chunks):
        place = 0
        for start, stop in parts:
            order.append((start, source, place, place + stop - start))
            place += stop - start
    order.sort()
    width = blocks.shape[0] * blocks.shape[2]

    def kernel(x_ref, o_ref):
        x = [x_ref[source].astype(F32) for source in range(len(chunks))]
        o_ref[...] = jnp.concatenate([x[i][:, low:high] for _, i, low, high in order], axis=1)

    return pl.pallas_call(
        kernel,
        out_shape=jax.ShapeDtypeStruct((blocks.shape[1], width), F32),
        cost_estimate=pl.CostEstimate(
            flops=blocks.size, bytes_accessed=6 * blocks.size, transcendentals=0
        ),
        name="collect_columns",
    )(blocks)


def exchange(value, axis, size, offset):
    return lax.ppermute(value, axis, [(i, i ^ offset) for i in range(size)])


def after(value, *others):
    return lax.optimization_barrier((value,) + others)[0]


def half_blocks(size):
    if size == 4:
        return [(0, 0), (0, 1), (1, 0), (2, 1), (2, 0), (3, 0), (1, 1), (3, 1)]
    return [(j, half) for j in range(size) for half in range(2)]


def split_halves(value, j, found):
    half = value.shape[0] // 2
    found[j, 0], found[j, 1] = (value, 0), (value, half)


def gather_two(first, second, size, wait):
    send = functools.partial(exchange, axis="ctx", size=size)
    half = first.shape[0] // 2
    left, right = {}, {}
    split_halves(first, 0, left)
    split_halves(second, 0, right)
    if size != 4:
        for j in range(1, size):
            split_halves(send(first, offset=j), j, left)
        for j in range(1, size):
            split_halves(send(second, offset=j), j, right)
        return left, right
    one, two = send(first, offset=1), send(first, offset=2)
    split_halves(one, 1, left)
    split_halves(two, 2, left)
    one, two, second = lax.optimization_barrier((one, two, second) + wait)[:3]
    near = send(jnp.concatenate([two[half:], second], axis=0), offset=1)
    far = send(jnp.concatenate([one[:half], second], axis=0), offset=2)
    left[3, 0], left[3, 1] = (far, 0), (near, 0)
    right[1, 0], right[1, 1] = (near, half), (near, 2 * half)
    right[2, 0], right[2, 1] = (far, half), (far, 2 * half)
    right[3, 0] = (send(near[half : 2 * half], offset=2), 0)
    right[3, 1] = (send(far[2 * half :], offset=1), 0)
    return left, right


def sum_ranges(size):
    if size == 4:
        return (0, 4), [(4, 6), (6, 8)]
    return (0, 2), [(2 * j, 2 * j + 2) for j in range(1, size)]


def sum_send(pieces, size):
    distances = (2, 1) if size == 4 else range(1, size)
    return tuple(exchange(x.astype(BF), "ctx", size, j) for x, j in zip(pieces, distances))


def sum_end(own, arrived, size):
    if size != 4:
        return sum([x.astype(F32) for x in arrived], own), arrived, arrived
    half = own.shape[0] // 4
    far, near = arrived
    top = (own[2 * half : 3 * half] + far[half:].astype(F32)).astype(BF)
    low = (own[3 * half :] + near[half:].astype(F32)).astype(BF)
    sent = (top, low)
    last = (exchange(top, "ctx", size, 1), exchange(low, "ctx", size, 2))
    top = own[:half] + far[:half].astype(F32) + last[0].astype(F32)
    low = own[half : 2 * half] + near[:half].astype(F32) + last[1].astype(F32)
    return jnp.concatenate([top, low], axis=0), last, sent


def gather_small(value, devices):
    copies = jnp.broadcast_to(value, (devices,) + value.shape)
    return lax.all_to_all(copies, ALL, split_axis=0, concat_axis=0, tiled=True)


def gather_dp(value):
    return lax.all_gather(value, "dp", axis=0, tiled=True)


def scatter_dp(value):
    return lax.psum_scatter(value, "dp", scatter_dimension=0, tiled=True)


def swap_ctx(value):
    return lax.all_to_all(value, "ctx", split_axis=0, concat_axis=0, tiled=True)


def matmul(a, b):
    return jnp.dot(a, b, preferred_element_type=F32)


def matmul_t(a, b):
    return lax.dot_general(a, b, (((1,), (1,)), ((), ())), preferred_element_type=F32)


def outer(a, b):
    return lax.dot_general(a, b, (((0,), (0,)), ((), ())), preferred_element_type=F32)


CONTRACT = {"nn": ((1,), (0,)), "nt": ((1,), (1,)), "tn": ((0,), (0,))}


def tile_of(size):
    return next(t for t in (1024, 768, 512, 384, 256, 128, size) if size % t == 0)


def product(kind, pairs, outs=(BF,), finish=None, extras=(), row_range=None):
    a, b = pairs[0]
    rows = a.shape[1] if kind == "tn" else a.shape[0]
    columns = b.shape[0] if kind == "nt" else b.shape[1]
    low, high = row_range or (0, rows)
    tall, wide = tile_of(high - low), tile_of(columns)
    skip = low // tall
    in_specs, operands = [], []
    for a, b in pairs:
        if kind == "tn":
            in_specs.append(pl.BlockSpec((a.shape[0], tall), lambda j, i: (0, i + skip)))
        else:
            in_specs.append(pl.BlockSpec((tall, a.shape[1]), lambda j, i: (i + skip, 0)))
        if kind == "nt":
            in_specs.append(pl.BlockSpec((wide, b.shape[1]), lambda j, i: (j, 0)))
        else:
            in_specs.append(pl.BlockSpec((b.shape[0], wide), lambda j, i: (0, j)))
        operands += [a, b]
    for extra in extras:
        if extra.shape[0] == 1:
            in_specs.append(pl.BlockSpec((1, wide), lambda j, i: (0, j)))
        else:
            in_specs.append(pl.BlockSpec((tall, wide), lambda j, i: (i + skip, j)))
        operands.append(extra)
    count, chunk = len(pairs), min(256, wide)
    depth = sum(a.shape[0] if kind == "tn" else a.shape[1] for a, _ in pairs)

    def kernel(*refs):
        for start in range(0, wide, chunk):
            part = slice(start, start + chunk)
            total = None
            for p in range(count):
                right = refs[2 * p + 1]
                right = right[part, :] if kind == "nt" else right[:, part]
                term = lax.dot_general(
                    refs[2 * p][...], right, (CONTRACT[kind], ((), ())), preferred_element_type=F32
                )
                total = term if total is None else total + term
            more = [refs[2 * count + n][:, part] for n in range(len(extras))]
            results = finish(total, *more) if finish else (total,)
            for ref, value in zip(refs[-len(outs) :], results):
                ref[:, part] = value.astype(ref.dtype)

    shape = (high - low, columns)
    result = pl.pallas_call(
        kernel,
        grid=(columns // wide, (high - low) // tall),
        in_specs=in_specs,
        out_specs=[pl.BlockSpec((tall, wide), lambda j, i: (i, j))] * len(outs),
        out_shape=[jax.ShapeDtypeStruct(shape, dtype) for dtype in outs],
        compiler_params=pltpu.CompilerParams(vmem_limit_bytes=56 * 1024 * 1024),
        cost_estimate=pl.CostEstimate(
            flops=int(2 * FRACTION * shape[0] * shape[1] * depth),
            bytes_accessed=shape[0] * shape[1],
            transcendentals=0,
        ),
        name="product_" + kind,
    )(*operands)
    return result if len(outs) > 1 else result[0]


def standardise(hidden):
    average = jnp.mean(hidden, axis=-1, keepdims=True)
    centred = hidden - average
    variance = jnp.mean(centred * centred, axis=-1, keepdims=True)
    scale = lax.rsqrt(variance + EPS)
    return centred * scale, scale


def gelu_pair(x):
    root, cubic = math.sqrt(2.0 / math.pi), 0.044715
    square = x * x
    gate = 0.5 + 0.5 * jnp.tanh(x * (root + (root * cubic) * square))
    value = x * gate
    slope = gate + value * (1.0 - gate) * (2.0 * root + (6.0 * root * cubic) * square)
    return value, slope


def on_device(
    hidden_in,
    ln_gain,
    ln_bias,
    w_qkv,
    b_qkv,
    w_out,
    b_out,
    w_up,
    b_up,
    w_down,
    b_down,
    segment_ids,
    positions,
    token_order,
    grad_out,
):
    N, C = lax.axis_size("dp"), lax.axis_size("ctx")
    c = lax.axis_index("ctx")
    rows, own_slots, width = hidden_in.shape
    assert rows == 1
    heads = width // HEAD
    own_heads = heads // C
    groups = own_heads // 2
    ff_block = w_down.shape[0]
    row_block = w_qkv.shape[0]
    own_ff = N * ff_block
    hidden_own = hidden_in.reshape(own_slots, width)
    grad_own = grad_out.reshape(own_slots, width)


    sizes = [ln_gain.shape[0], ln_bias.shape[0], b_qkv.shape[0], b_out.shape[0]]
    sizes += [b_up.shape[0], b_down.shape[0]]
    cuts = [sum(sizes[:i]) for i in range(1, len(sizes))]
    small = jnp.concatenate([ln_gain, ln_bias, b_qkv, b_out, b_up, b_down])
    small = gather_small(small, N * C)
    hidden_parts, grad_parts = gather_two(hidden_own, grad_own, C, (small,))
    pieces = jnp.split(small, cuts, axis=1)
    gain, shift, qkv_bias, out_bias, up_bias, down_bias = [p.reshape(-1).astype(F32) for p in pieces]
    qkv_chunks = [
        [
            (part * width + (i * C + t) * HEAD, part * width + (i * C + t + 1) * HEAD)
            for pair in range(groups)
            for part in range(3)
            for i in (2 * pair, 2 * pair + 1)
        ]
        for t in range(C)
    ]
    up_chunks = [
        [((i * C + t) * ff_block, (i * C + t + 1) * ff_block) for i in range(N)] for t in range(C)
    ]
    aligned = row_block == HEAD
    if aligned:
        w_out_own = gather_dp(w_out)
    else:
        everything = lax.all_gather(w_out, ALL, axis=0, tiled=True)
        everything = everything.reshape(own_heads, C, HEAD, width)
        w_out_own = lax.dynamic_index_in_dim(everything, c, 1, keepdims=False)
        w_out_own = w_out_own.reshape(own_heads * HEAD, width)
    up_rows = swap_ctx(deal_columns((w_up,), (up_chunks,))).reshape(C * row_block, -1)
    qkv_send = deal_columns((w_qkv,), (qkv_chunks,))
    w_up_own = gather_dp(up_rows)

    half_block = jnp.array([j for j, _ in half_blocks(C)], jnp.int32) ^ c
    half_block = 2 * half_block + jnp.array([half for _, half in half_blocks(C)], jnp.int32)
    row_order, row_ids = token_order.reshape(-1), segment_ids.reshape(-1)
    slots = row_order.shape[0]
    first = jnp.zeros_like(row_order)
    for document in range(DOCS):
        inside = row_ids == document
        first = jnp.where(inside, jnp.min(jnp.where(inside, row_order, slots)), first)
    order_all, first_all = [
        jnp.take(x.reshape(2 * C, -1), half_block, axis=0).reshape(-1) for x in (row_order, first)
    ]
    position_all = order_all - first_all
    block_place = order_all[::BLK] // BLK
    slot_block = jnp.argsort(block_place).astype(jnp.int32)
    first_place = jnp.take(first_all.reshape(-1, BLK), slot_block, axis=0)
    half = ROT // 2
    lane = jnp.arange(PAIR, dtype=jnp.int32) % HEAD
    frequency = 10000.0 ** (-(lane % half).astype(F32) * 2.0 / ROT)
    frequency = jnp.where(lane < ROT, frequency, 0.0)
    angles = position_all.astype(F32)[:, None] * frequency
    cosine, sine = jnp.cos(angles), jnp.sin(angles) * jnp.where(lane < half, -1.0, 1.0)

    own_bias = lax.dynamic_index_in_dim(qkv_bias.reshape(3, groups, 2, C, HEAD), c, 3, keepdims=False)
    own_bias = own_bias.transpose(1, 0, 2, 3).reshape(-1)
    gain, cosine, sine, first_place, block_place, slot_block, own_bias = lax.optimization_barrier(
        (gain, cosine, sine, first_place, block_place, slot_block, own_bias)
    )
    step = own_slots // 2
    normed, xhat_all = norm_blocks(hidden_parts, half_blocks(C), step, gain, shift)
    w_down_own = gather_dp(after(w_down, up_rows))
    own_up_bias = lax.dynamic_index_in_dim(up_bias.reshape(N, C, ff_block), c, 1, keepdims=False)
    up = matmul(after(normed, w_out_own), w_up_own) + own_up_bias.reshape(-1)
    value, slope = gelu_pair(up)
    active, slope = lax.optimization_barrier((value.astype(BF), slope))
    if C == 4:
        for key in ((3, 0), (3, 1)):
            grad_parts[key] = (after(grad_parts[key][0], active), grad_parts[key][1])
    grad_all = join_blocks(grad_parts, half_blocks(C), step)
    qkv_rows = swap_ctx(after(qkv_send, grad_all)).reshape(C * row_block, -1)
    w_qkv_own = gather_dp(qkv_rows)
    d_attended = matmul_t(grad_all, w_out_own).astype(BF)

    def column_grad(part, chunks):
        own = scatter_dp(part)
        return own, collect_columns(swap_ctx(own.reshape(C, row_block, -1)), chunks)

    d_up = (matmul_t(after(grad_all, d_attended), w_down_own) * slope).astype(BF)
    up_part = outer(normed, d_up).astype(BF)
    up_rows_grad, up_grad = column_grad(up_part, up_chunks)

    down_part = outer(after(active, up_part), grad_all).astype(BF)
    down_rows = scatter_dp(down_part)


    qkv = matmul(after(normed, down_part), w_qkv_own) + own_bias
    attended, d_qkv = attention(
        qkv, d_attended, cosine, sine, first_place, block_place, slot_block
    )

    near_range, away_ranges = sum_ranges(C)

    def out_rows(half_range, dtype, attended):
        pairs = [(active, w_down_own), (attended, w_out_own)]
        return product("nn", pairs, (dtype,), row_range=[i * step for i in half_range])

    out_away = [out_rows(r, BF, attended) for r in away_ranges[:1]]
    attended_then = after(attended, up_grad, *out_away)
    out_away += [out_rows(r, BF, attended_then) for r in away_ranges[1:]]
    out_arrived = sum_send(out_away, C)
    out_part = outer(after(attended, *out_away), grad_all)
    if aligned:
        out_part = out_part.astype(BF)
        out_grad = scatter_dp(out_part)
    else:
        spread = jnp.zeros((own_heads, C, HEAD, width), F32)
        spread = lax.dynamic_update_index_in_dim(
            spread, out_part.reshape(own_heads, HEAD, width), c, 1
        )
        out_grad = lax.psum_scatter(
            spread.reshape(heads * HEAD, width), ALL, scatter_dimension=0, tiled=True
        )

    qkv_part = outer(after(normed, up_rows_grad, out_part), d_qkv).astype(BF)
    _, qkv_grad = column_grad(qkv_part, qkv_chunks)
    out_near = out_rows(near_range, F32, after(attended, qkv_part))

    def normed_rows(half_range, dtype, d_qkv):
        pairs = [(d_qkv, w_qkv_own), (d_up, w_up_own)]
        return product("nt", pairs, (dtype,), row_range=[i * step for i in half_range])

    d_away = [normed_rows(r, BF, after(d_qkv, out_near)) for r in away_ranges]
    d_arrived = sum_send(d_away, C)
    d_near = normed_rows(near_range, F32, after(d_qkv, *d_away, *out_arrived))
    out_sum, _, _ = sum_end(after(out_near, d_near), out_arrived, C)
    output = hidden_own.astype(F32) + out_sum + (out_bias + down_bias)
    output = output.astype(BF).reshape(hidden_in.shape)

    down_grad = after(down_rows, d_near).astype(F32)
    out_grad = after(out_grad, d_near).astype(F32)

    devices = N * C
    gain_grad = shift_grad = 0.0
    for r, piece in zip([near_range] + away_ranges, [d_near] + d_away):
        piece = piece.astype(F32)
        gain_grad += jnp.sum(piece * xhat_all[r[0] * step : r[1] * step].astype(F32), axis=0)
        shift_grad += jnp.sum(piece, axis=0)
    bias_grad = jnp.sum(grad_own.astype(F32), axis=0)
    up_bias_grad = jnp.sum(d_up.astype(F32), axis=0).reshape(N, 1, ff_block)
    qkv_bias_grad = jnp.sum(d_qkv.astype(F32), axis=0).reshape(groups, 3, 2, HEAD)
    qkv_bias_grad = qkv_bias_grad.transpose(1, 0, 2, 3)[:, :, :, None, :]
    mine = jnp.arange(C) == c
    up_bias_grad = jnp.where(mine[None, :, None], up_bias_grad, 0.0)
    qkv_bias_grad = jnp.where(mine[None, None, None, :, None], qkv_bias_grad, 0.0)
    small = [gain_grad, shift_grad, qkv_bias_grad, bias_grad, up_bias_grad]
    small = jnp.concatenate([s.reshape(devices, -1) for s in small], axis=1)
    d_normed, _, d_sent = sum_end(d_near, d_arrived, C)
    small = after(small, *d_sent)
    small = lax.all_to_all(small, ALL, split_axis=0, concat_axis=0, tiled=True)
    small = jnp.split(jnp.sum(small, axis=0), cuts[:4])

    d_normed = after(d_normed, down_rows, *small)
    xhat, scale = standardise(hidden_own.astype(F32))
    e = d_normed * gain
    d_hidden = e - jnp.mean(e, axis=-1, keepdims=True)
    d_hidden = (d_hidden - xhat * jnp.mean(e * xhat, axis=-1, keepdims=True)) * scale
    grad_in = (grad_own.astype(F32) + d_hidden).astype(BF).reshape(hidden_in.shape)

    return (
        output,
        grad_in,
        small[0],
        small[1],
        qkv_grad,
        small[2],
        out_grad,
        small[3],
        up_grad,
        small[4],
        down_grad,
        small[3],
    )


def solution(mesh):
    both = P(("dp", "ctx"))
    matrix = P(("dp", "ctx"), None)
    slots = P("dp", "ctx", None)
    in_specs = (
        slots,
        both,
        both,
        matrix,
        both,
        matrix,
        both,
        matrix,
        both,
        matrix,
        both,
        P("dp", None),
        P("dp", "ctx"),
        P("dp", None),
        slots,
    )
    out_specs = (
        slots,
        slots,
        both,
        both,
        matrix,
        both,
        matrix,
        both,
        matrix,
        both,
        matrix,
        both,
    )
    return jax.shard_map(
        on_device, mesh=mesh, in_specs=in_specs, out_specs=out_specs, check_vma=False
    )
```

```python
import functools
import math

import jax
import jax.numpy as jnp
from jax import lax
from jax.experimental import pallas as pl
from jax.experimental.pallas import tpu as pltpu
from jax.sharding import PartitionSpec as P

HEAD = 64
ROT = 32
BLK = 128
DOCS = 4
EPS = 1e-05
NEG = -1e30
PAIR = 2 * HEAD
KEYS = 256
LONGEST = 1024
PAIRS = 2
LOOSE = 2
FRACTION = 5.0
SCALE = HEAD**-0.5
ALL = ("dp", "ctx")
BF = jnp.bfloat16
F32 = jnp.float32


def partner(x):
    lane = lax.broadcasted_iota(jnp.int32, x.shape, 1) % HEAD
    return jnp.where(
        lane < ROT // 2, pltpu.roll(x, PAIR - ROT // 2, 1), pltpu.roll(x, ROT // 2, 1)
    )


def dot(a, b):
    return jnp.dot(a, b, preferred_element_type=F32)


def dot_t(a, b):
    return lax.dot_general(a, b, (((1,), (1,)), ((), ())), preferred_element_type=F32)


def aligned_rows(index, size):
    return pl.ds(pl.multiple_of(index * size, size), size)


def attention_kernel(
    place_ref,
    slot_ref,
    low_ref,
    qkv_ref,
    cot_ref,
    cos_ref,
    sin_ref,
    first_ref,
    att_ref,
    grad_ref,
    q_st,
    do_st,
    k_s,
    v_s,
    k_t,
    v_t,
    dk_s,
    dv_s,
    p_s,
    dp_s,
):
    slots = qkv_ref.shape[0]
    blocks = slots // BLK
    pairs = k_s.shape[0]
    lane_first = lax.broadcasted_iota(jnp.int32, (BLK, PAIR), 1) < HEAD
    row_first = lax.broadcasted_iota(jnp.int32, (PAIR, BLK), 0) < HEAD

    def stack(value):
        zero = jnp.zeros_like(value)
        both = [jnp.where(lane_first, value, zero), jnp.where(lane_first, zero, value)]
        return jnp.concatenate(both, axis=0).astype(BF)

    def columns(pair, which, count=3):
        start = (pair * count + which) * PAIR
        return slice(start, start + PAIR)

    def load_block(b, carry):
        rows = aligned_rows(b, BLK)
        place = place_ref[b]
        out_rows = aligned_rows(place, BLK)
        cosine = cos_ref[rows, :]
        sine = sin_ref[rows, :]
        for pair in range(pairs):
            q = qkv_ref[rows, columns(pair, 0)]
            k = qkv_ref[rows, columns(pair, 1)]
            v = qkv_ref[rows, columns(pair, 2)]
            q = (q * cosine + partner(q) * sine).astype(BF).astype(F32) * SCALE
            k = k * cosine + partner(k) * sine
            q_st[pair, aligned_rows(place, 2 * BLK), :] = stack(q)
            do = cot_ref[rows, columns(pair, 0, 1)].astype(F32)
            do_st[pair, aligned_rows(place, 2 * BLK), :] = stack(do)
            k_s[pair, out_rows, :] = k.astype(BF)
            v_s[pair, out_rows, :] = v.astype(BF)
            k_t[pair, out_rows, :] = k.T.astype(BF)
            v_t[pair, out_rows, :] = v.T.astype(BF)
        return carry

    lax.fori_loop(0, blocks, load_block, 0, unroll=LOOSE)
    dk_s[...] = jnp.zeros_like(dk_s)
    dv_s[...] = jnp.zeros_like(dv_s)

    def tiles_of(i, low, count):
        stacked = aligned_rows(i, 2 * BLK)
        first = first_ref[pl.ds(i, 1), :]
        row = lax.broadcasted_iota(jnp.int32, (KEYS, BLK), 0)
        own = i * BLK + lax.broadcasted_iota(jnp.int32, (1, BLK), 1)
        every = range(pairs)
        top = [None] * pairs
        for t in range(count):
            keys = aligned_rows(low + t, KEYS)
            part = slice(t * KEYS, (t + 1) * KEYS)
            place = (low + t) * KEYS
            allowed = row >= first - place
            if t == count - 1:
                allowed = allowed & (row <= own - place)
            allowed = jnp.concatenate([allowed, allowed], axis=1)
            for pair in every:
                s = dot_t(k_s[pair, keys, :], q_st[pair, stacked, :])
                s = jnp.where(allowed, s, NEG)
                p_s[pair, part, :] = s
                dp_s[pair, part, :] = dot_t(v_s[pair, keys, :], do_st[pair, stacked, :])
                here = jnp.max(s, axis=0, keepdims=True)
                top[pair] = here if t == 0 else jnp.maximum(top[pair], here)
        total = [0.0] * pairs
        inner = [0.0] * pairs
        for t in range(count):
            part = slice(t * KEYS, (t + 1) * KEYS)
            for pair in every:
                p = jnp.exp(p_s[pair, part, :] - top[pair])
                p_s[pair, part, :] = p
                total[pair] += jnp.sum(p, axis=0, keepdims=True)
                inner[pair] += jnp.sum(p * dp_s[pair, part, :], axis=0, keepdims=True)
        inverse = [1.0 / x for x in total]
        inner = [x * y for x, y in zip(inner, inverse)]
        out = [0.0] * pairs
        dq = [0.0] * pairs
        for t in range(count):
            part = slice(t * KEYS, (t + 1) * KEYS)
            keys = aligned_rows(low + t, KEYS)
            for pair in every:
                p = p_s[pair, part, :] * inverse[pair]
                ds = (p * (dp_s[pair, part, :] - inner[pair])).astype(BF)
                p = p.astype(BF)
                v_turned = v_t[pair, keys, :]
                k_turned = k_t[pair, keys, :]
                v_turned = jnp.concatenate([v_turned[:BLK], v_turned[BLK:]], axis=1)
                k_turned = jnp.concatenate([k_turned[:BLK], k_turned[BLK:]], axis=1)
                out[pair] += dot(v_turned, p)
                dq[pair] += dot(k_turned, ds)
                dv_s[pair, keys, :] += dot(p, do_st[pair, stacked, :])
                dk_s[pair, keys, :] += dot(ds, q_st[pair, stacked, :])
        slot_rows = aligned_rows(slot_ref[i], BLK)
        for pair in every:
            x = jnp.where(row_first, out[pair][:, :BLK], out[pair][:, BLK:]).T
            att_ref[slot_rows, columns(pair, 0, 1)] = x.astype(BF)
            x = (jnp.where(row_first, dq[pair][:, :BLK], dq[pair][:, BLK:]) * SCALE).T
            x = x * cos_ref[slot_rows, :] - partner(x) * sin_ref[slot_rows, :]
            grad_ref[slot_rows, columns(pair, 0)] = x.astype(BF)

    most = p_s.shape[1] // KEYS

    def query_block(i, carry):
        low = low_ref[i]
        count = (i * BLK) // KEYS + 1 - low
        for n in range(1, most + 1):
            pl.when(count == n)(functools.partial(tiles_of, i, low, n))
        return carry

    lax.fori_loop(0, blocks, query_block, 0)

    def store_block(b, carry):
        rows = aligned_rows(b, BLK)
        in_rows = aligned_rows(place_ref[b], BLK)
        for pair in range(pairs):
            dk = dk_s[pair, in_rows, :]
            dk = dk * cos_ref[rows, :] - partner(dk) * sin_ref[rows, :]
            grad_ref[rows, columns(pair, 1)] = dk.astype(BF)
            grad_ref[rows, columns(pair, 2)] = dv_s[pair, in_rows, :].astype(BF)
        return carry

    lax.fori_loop(0, blocks, store_block, 0, unroll=LOOSE)


def attention(qkv, cotangent, cosine, sine, first_place, block_place, slot_block):
    slots, width = qkv.shape
    groups = width // (3 * PAIR)
    pairs = math.gcd(groups, PAIRS)
    wide = pairs * PAIR
    blocks = slots // BLK
    low = first_place[:, 0] // KEYS
    once = pl.Buffered(1)
    most = min(LONGEST // KEYS + 1, slots // KEYS)
    grid_spec = pltpu.PrefetchScalarGridSpec(
        num_scalar_prefetch=3,
        grid=(groups // pairs,),
        in_specs=[
            pl.BlockSpec((slots, 3 * wide), lambda g, *_: (0, g)),
            pl.BlockSpec((slots, wide), lambda g, *_: (0, g)),
            pl.BlockSpec((slots, PAIR), lambda g, *_: (0, 0), pipeline_mode=once),
            pl.BlockSpec((slots, PAIR), lambda g, *_: (0, 0), pipeline_mode=once),
            pl.BlockSpec((blocks, BLK), lambda g, *_: (0, 0), pipeline_mode=once),
        ],
        out_specs=[
            pl.BlockSpec((slots, wide), lambda g, *_: (0, g)),
            pl.BlockSpec((slots, 3 * wide), lambda g, *_: (0, g)),
        ],
        scratch_shapes=[
            pltpu.VMEM((pairs, 2 * slots, PAIR), BF),
            pltpu.VMEM((pairs, 2 * slots, PAIR), BF),
            pltpu.VMEM((pairs, slots, PAIR), BF),
            pltpu.VMEM((pairs, slots, PAIR), BF),
            pltpu.VMEM((pairs, slots, PAIR), BF),
            pltpu.VMEM((pairs, slots, PAIR), BF),
            pltpu.VMEM((pairs, slots, PAIR), F32),
            pltpu.VMEM((pairs, slots, PAIR), F32),
            pltpu.VMEM((pairs, most * KEYS, 2 * BLK), F32),
            pltpu.VMEM((pairs, most * KEYS, 2 * BLK), F32),
        ],
    )
    tiles = groups * blocks * (blocks // 4)
    return pl.pallas_call(
        attention_kernel,
        out_shape=[
            jax.ShapeDtypeStruct((slots, groups * PAIR), BF),
            jax.ShapeDtypeStruct((slots, width), BF),
        ],
        grid_spec=grid_spec,
        compiler_params=pltpu.CompilerParams(vmem_limit_bytes=50 * 1024 * 1024),
        cost_estimate=pl.CostEstimate(
            flops=tiles * 2 * BLK * BLK * PAIR,
            bytes_accessed=qkv.size,
            transcendentals=0,
        ),
        name="attention",
    )(block_place, slot_block, low, qkv, cotangent, cosine, sine, first_place)


def pick_rows(found, order, rows):
    arrays, places = [], []
    for key in order:
        array, start = found[key]
        held = [i for i, known in enumerate(arrays) if known is array]
        if not held:
            arrays.append(array)
            held = [len(arrays) - 1]
        places.append((held[0], start // rows))
    return arrays, places


def visit_blocks(body, found, order, rows, extra, outs, name):
    arrays, places = pick_rows(found, order, rows)
    width = arrays[0].shape[1]

    def kernel(*refs):
        step = pl.program_id(0)
        given = refs[len(arrays) : len(arrays) + len(extra)]
        for number, (which, block) in enumerate(places):

            @pl.when(step == number)
            def _(ref=refs[which], block=block):
                results = body(ref[block * rows : (block + 1) * rows, :], *[g[...] for g in given])
                for out, value in zip(refs[-outs:], results):
                    out[...] = value

    once = pl.Buffered(1)
    held = arrays + list(extra)
    size = len(order) * rows * width
    return pl.pallas_call(
        kernel,
        grid=(len(order),),
        in_specs=[pl.BlockSpec(a.shape, lambda i: (0, 0), pipeline_mode=once) for a in held],
        out_specs=[pl.BlockSpec((rows, width), lambda i: (i, 0))] * outs,
        out_shape=[jax.ShapeDtypeStruct((len(order) * rows, width), BF)] * outs,
        compiler_params=pltpu.CompilerParams(vmem_limit_bytes=40 * 1024 * 1024),
        cost_estimate=pl.CostEstimate(flops=size * 10, bytes_accessed=4 * size, transcendentals=0),
        name=name,
    )(*held)


def norm_blocks(found, order, rows, gain, shift):
    def body(x, gain, shift):
        x, _ = standardise(x.astype(F32))
        return (x * gain + shift).astype(BF), x.astype(BF)

    return visit_blocks(body, found, order, rows, [gain[None, :], shift[None, :]], 2, "norm_rows")


def join_blocks(found, order, rows):
    return visit_blocks(lambda x: (x,), found, order, rows, [], 1, "join_rows")[0]


def deal_columns(matrices, chunks):
    rows = matrices[0].shape[0]
    width = sum(stop - start for parts in chunks for start, stop in parts[0])
    size = rows * width * len(chunks[0])

    def kernel(*refs):
        values = [ref[...].astype(F32) for ref in refs[:-1]]
        for target in range(len(chunks[0])):
            part = [
                x[:, start:stop] for x, parts in zip(values, chunks) for start, stop in parts[target]
            ]
            refs[-1][target] = jnp.concatenate(part, axis=1).astype(BF)

    return pl.pallas_call(
        kernel,
        out_shape=jax.ShapeDtypeStruct((len(chunks[0]), rows, width), BF),
        cost_estimate=pl.CostEstimate(flops=size, bytes_accessed=4 * size, transcendentals=0),
        name="deal_columns",
    )(*matrices)


def collect_columns(blocks, chunks):
    order = []
    for source, parts in enumerate(chunks):
        place = 0
        for start, stop in parts:
            order.append((start, source, place, place + stop - start))
            place += stop - start
    order.sort()
    width = blocks.shape[0] * blocks.shape[2]

    def kernel(x_ref, o_ref):
        x = [x_ref[source].astype(F32) for source in range(len(chunks))]
        o_ref[...] = jnp.concatenate([x[i][:, low:high] for _, i, low, high in order], axis=1)

    return pl.pallas_call(
        kernel,
        out_shape=jax.ShapeDtypeStruct((blocks.shape[1], width), F32),
        cost_estimate=pl.CostEstimate(
            flops=blocks.size, bytes_accessed=6 * blocks.size, transcendentals=0
        ),
        name="collect_columns",
    )(blocks)


def exchange(value, axis, size, offset):
    return lax.ppermute(value, axis, [(i, i ^ offset) for i in range(size)])


def after(value, *others):
    return lax.optimization_barrier((value,) + others)[0]


def half_blocks(size):
    if size == 4:
        return [(0, 0), (0, 1), (1, 0), (2, 1), (2, 0), (3, 0), (1, 1), (3, 1)]
    return [(j, half) for j in range(size) for half in range(2)]


def split_halves(value, j, found):
    half = value.shape[0] // 2
    found[j, 0], found[j, 1] = (value, 0), (value, half)


def gather_two(first, second, size, wait):
    send = functools.partial(exchange, axis="ctx", size=size)
    half = first.shape[0] // 2
    left, right = {}, {}
    split_halves(first, 0, left)
    split_halves(second, 0, right)
    if size != 4:
        for j in range(1, size):
            split_halves(send(first, offset=j), j, left)
        for j in range(1, size):
            split_halves(send(second, offset=j), j, right)
        return left, right
    one, two = send(first, offset=1), send(first, offset=2)
    split_halves(one, 1, left)
    split_halves(two, 2, left)
    one, two, second = lax.optimization_barrier((one, two, second) + wait)[:3]
    near = send(jnp.concatenate([two[half:], second], axis=0), offset=1)
    far = send(jnp.concatenate([one[:half], second], axis=0), offset=2)
    left[3, 0], left[3, 1] = (far, 0), (near, 0)
    right[1, 0], right[1, 1] = (near, half), (near, 2 * half)
    right[2, 0], right[2, 1] = (far, half), (far, 2 * half)
    right[3, 0] = (send(near[half : 2 * half], offset=2), 0)
    right[3, 1] = (send(far[2 * half :], offset=1), 0)
    return left, right


def sum_ranges(size):
    if size == 4:
        return (0, 4), [(4, 6), (6, 8)]
    return (0, 2), [(2 * j, 2 * j + 2) for j in range(1, size)]


def sum_send(pieces, size):
    distances = (2, 1) if size == 4 else range(1, size)
    return tuple(exchange(x.astype(BF), "ctx", size, j) for x, j in zip(pieces, distances))


def sum_end(own, arrived, size, together=False):
    if size != 4:
        return sum([x.astype(F32) for x in arrived], own), arrived, arrived
    half = own.shape[0] // 4
    far, near = arrived
    top = (own[2 * half : 3 * half] + far[half:].astype(F32)).astype(BF)
    low = (own[3 * half :] + near[half:].astype(F32)).astype(BF)
    sent = lax.optimization_barrier((top, low)) if together else (top, low)
    last = (exchange(sent[0], "ctx", size, 1), exchange(sent[1], "ctx", size, 2))
    top = own[:half] + far[:half].astype(F32) + last[0].astype(F32)
    low = own[half : 2 * half] + near[:half].astype(F32) + last[1].astype(F32)
    return jnp.concatenate([top, low], axis=0), last, sent


def gather_small(value, devices):
    copies = jnp.broadcast_to(value, (devices,) + value.shape)
    return lax.all_to_all(copies, ALL, split_axis=0, concat_axis=0, tiled=True)


def gather_dp(value):
    return lax.all_gather(value, "dp", axis=0, tiled=True)


def scatter_dp(value):
    return lax.psum_scatter(value, "dp", scatter_dimension=0, tiled=True)


def swap_ctx(value):
    return lax.all_to_all(value, "ctx", split_axis=0, concat_axis=0, tiled=True)


def matmul(a, b):
    return jnp.dot(a, b, preferred_element_type=F32)


def matmul_t(a, b):
    return lax.dot_general(a, b, (((1,), (1,)), ((), ())), preferred_element_type=F32)


def outer(a, b):
    return lax.dot_general(a, b, (((0,), (0,)), ((), ())), preferred_element_type=F32)


CONTRACT = {"nn": ((1,), (0,)), "nt": ((1,), (1,)), "tn": ((0,), (0,))}


def tile_of(size):
    return next(t for t in (1024, 768, 512, 384, 256, 128, size) if size % t == 0)


def product(kind, pairs, outs=(BF,), finish=None, extras=(), row_range=None):
    a, b = pairs[0]
    rows = a.shape[1] if kind == "tn" else a.shape[0]
    columns = b.shape[0] if kind == "nt" else b.shape[1]
    low, high = row_range or (0, rows)
    tall, wide = tile_of(high - low), tile_of(columns)
    skip = low // tall
    in_specs, operands = [], []
    for a, b in pairs:
        if kind == "tn":
            in_specs.append(pl.BlockSpec((a.shape[0], tall), lambda j, i: (0, i + skip)))
        else:
            in_specs.append(pl.BlockSpec((tall, a.shape[1]), lambda j, i: (i + skip, 0)))
        if kind == "nt":
            in_specs.append(pl.BlockSpec((wide, b.shape[1]), lambda j, i: (j, 0)))
        else:
            in_specs.append(pl.BlockSpec((b.shape[0], wide), lambda j, i: (0, j)))
        operands += [a, b]
    for extra in extras:
        if extra.shape[0] == 1:
            in_specs.append(pl.BlockSpec((1, wide), lambda j, i: (0, j)))
        else:
            in_specs.append(pl.BlockSpec((tall, wide), lambda j, i: (i + skip, j)))
        operands.append(extra)
    count, chunk = len(pairs), min(256, wide)
    depth = sum(a.shape[0] if kind == "tn" else a.shape[1] for a, _ in pairs)

    def kernel(*refs):
        for start in range(0, wide, chunk):
            part = slice(start, start + chunk)
            total = None
            for p in range(count):
                right = refs[2 * p + 1]
                right = right[part, :] if kind == "nt" else right[:, part]
                term = lax.dot_general(
                    refs[2 * p][...], right, (CONTRACT[kind], ((), ())), preferred_element_type=F32
                )
                total = term if total is None else total + term
            more = [refs[2 * count + n][:, part] for n in range(len(extras))]
            results = finish(total, *more) if finish else (total,)
            for ref, value in zip(refs[-len(outs) :], results):
                ref[:, part] = value.astype(ref.dtype)

    shape = (high - low, columns)
    result = pl.pallas_call(
        kernel,
        grid=(columns // wide, (high - low) // tall),
        in_specs=in_specs,
        out_specs=[pl.BlockSpec((tall, wide), lambda j, i: (i, j))] * len(outs),
        out_shape=[jax.ShapeDtypeStruct(shape, dtype) for dtype in outs],
        compiler_params=pltpu.CompilerParams(vmem_limit_bytes=56 * 1024 * 1024),
        cost_estimate=pl.CostEstimate(
            flops=int(2 * FRACTION * shape[0] * shape[1] * depth),
            bytes_accessed=shape[0] * shape[1],
            transcendentals=0,
        ),
        name="product_" + kind,
    )(*operands)
    return result if len(outs) > 1 else result[0]


def standardise(hidden):
    average = jnp.mean(hidden, axis=-1, keepdims=True)
    centred = hidden - average
    variance = jnp.mean(centred * centred, axis=-1, keepdims=True)
    scale = lax.rsqrt(variance + EPS)
    return centred * scale, scale


def gelu_pair(x):
    root, cubic = math.sqrt(2.0 / math.pi), 0.044715
    square = x * x
    gate = 0.5 + 0.5 * jnp.tanh(x * (root + (root * cubic) * square))
    value = x * gate
    slope = gate + value * (1.0 - gate) * (2.0 * root + (6.0 * root * cubic) * square)
    return value, slope


def on_device(
    hidden_in,
    ln_gain,
    ln_bias,
    w_qkv,
    b_qkv,
    w_out,
    b_out,
    w_up,
    b_up,
    w_down,
    b_down,
    segment_ids,
    positions,
    token_order,
    grad_out,
):
    N, C = lax.axis_size("dp"), lax.axis_size("ctx")
    c = lax.axis_index("ctx")
    rows, own_slots, width = hidden_in.shape
    assert rows == 1
    heads = width // HEAD
    own_heads = heads // C
    groups = own_heads // 2
    ff_block = w_down.shape[0]
    row_block = w_qkv.shape[0]
    own_ff = N * ff_block
    hidden_own = hidden_in.reshape(own_slots, width)
    grad_own = grad_out.reshape(own_slots, width)


    sizes = [ln_gain.shape[0], ln_bias.shape[0], b_qkv.shape[0], b_out.shape[0]]
    sizes += [b_up.shape[0], b_down.shape[0]]
    cuts = [sum(sizes[:i]) for i in range(1, len(sizes))]
    small = jnp.concatenate([ln_gain, ln_bias, b_qkv, b_out, b_up, b_down])
    small = gather_small(small, N * C)
    hidden_parts, grad_parts = gather_two(hidden_own, grad_own, C, (small,))
    pieces = jnp.split(small, cuts, axis=1)
    gain, shift, qkv_bias, out_bias, up_bias, down_bias = [p.reshape(-1).astype(F32) for p in pieces]
    qkv_chunks = [
        [
            (part * width + (i * C + t) * HEAD, part * width + (i * C + t + 1) * HEAD)
            for pair in range(groups)
            for part in range(3)
            for i in (2 * pair, 2 * pair + 1)
        ]
        for t in range(C)
    ]
    up_chunks = [
        [((i * C + t) * ff_block, (i * C + t + 1) * ff_block) for i in range(N)] for t in range(C)
    ]
    aligned = row_block == HEAD
    if aligned:
        w_out_own = gather_dp(w_out)
    else:
        everything = lax.all_gather(w_out, ALL, axis=0, tiled=True)
        everything = everything.reshape(own_heads, C, HEAD, width)
        w_out_own = lax.dynamic_index_in_dim(everything, c, 1, keepdims=False)
        w_out_own = w_out_own.reshape(own_heads * HEAD, width)
    both_rows = swap_ctx(deal_columns((w_up, w_qkv), (up_chunks, qkv_chunks)))
    both_rows = both_rows.reshape(C * row_block, -1)
    up_rows, qkv_rows = both_rows[:, :own_ff], both_rows[:, own_ff:]
    w_up_own = gather_dp(up_rows)

    half_block = jnp.array([j for j, _ in half_blocks(C)], jnp.int32) ^ c
    half_block = 2 * half_block + jnp.array([half for _, half in half_blocks(C)], jnp.int32)
    row_order, row_ids = token_order.reshape(-1), segment_ids.reshape(-1)
    slots = row_order.shape[0]
    first = jnp.zeros_like(row_order)
    for document in range(DOCS):
        inside = row_ids == document
        first = jnp.where(inside, jnp.min(jnp.where(inside, row_order, slots)), first)
    order_all, first_all = [
        jnp.take(x.reshape(2 * C, -1), half_block, axis=0).reshape(-1) for x in (row_order, first)
    ]
    position_all = order_all - first_all
    block_place = order_all[::BLK] // BLK
    slot_block = jnp.argsort(block_place).astype(jnp.int32)
    first_place = jnp.take(first_all.reshape(-1, BLK), slot_block, axis=0)
    half = ROT // 2
    lane = jnp.arange(PAIR, dtype=jnp.int32) % HEAD
    frequency = 10000.0 ** (-(lane % half).astype(F32) * 2.0 / ROT)
    frequency = jnp.where(lane < ROT, frequency, 0.0)
    angles = position_all.astype(F32)[:, None] * frequency
    cosine, sine = jnp.cos(angles), jnp.sin(angles) * jnp.where(lane < half, -1.0, 1.0)

    own_bias = lax.dynamic_index_in_dim(qkv_bias.reshape(3, groups, 2, C, HEAD), c, 3, keepdims=False)
    own_bias = own_bias.transpose(1, 0, 2, 3).reshape(-1)
    gain, cosine, sine, first_place, block_place, slot_block, own_bias = lax.optimization_barrier(
        (gain, cosine, sine, first_place, block_place, slot_block, own_bias)
    )
    step = own_slots // 2
    normed, xhat_all = norm_blocks(hidden_parts, half_blocks(C), step, gain, shift)
    w_down_own = gather_dp(after(w_down, up_rows))
    own_up_bias = lax.dynamic_index_in_dim(up_bias.reshape(N, C, ff_block), c, 1, keepdims=False)
    up = matmul(after(normed, w_out_own), w_up_own) + own_up_bias.reshape(-1)
    value, slope = gelu_pair(up)
    active, slope = lax.optimization_barrier((value.astype(BF), slope))
    if C == 4:
        for key in ((3, 0), (3, 1)):
            grad_parts[key] = (after(grad_parts[key][0], active), grad_parts[key][1])
    grad_all = join_blocks(grad_parts, half_blocks(C), step)
    w_qkv_own = gather_dp(qkv_rows)
    d_attended = matmul_t(grad_all, w_out_own).astype(BF)

    def column_grad(part, chunks):
        own = scatter_dp(part)
        return own, collect_columns(swap_ctx(own.reshape(C, row_block, -1)), chunks)

    d_up = (matmul_t(after(grad_all, d_attended), w_down_own) * slope).astype(BF)
    up_part = outer(normed, d_up).astype(BF)
    up_rows_grad, up_grad = column_grad(up_part, up_chunks)

    down_part = outer(after(active, up_part), grad_all).astype(BF)
    down_rows = scatter_dp(down_part)


    qkv = matmul(after(normed, down_part), w_qkv_own) + own_bias
    attended, d_qkv = attention(
        qkv, d_attended, cosine, sine, first_place, block_place, slot_block
    )

    near_range, away_ranges = sum_ranges(C)

    def out_rows(half_range, dtype, attended):
        pairs = [(active, w_down_own), (attended, w_out_own)]
        return product("nn", pairs, (dtype,), row_range=[i * step for i in half_range])

    out_away = [out_rows(r, BF, attended) for r in away_ranges[:1]]
    attended_then = after(attended, up_grad, *out_away)
    out_away += [out_rows(r, BF, attended_then) for r in away_ranges[1:]]
    out_arrived = sum_send(out_away, C)
    out_part = outer(after(attended, *out_away), grad_all)
    if aligned:
        out_part = out_part.astype(BF)
        out_grad = scatter_dp(out_part)
    else:
        spread = jnp.zeros((own_heads, C, HEAD, width), F32)
        spread = lax.dynamic_update_index_in_dim(
            spread, out_part.reshape(own_heads, HEAD, width), c, 1
        )
        out_grad = lax.psum_scatter(
            spread.reshape(heads * HEAD, width), ALL, scatter_dimension=0, tiled=True
        )

    qkv_part = outer(after(normed, up_rows_grad, out_part), d_qkv).astype(BF)
    _, qkv_grad = column_grad(qkv_part, qkv_chunks)
    out_near = out_rows(near_range, F32, after(attended, qkv_part))

    def normed_rows(half_range, dtype, d_qkv):
        pairs = [(d_qkv, w_qkv_own), (d_up, w_up_own)]
        return product("nt", pairs, (dtype,), row_range=[i * step for i in half_range])

    d_away = [normed_rows(r, BF, after(d_qkv, out_near)) for r in away_ranges]
    d_arrived = sum_send(d_away, C)
    d_near = normed_rows(near_range, F32, after(d_qkv, *d_away, *out_arrived))
    out_sum, _, _ = sum_end(after(out_near, d_near), out_arrived, C)
    output = hidden_own.astype(F32) + out_sum + (out_bias + down_bias)
    output = output.astype(BF).reshape(hidden_in.shape)

    down_grad = after(down_rows, d_near).astype(F32)
    out_grad = after(out_grad, d_near).astype(F32)

    devices = N * C
    gain_grad = shift_grad = 0.0
    for r, piece in zip([near_range] + away_ranges, [d_near] + d_away):
        piece = piece.astype(F32)
        gain_grad += jnp.sum(piece * xhat_all[r[0] * step : r[1] * step].astype(F32), axis=0)
        shift_grad += jnp.sum(piece, axis=0)
    bias_grad = jnp.sum(grad_own.astype(F32), axis=0)
    up_bias_grad = jnp.sum(d_up.astype(F32), axis=0).reshape(N, 1, ff_block)
    qkv_bias_grad = jnp.sum(d_qkv.astype(F32), axis=0).reshape(groups, 3, 2, HEAD)
    qkv_bias_grad = qkv_bias_grad.transpose(1, 0, 2, 3)[:, :, :, None, :]
    mine = jnp.arange(C) == c
    up_bias_grad = jnp.where(mine[None, :, None], up_bias_grad, 0.0)
    qkv_bias_grad = jnp.where(mine[None, None, None, :, None], qkv_bias_grad, 0.0)
    small = [gain_grad, shift_grad, qkv_bias_grad, bias_grad, up_bias_grad]
    small = jnp.concatenate([s.reshape(devices, -1) for s in small], axis=1)
    d_normed, _, d_sent = sum_end(d_near, d_arrived, C, True)
    small = after(small, *d_sent)
    small = lax.all_to_all(small, ALL, split_axis=0, concat_axis=0, tiled=True)
    small = jnp.split(jnp.sum(small, axis=0), cuts[:4])

    d_normed = after(d_normed, down_rows, qkv_grad, *small)
    xhat, scale = standardise(hidden_own.astype(F32))
    e = d_normed * gain
    d_hidden = e - jnp.mean(e, axis=-1, keepdims=True)
    d_hidden = (d_hidden - xhat * jnp.mean(e * xhat, axis=-1, keepdims=True)) * scale
    grad_in = (grad_own.astype(F32) + d_hidden).astype(BF).reshape(hidden_in.shape)

    return (
        output,
        grad_in,
        small[0],
        small[1],
        qkv_grad,
        small[2],
        out_grad,
        small[3],
        up_grad,
        small[4],
        down_grad,
        small[3],
    )


def solution(mesh):
    both = P(("dp", "ctx"))
    matrix = P(("dp", "ctx"), None)
    slots = P("dp", "ctx", None)
    in_specs = (
        slots,
        both,
        both,
        matrix,
        both,
        matrix,
        both,
        matrix,
        both,
        matrix,
        both,
        P("dp", None),
        P("dp", "ctx"),
        P("dp", None),
        slots,
    )
    out_specs = (
        slots,
        slots,
        both,
        both,
        matrix,
        both,
        matrix,
        both,
        matrix,
        both,
        matrix,
        both,
    )
    return jax.shard_map(
        on_device, mesh=mesh, in_specs=in_specs, out_specs=out_specs, check_vma=False
    )
```

```python
import functools
import math

import jax
import jax.numpy as jnp
from jax import lax
from jax.experimental import pallas as pl
from jax.experimental.pallas import tpu as pltpu
from jax.sharding import PartitionSpec as P

HEAD = 64
ROT = 32
BLK = 128
DOCS = 4
EPS = 1e-05
NEG = -1e30
PAIR = 2 * HEAD
KEYS = 256
LONGEST = 1024
PAIRS = 2
LOOSE = 2
FRACTION = 5.0
SCALE = HEAD**-0.5
ALL = ("dp", "ctx")
BF = jnp.bfloat16
F32 = jnp.float32


def partner(x):
    lane = lax.broadcasted_iota(jnp.int32, x.shape, 1) % HEAD
    return jnp.where(
        lane < ROT // 2, pltpu.roll(x, PAIR - ROT // 2, 1), pltpu.roll(x, ROT // 2, 1)
    )


def dot(a, b):
    return jnp.dot(a, b, preferred_element_type=F32)


def dot_t(a, b):
    return lax.dot_general(a, b, (((1,), (1,)), ((), ())), preferred_element_type=F32)


def aligned_rows(index, size):
    return pl.ds(pl.multiple_of(index * size, size), size)


def attention_kernel(
    place_ref,
    slot_ref,
    low_ref,
    qkv_ref,
    cot_ref,
    cos_ref,
    sin_ref,
    first_ref,
    att_ref,
    grad_ref,
    q_st,
    do_st,
    k_s,
    v_s,
    k_t,
    v_t,
    dk_s,
    dv_s,
    p_s,
    dp_s,
):
    slots = qkv_ref.shape[0]
    blocks = slots // BLK
    pairs = k_s.shape[0]
    lane_first = lax.broadcasted_iota(jnp.int32, (BLK, PAIR), 1) < HEAD
    row_first = lax.broadcasted_iota(jnp.int32, (PAIR, BLK), 0) < HEAD

    def stack(value):
        zero = jnp.zeros_like(value)
        both = [jnp.where(lane_first, value, zero), jnp.where(lane_first, zero, value)]
        return jnp.concatenate(both, axis=0).astype(BF)

    def columns(pair, which, count=3):
        start = (pair * count + which) * PAIR
        return slice(start, start + PAIR)

    def load_block(b, carry):
        rows = aligned_rows(b, BLK)
        place = place_ref[b]
        out_rows = aligned_rows(place, BLK)
        cosine = cos_ref[rows, :]
        sine = sin_ref[rows, :]
        for pair in range(pairs):
            q = qkv_ref[rows, columns(pair, 0)]
            k = qkv_ref[rows, columns(pair, 1)]
            v = qkv_ref[rows, columns(pair, 2)]
            q = (q * cosine + partner(q) * sine).astype(BF).astype(F32) * SCALE
            k = k * cosine + partner(k) * sine
            q_st[pair, aligned_rows(place, 2 * BLK), :] = stack(q)
            do = cot_ref[rows, columns(pair, 0, 1)].astype(F32)
            do_st[pair, aligned_rows(place, 2 * BLK), :] = stack(do)
            k_s[pair, out_rows, :] = k.astype(BF)
            v_s[pair, out_rows, :] = v.astype(BF)
            k_t[pair, out_rows, :] = k.T.astype(BF)
            v_t[pair, out_rows, :] = v.T.astype(BF)
        return carry

    lax.fori_loop(0, blocks, load_block, 0, unroll=LOOSE)
    dk_s[...] = jnp.zeros_like(dk_s)
    dv_s[...] = jnp.zeros_like(dv_s)

    def tiles_of(i, low, count):
        stacked = aligned_rows(i, 2 * BLK)
        first = first_ref[pl.ds(i, 1), :]
        row = lax.broadcasted_iota(jnp.int32, (KEYS, BLK), 0)
        own = i * BLK + lax.broadcasted_iota(jnp.int32, (1, BLK), 1)
        every = range(pairs)
        top = [None] * pairs
        for t in range(count):
            keys = aligned_rows(low + t, KEYS)
            part = slice(t * KEYS, (t + 1) * KEYS)
            place = (low + t) * KEYS
            allowed = row >= first - place
            if t == count - 1:
                allowed = allowed & (row <= own - place)
            allowed = jnp.concatenate([allowed, allowed], axis=1)
            for pair in every:
                s = dot_t(k_s[pair, keys, :], q_st[pair, stacked, :])
                s = jnp.where(allowed, s, NEG)
                p_s[pair, part, :] = s
                dp_s[pair, part, :] = dot_t(v_s[pair, keys, :], do_st[pair, stacked, :])
                here = jnp.max(s, axis=0, keepdims=True)
                top[pair] = here if t == 0 else jnp.maximum(top[pair], here)
        total = [0.0] * pairs
        inner = [0.0] * pairs
        for t in range(count):
            part = slice(t * KEYS, (t + 1) * KEYS)
            for pair in every:
                p = jnp.exp(p_s[pair, part, :] - top[pair])
                p_s[pair, part, :] = p
                total[pair] += jnp.sum(p, axis=0, keepdims=True)
                inner[pair] += jnp.sum(p * dp_s[pair, part, :], axis=0, keepdims=True)
        inverse = [1.0 / x for x in total]
        inner = [x * y for x, y in zip(inner, inverse)]
        out = [0.0] * pairs
        dq = [0.0] * pairs
        for t in range(count):
            part = slice(t * KEYS, (t + 1) * KEYS)
            keys = aligned_rows(low + t, KEYS)
            for pair in every:
                p = p_s[pair, part, :] * inverse[pair]
                ds = (p * (dp_s[pair, part, :] - inner[pair])).astype(BF)
                p = p.astype(BF)
                v_turned = v_t[pair, keys, :]
                k_turned = k_t[pair, keys, :]
                v_turned = jnp.concatenate([v_turned[:BLK], v_turned[BLK:]], axis=1)
                k_turned = jnp.concatenate([k_turned[:BLK], k_turned[BLK:]], axis=1)
                out[pair] += dot(v_turned, p)
                dq[pair] += dot(k_turned, ds)
                dv_s[pair, keys, :] += dot(p, do_st[pair, stacked, :])
                dk_s[pair, keys, :] += dot(ds, q_st[pair, stacked, :])
        slot_rows = aligned_rows(slot_ref[i], BLK)
        for pair in every:
            x = jnp.where(row_first, out[pair][:, :BLK], out[pair][:, BLK:]).T
            att_ref[slot_rows, columns(pair, 0, 1)] = x.astype(BF)
            x = (jnp.where(row_first, dq[pair][:, :BLK], dq[pair][:, BLK:]) * SCALE).T
            x = x * cos_ref[slot_rows, :] - partner(x) * sin_ref[slot_rows, :]
            grad_ref[slot_rows, columns(pair, 0)] = x.astype(BF)

    most = p_s.shape[1] // KEYS

    def query_block(i, carry):
        low = low_ref[i]
        count = (i * BLK) // KEYS + 1 - low
        for n in range(1, most + 1):
            pl.when(count == n)(functools.partial(tiles_of, i, low, n))
        return carry

    lax.fori_loop(0, blocks, query_block, 0)

    def store_block(b, carry):
        rows = aligned_rows(b, BLK)
        in_rows = aligned_rows(place_ref[b], BLK)
        for pair in range(pairs):
            dk = dk_s[pair, in_rows, :]
            dk = dk * cos_ref[rows, :] - partner(dk) * sin_ref[rows, :]
            grad_ref[rows, columns(pair, 1)] = dk.astype(BF)
            grad_ref[rows, columns(pair, 2)] = dv_s[pair, in_rows, :].astype(BF)
        return carry

    lax.fori_loop(0, blocks, store_block, 0, unroll=LOOSE)


def attention(qkv, cotangent, cosine, sine, first_place, block_place, slot_block):
    slots, width = qkv.shape
    groups = width // (3 * PAIR)
    pairs = math.gcd(groups, PAIRS)
    wide = pairs * PAIR
    blocks = slots // BLK
    low = first_place[:, 0] // KEYS
    once = pl.Buffered(1)
    most = min(LONGEST // KEYS + 1, slots // KEYS)
    grid_spec = pltpu.PrefetchScalarGridSpec(
        num_scalar_prefetch=3,
        grid=(groups // pairs,),
        in_specs=[
            pl.BlockSpec((slots, 3 * wide), lambda g, *_: (0, g)),
            pl.BlockSpec((slots, wide), lambda g, *_: (0, g)),
            pl.BlockSpec((slots, PAIR), lambda g, *_: (0, 0), pipeline_mode=once),
            pl.BlockSpec((slots, PAIR), lambda g, *_: (0, 0), pipeline_mode=once),
            pl.BlockSpec((blocks, BLK), lambda g, *_: (0, 0), pipeline_mode=once),
        ],
        out_specs=[
            pl.BlockSpec((slots, wide), lambda g, *_: (0, g)),
            pl.BlockSpec((slots, 3 * wide), lambda g, *_: (0, g)),
        ],
        scratch_shapes=[
            pltpu.VMEM((pairs, 2 * slots, PAIR), BF),
            pltpu.VMEM((pairs, 2 * slots, PAIR), BF),
            pltpu.VMEM((pairs, slots, PAIR), BF),
            pltpu.VMEM((pairs, slots, PAIR), BF),
            pltpu.VMEM((pairs, slots, PAIR), BF),
            pltpu.VMEM((pairs, slots, PAIR), BF),
            pltpu.VMEM((pairs, slots, PAIR), F32),
            pltpu.VMEM((pairs, slots, PAIR), F32),
            pltpu.VMEM((pairs, most * KEYS, 2 * BLK), F32),
            pltpu.VMEM((pairs, most * KEYS, 2 * BLK), F32),
        ],
    )
    tiles = groups * blocks * (blocks // 4)
    return pl.pallas_call(
        attention_kernel,
        out_shape=[
            jax.ShapeDtypeStruct((slots, groups * PAIR), BF),
            jax.ShapeDtypeStruct((slots, width), BF),
        ],
        grid_spec=grid_spec,
        compiler_params=pltpu.CompilerParams(vmem_limit_bytes=50 * 1024 * 1024),
        cost_estimate=pl.CostEstimate(
            flops=tiles * 2 * BLK * BLK * PAIR,
            bytes_accessed=qkv.size,
            transcendentals=0,
        ),
        name="attention",
    )(block_place, slot_block, low, qkv, cotangent, cosine, sine, first_place)


def pick_rows(found, order, rows):
    arrays, places = [], []
    for key in order:
        array, start = found[key]
        held = [i for i, known in enumerate(arrays) if known is array]
        if not held:
            arrays.append(array)
            held = [len(arrays) - 1]
        places.append((held[0], start // rows))
    return arrays, places


def visit_blocks(body, found, order, rows, extra, outs, name):
    arrays, places = pick_rows(found, order, rows)
    width = arrays[0].shape[1]

    def kernel(*refs):
        step = pl.program_id(0)
        given = refs[len(arrays) : len(arrays) + len(extra)]
        for number, (which, block) in enumerate(places):

            @pl.when(step == number)
            def _(ref=refs[which], block=block):
                results = body(ref[block * rows : (block + 1) * rows, :], *[g[...] for g in given])
                for out, value in zip(refs[-outs:], results):
                    out[...] = value

    once = pl.Buffered(1)
    held = arrays + list(extra)
    size = len(order) * rows * width
    return pl.pallas_call(
        kernel,
        grid=(len(order),),
        in_specs=[pl.BlockSpec(a.shape, lambda i: (0, 0), pipeline_mode=once) for a in held],
        out_specs=[pl.BlockSpec((rows, width), lambda i: (i, 0))] * outs,
        out_shape=[jax.ShapeDtypeStruct((len(order) * rows, width), BF)] * outs,
        compiler_params=pltpu.CompilerParams(vmem_limit_bytes=40 * 1024 * 1024),
        cost_estimate=pl.CostEstimate(flops=size * 10, bytes_accessed=4 * size, transcendentals=0),
        name=name,
    )(*held)


def norm_blocks(found, order, rows, gain, shift):
    def body(x, gain, shift):
        x, _ = standardise(x.astype(F32))
        return (x * gain + shift).astype(BF), x.astype(BF)

    return visit_blocks(body, found, order, rows, [gain[None, :], shift[None, :]], 2, "norm_rows")


def join_blocks(found, order, rows):
    return visit_blocks(lambda x: (x,), found, order, rows, [], 1, "join_rows")[0]


def deal_columns(matrices, chunks):
    rows = matrices[0].shape[0]
    width = sum(stop - start for parts in chunks for start, stop in parts[0])
    size = rows * width * len(chunks[0])

    def kernel(*refs):
        values = [ref[...].astype(F32) for ref in refs[:-1]]
        for target in range(len(chunks[0])):
            part = [
                x[:, start:stop] for x, parts in zip(values, chunks) for start, stop in parts[target]
            ]
            refs[-1][target] = jnp.concatenate(part, axis=1).astype(BF)

    return pl.pallas_call(
        kernel,
        out_shape=jax.ShapeDtypeStruct((len(chunks[0]), rows, width), BF),
        cost_estimate=pl.CostEstimate(flops=size, bytes_accessed=4 * size, transcendentals=0),
        name="deal_columns",
    )(*matrices)


def collect_columns(blocks, chunks):
    order = []
    for source, parts in enumerate(chunks):
        place = 0
        for start, stop in parts:
            order.append((start, source, place, place + stop - start))
            place += stop - start
    order.sort()
    width = blocks.shape[0] * blocks.shape[2]

    def kernel(x_ref, o_ref):
        x = [x_ref[source].astype(F32) for source in range(len(chunks))]
        o_ref[...] = jnp.concatenate([x[i][:, low:high] for _, i, low, high in order], axis=1)

    return pl.pallas_call(
        kernel,
        out_shape=jax.ShapeDtypeStruct((blocks.shape[1], width), F32),
        cost_estimate=pl.CostEstimate(
            flops=blocks.size, bytes_accessed=6 * blocks.size, transcendentals=0
        ),
        name="collect_columns",
    )(blocks)


def exchange(value, axis, size, offset):
    return lax.ppermute(value, axis, [(i, i ^ offset) for i in range(size)])


def after(value, *others):
    return lax.optimization_barrier((value,) + others)[0]


def half_blocks(size):
    if size == 4:
        return [(0, 0), (0, 1), (1, 0), (2, 1), (2, 0), (3, 0), (1, 1), (3, 1)]
    return [(j, half) for j in range(size) for half in range(2)]


def split_halves(value, j, found):
    half = value.shape[0] // 2
    found[j, 0], found[j, 1] = (value, 0), (value, half)


def gather_two(first, second, size, wait):
    send = functools.partial(exchange, axis="ctx", size=size)
    half = first.shape[0] // 2
    left, right = {}, {}
    split_halves(first, 0, left)
    split_halves(second, 0, right)
    if size != 4:
        for j in range(1, size):
            split_halves(send(first, offset=j), j, left)
        for j in range(1, size):
            split_halves(send(second, offset=j), j, right)
        return left, right
    one, two = send(first, offset=1), send(first, offset=2)
    split_halves(one, 1, left)
    split_halves(two, 2, left)
    one, two, second = lax.optimization_barrier((one, two, second) + wait)[:3]
    near = send(jnp.concatenate([two[half:], second], axis=0), offset=1)
    far = send(jnp.concatenate([one[:half], second], axis=0), offset=2)
    left[3, 0], left[3, 1] = (far, 0), (near, 0)
    right[1, 0], right[1, 1] = (near, half), (near, 2 * half)
    right[2, 0], right[2, 1] = (far, half), (far, 2 * half)
    right[3, 0] = (send(near[half : 2 * half], offset=2), 0)
    right[3, 1] = (send(far[2 * half :], offset=1), 0)
    return left, right


def sum_ranges(size):
    if size == 4:
        return (0, 4), [(4, 6), (6, 8)]
    return (0, 2), [(2 * j, 2 * j + 2) for j in range(1, size)]


def sum_send(pieces, size):
    distances = (2, 1) if size == 4 else range(1, size)
    return tuple(exchange(x.astype(BF), "ctx", size, j) for x, j in zip(pieces, distances))


def sum_end(own, arrived, size):
    if size != 4:
        return sum([x.astype(F32) for x in arrived], own), arrived, arrived
    half = own.shape[0] // 4
    far, near = arrived
    top = (own[2 * half : 3 * half] + far[half:].astype(F32)).astype(BF)
    low = (own[3 * half :] + near[half:].astype(F32)).astype(BF)
    sent = lax.optimization_barrier((top, low))
    last = (exchange(sent[0], "ctx", size, 1), exchange(sent[1], "ctx", size, 2))
    top = own[:half] + far[:half].astype(F32) + last[0].astype(F32)
    low = own[half : 2 * half] + near[:half].astype(F32) + last[1].astype(F32)
    return jnp.concatenate([top, low], axis=0), last, sent


def gather_small(value, devices):
    copies = jnp.broadcast_to(value, (devices,) + value.shape)
    return lax.all_to_all(copies, ALL, split_axis=0, concat_axis=0, tiled=True)


def gather_dp(value):
    return lax.all_gather(value, "dp", axis=0, tiled=True)


def scatter_dp(value):
    return lax.psum_scatter(value, "dp", scatter_dimension=0, tiled=True)


def swap_ctx(value):
    return lax.all_to_all(value, "ctx", split_axis=0, concat_axis=0, tiled=True)


def matmul(a, b):
    return jnp.dot(a, b, preferred_element_type=F32)


def matmul_t(a, b):
    return lax.dot_general(a, b, (((1,), (1,)), ((), ())), preferred_element_type=F32)


def outer(a, b):
    return lax.dot_general(a, b, (((0,), (0,)), ((), ())), preferred_element_type=F32)


CONTRACT = {"nn": ((1,), (0,)), "nt": ((1,), (1,)), "tn": ((0,), (0,))}


def tile_of(size):
    return next(t for t in (1024, 768, 512, 384, 256, 128, size) if size % t == 0)


def product(kind, pairs, outs=(BF,), finish=None, extras=(), row_range=None):
    a, b = pairs[0]
    rows = a.shape[1] if kind == "tn" else a.shape[0]
    columns = b.shape[0] if kind == "nt" else b.shape[1]
    low, high = row_range or (0, rows)
    tall, wide = tile_of(high - low), tile_of(columns)
    skip = low // tall
    in_specs, operands = [], []
    for a, b in pairs:
        if kind == "tn":
            in_specs.append(pl.BlockSpec((a.shape[0], tall), lambda j, i: (0, i + skip)))
        else:
            in_specs.append(pl.BlockSpec((tall, a.shape[1]), lambda j, i: (i + skip, 0)))
        if kind == "nt":
            in_specs.append(pl.BlockSpec((wide, b.shape[1]), lambda j, i: (j, 0)))
        else:
            in_specs.append(pl.BlockSpec((b.shape[0], wide), lambda j, i: (0, j)))
        operands += [a, b]
    for extra in extras:
        if extra.shape[0] == 1:
            in_specs.append(pl.BlockSpec((1, wide), lambda j, i: (0, j)))
        else:
            in_specs.append(pl.BlockSpec((tall, wide), lambda j, i: (i + skip, j)))
        operands.append(extra)
    count, chunk = len(pairs), min(256, wide)
    depth = sum(a.shape[0] if kind == "tn" else a.shape[1] for a, _ in pairs)

    def kernel(*refs):
        for start in range(0, wide, chunk):
            part = slice(start, start + chunk)
            total = None
            for p in range(count):
                right = refs[2 * p + 1]
                right = right[part, :] if kind == "nt" else right[:, part]
                term = lax.dot_general(
                    refs[2 * p][...], right, (CONTRACT[kind], ((), ())), preferred_element_type=F32
                )
                total = term if total is None else total + term
            more = [refs[2 * count + n][:, part] for n in range(len(extras))]
            results = finish(total, *more) if finish else (total,)
            for ref, value in zip(refs[-len(outs) :], results):
                ref[:, part] = value.astype(ref.dtype)

    shape = (high - low, columns)
    result = pl.pallas_call(
        kernel,
        grid=(columns // wide, (high - low) // tall),
        in_specs=in_specs,
        out_specs=[pl.BlockSpec((tall, wide), lambda j, i: (i, j))] * len(outs),
        out_shape=[jax.ShapeDtypeStruct(shape, dtype) for dtype in outs],
        compiler_params=pltpu.CompilerParams(vmem_limit_bytes=56 * 1024 * 1024),
        cost_estimate=pl.CostEstimate(
            flops=int(2 * FRACTION * shape[0] * shape[1] * depth),
            bytes_accessed=shape[0] * shape[1],
            transcendentals=0,
        ),
        name="product_" + kind,
    )(*operands)
    return result if len(outs) > 1 else result[0]


def standardise(hidden):
    average = jnp.mean(hidden, axis=-1, keepdims=True)
    centred = hidden - average
    variance = jnp.mean(centred * centred, axis=-1, keepdims=True)
    scale = lax.rsqrt(variance + EPS)
    return centred * scale, scale


def gelu_pair(x):
    root, cubic = math.sqrt(2.0 / math.pi), 0.044715
    square = x * x
    gate = 0.5 + 0.5 * jnp.tanh(x * (root + (root * cubic) * square))
    value = x * gate
    slope = gate + value * (1.0 - gate) * (2.0 * root + (6.0 * root * cubic) * square)
    return value, slope


def on_device(
    hidden_in,
    ln_gain,
    ln_bias,
    w_qkv,
    b_qkv,
    w_out,
    b_out,
    w_up,
    b_up,
    w_down,
    b_down,
    segment_ids,
    positions,
    token_order,
    grad_out,
):
    N, C = lax.axis_size("dp"), lax.axis_size("ctx")
    c = lax.axis_index("ctx")
    rows, own_slots, width = hidden_in.shape
    assert rows == 1
    heads = width // HEAD
    own_heads = heads // C
    groups = own_heads // 2
    ff_block = w_down.shape[0]
    row_block = w_qkv.shape[0]
    own_ff = N * ff_block
    hidden_own = hidden_in.reshape(own_slots, width)
    grad_own = grad_out.reshape(own_slots, width)


    sizes = [ln_gain.shape[0], ln_bias.shape[0], b_qkv.shape[0], b_out.shape[0]]
    sizes += [b_up.shape[0], b_down.shape[0]]
    cuts = [sum(sizes[:i]) for i in range(1, len(sizes))]
    small = jnp.concatenate([ln_gain, ln_bias, b_qkv, b_out, b_up, b_down])
    small = gather_small(small, N * C)
    hidden_parts, grad_parts = gather_two(hidden_own, grad_own, C, (small,))
    pieces = jnp.split(small, cuts, axis=1)
    gain, shift, qkv_bias, out_bias, up_bias, down_bias = [p.reshape(-1).astype(F32) for p in pieces]
    qkv_chunks = [
        [
            (part * width + (i * C + t) * HEAD, part * width + (i * C + t + 1) * HEAD)
            for pair in range(groups)
            for part in range(3)
            for i in (2 * pair, 2 * pair + 1)
        ]
        for t in range(C)
    ]
    up_chunks = [
        [((i * C + t) * ff_block, (i * C + t + 1) * ff_block) for i in range(N)] for t in range(C)
    ]
    aligned = row_block == HEAD
    if aligned:
        w_out_own = gather_dp(w_out)
    else:
        everything = lax.all_gather(w_out, ALL, axis=0, tiled=True)
        everything = everything.reshape(own_heads, C, HEAD, width)
        w_out_own = lax.dynamic_index_in_dim(everything, c, 1, keepdims=False)
        w_out_own = w_out_own.reshape(own_heads * HEAD, width)
    both_rows = swap_ctx(deal_columns((w_up, w_qkv), (up_chunks, qkv_chunks)))
    both_rows = both_rows.reshape(C * row_block, -1)
    up_rows, qkv_rows = both_rows[:, :own_ff], both_rows[:, own_ff:]
    w_up_own = gather_dp(up_rows)

    half_block = jnp.array([j for j, _ in half_blocks(C)], jnp.int32) ^ c
    half_block = 2 * half_block + jnp.array([half for _, half in half_blocks(C)], jnp.int32)
    row_order, row_ids = token_order.reshape(-1), segment_ids.reshape(-1)
    slots = row_order.shape[0]
    first = jnp.zeros_like(row_order)
    for document in range(DOCS):
        inside = row_ids == document
        first = jnp.where(inside, jnp.min(jnp.where(inside, row_order, slots)), first)
    order_all, first_all = [
        jnp.take(x.reshape(2 * C, -1), half_block, axis=0).reshape(-1) for x in (row_order, first)
    ]
    position_all = order_all - first_all
    block_place = order_all[::BLK] // BLK
    slot_block = jnp.argsort(block_place).astype(jnp.int32)
    first_place = jnp.take(first_all.reshape(-1, BLK), slot_block, axis=0)
    half = ROT // 2
    lane = jnp.arange(PAIR, dtype=jnp.int32) % HEAD
    frequency = 10000.0 ** (-(lane % half).astype(F32) * 2.0 / ROT)
    frequency = jnp.where(lane < ROT, frequency, 0.0)
    angles = position_all.astype(F32)[:, None] * frequency
    cosine, sine = jnp.cos(angles), jnp.sin(angles) * jnp.where(lane < half, -1.0, 1.0)

    own_bias = lax.dynamic_index_in_dim(qkv_bias.reshape(3, groups, 2, C, HEAD), c, 3, keepdims=False)
    own_bias = own_bias.transpose(1, 0, 2, 3).reshape(-1)
    gain, cosine, sine, first_place, block_place, slot_block, own_bias = lax.optimization_barrier(
        (gain, cosine, sine, first_place, block_place, slot_block, own_bias)
    )
    step = own_slots // 2
    normed, xhat_all = norm_blocks(hidden_parts, half_blocks(C), step, gain, shift)
    w_down_own = gather_dp(after(w_down, up_rows))
    own_up_bias = lax.dynamic_index_in_dim(up_bias.reshape(N, C, ff_block), c, 1, keepdims=False)
    up = matmul(after(normed, w_out_own), w_up_own) + own_up_bias.reshape(-1)
    value, slope = gelu_pair(up)
    active, slope = lax.optimization_barrier((value.astype(BF), slope))
    if C == 4:
        for key in ((3, 0), (3, 1)):
            grad_parts[key] = (after(grad_parts[key][0], active), grad_parts[key][1])
    grad_all = join_blocks(grad_parts, half_blocks(C), step)
    w_qkv_own = gather_dp(qkv_rows)
    d_attended = matmul_t(grad_all, w_out_own).astype(BF)

    def column_grad(part, chunks):
        own = scatter_dp(part)
        return own, collect_columns(swap_ctx(own.reshape(C, row_block, -1)), chunks)

    d_up = (matmul_t(after(grad_all, d_attended), w_down_own) * slope).astype(BF)
    up_part = outer(normed, d_up).astype(BF)
    up_rows_grad, up_grad = column_grad(up_part, up_chunks)

    down_part = outer(after(active, up_part), grad_all).astype(BF)
    down_rows = scatter_dp(down_part)


    qkv = matmul(after(normed, down_part), w_qkv_own) + own_bias
    attended, d_qkv = attention(
        qkv, d_attended, cosine, sine, first_place, block_place, slot_block
    )

    near_range, away_ranges = sum_ranges(C)

    def out_rows(half_range, dtype, attended):
        pairs = [(active, w_down_own), (attended, w_out_own)]
        return product("nn", pairs, (dtype,), row_range=[i * step for i in half_range])

    qkv_part = outer(after(normed, up_rows_grad), d_qkv).astype(BF)
    _, qkv_grad = column_grad(qkv_part, qkv_chunks)
    out_part = outer(after(attended, qkv_part), grad_all)
    if aligned:
        out_part = out_part.astype(BF)
        out_grad = scatter_dp(out_part)
    else:
        spread = jnp.zeros((own_heads, C, HEAD, width), F32)
        spread = lax.dynamic_update_index_in_dim(
            spread, out_part.reshape(own_heads, HEAD, width), c, 1
        )
        out_grad = lax.psum_scatter(
            spread.reshape(heads * HEAD, width), ALL, scatter_dimension=0, tiled=True
        )

    attended_first = after(attended, out_part)
    out_away = [out_rows(r, BF, attended_first) for r in away_ranges[:1]]
    attended_then = after(attended, up_grad, *out_away)
    out_away += [out_rows(r, BF, attended_then) for r in away_ranges[1:]]
    out_arrived = sum_send(out_away, C)
    out_near = out_rows(near_range, F32, after(attended, *out_away))

    def normed_rows(half_range, dtype, d_qkv):
        pairs = [(d_qkv, w_qkv_own), (d_up, w_up_own)]
        return product("nt", pairs, (dtype,), row_range=[i * step for i in half_range])

    d_away = [normed_rows(r, BF, after(d_qkv, out_near)) for r in away_ranges]
    d_arrived = sum_send(d_away, C)
    d_near = normed_rows(near_range, F32, after(d_qkv, *d_away, *out_arrived))
    out_sum, _, _ = sum_end(after(out_near, d_near), out_arrived, C)
    output = hidden_own.astype(F32) + out_sum + (out_bias + down_bias)
    output = output.astype(BF).reshape(hidden_in.shape)

    down_grad = after(down_rows, d_near).astype(F32)
    out_grad = after(out_grad, d_near).astype(F32)

    devices = N * C
    gain_grad = shift_grad = 0.0
    for r, piece in zip([near_range] + away_ranges, [d_near] + d_away):
        piece = piece.astype(F32)
        gain_grad += jnp.sum(piece * xhat_all[r[0] * step : r[1] * step].astype(F32), axis=0)
        shift_grad += jnp.sum(piece, axis=0)
    bias_grad = jnp.sum(grad_own.astype(F32), axis=0)
    up_bias_grad = jnp.sum(d_up.astype(F32), axis=0).reshape(N, 1, ff_block)
    qkv_bias_grad = jnp.sum(d_qkv.astype(F32), axis=0).reshape(groups, 3, 2, HEAD)
    qkv_bias_grad = qkv_bias_grad.transpose(1, 0, 2, 3)[:, :, :, None, :]
    mine = jnp.arange(C) == c
    up_bias_grad = jnp.where(mine[None, :, None], up_bias_grad, 0.0)
    qkv_bias_grad = jnp.where(mine[None, None, None, :, None], qkv_bias_grad, 0.0)
    small = [gain_grad, shift_grad, qkv_bias_grad, bias_grad, up_bias_grad]
    small = jnp.concatenate([s.reshape(devices, -1) for s in small], axis=1)
    d_normed, _, d_sent = sum_end(d_near, d_arrived, C)
    small = after(small, *d_sent)
    small = lax.all_to_all(small, ALL, split_axis=0, concat_axis=0, tiled=True)
    small = jnp.split(jnp.sum(small, axis=0), cuts[:4])

    d_normed = after(d_normed, down_rows, *small)
    xhat, scale = standardise(hidden_own.astype(F32))
    e = d_normed * gain
    d_hidden = e - jnp.mean(e, axis=-1, keepdims=True)
    d_hidden = (d_hidden - xhat * jnp.mean(e * xhat, axis=-1, keepdims=True)) * scale
    grad_in = (grad_own.astype(F32) + d_hidden).astype(BF).reshape(hidden_in.shape)

    return (
        output,
        grad_in,
        small[0],
        small[1],
        qkv_grad,
        small[2],
        out_grad,
        small[3],
        up_grad,
        small[4],
        down_grad,
        small[3],
    )


def solution(mesh):
    both = P(("dp", "ctx"))
    matrix = P(("dp", "ctx"), None)
    slots = P("dp", "ctx", None)
    in_specs = (
        slots,
        both,
        both,
        matrix,
        both,
        matrix,
        both,
        matrix,
        both,
        matrix,
        both,
        P("dp", None),
        P("dp", "ctx"),
        P("dp", None),
        slots,
    )
    out_specs = (
        slots,
        slots,
        both,
        both,
        matrix,
        both,
        matrix,
        both,
        matrix,
        both,
        matrix,
        both,
    )
    return jax.shard_map(
        on_device, mesh=mesh, in_specs=in_specs, out_specs=out_specs, check_vma=False
    )
```
